32 devices in a mesh: lat: 8 (over z, x), lon: 4 (over y, core).
Axes of the slice: x: 2, y: 2, z: 4, core: 2. Of those that a mesh axis runs over, the one named last changes fastest.
Arguments:
- pixels: bfloat16 [2, 48, 48, 1280], P(None, 'lat', 'lon'), may hold values from -6 to 6
- targets: bfloat16 [2, 2, 48, 48, 1280], P(None, None, 'lat', 'lon'), may hold values from -6 to 6
- mask: int32 [2, 48, 48], P(None, 'lat', 'lon'), may hold values 0 or 1
- lat_rows: int32 [48], P('lat'), may hold values from 0 to 47
- adam_params: float32 [6510080], P(('lat', 'lon')), may hold values from -1.5 to 1.5
- adam_m: float32 [6510080], P(('lat', 'lon')), may hold values from -1.7881393e-07 to 1.7881393e-07
- adam_v: float32 [6510080], P(('lat', 'lon')), may hold values from 3.135334e-15 to 1.2541336e-14
- mlp_weights: float32 [2, 2, 3072, 768], P(None, None, 'lon'), may hold values from -1 to 1
- mlp_momentum: float32 [2, 2, 3072, 768], P(None, None, 'lon'), may hold values from -1.4305115e-06 to 1.4305115e-06
Outputs:
- adam_params_new: float32 [6510080], P(('lat', 'lon'))
- adam_m_new: float32 [6510080], P(('lat', 'lon'))
- adam_v_new: float32 [6510080], P(('lat', 'lon'))
- mlp_weights_new: float32 [2, 2, 3072, 768], P(None, None, 'lon')
- mlp_momentum_new: float32 [2, 2, 3072, 768], P(None, None, 'lon')
- loss: float32 [], replicated
- grad_norm: float32 [], replicated
The draws below stay inside these ranges and needn't reach their ends.
All inputs are finite; a program needn't handle non-finite values. No bound on the sum of `mask` on one device may be relied on, other than what follows from the above.
Results may differ from the reference program's by a relative error of at most 0.012.
Values may be sent and summed in bfloat16 or wider, within the bound.
No kernel may reach another device: no remote copies, remote signals or barrier semaphores. Data moves between devices by JAX's collectives and lax.ppermute only.
A program may use at most 512 MiB of HBM per device.

```python
import math
import jax
import jax.numpy as jnp
from jax import lax

D = 768
FF = 3072
NB = 8
PIX = 1280
BS = 96
L = 2
STEPS = 2
NS_STEPS = 2
STEP_NUM = 5
ITEMS = 2
NLAT = 48
NLON = 48
ADAM_RAW = 6510080
ADAM = 6510080


def draw_adam_params(key, part):
    key_list = jax.random.split(key, 10)

    def normal_part(key_index, amount, spread):
        return jnp.clip(jax.random.normal(key_list[key_index], (amount,), jnp.float32), -4.0, 4.0) * spread
    embed_part = normal_part(0, 3 * PIX * D, (3 * PIX) ** (-0.5))
    head_part = normal_part(1, 3 * D * PIX, (3 * D) ** (-0.5))
    spec_part = normal_part(2, L * 4 * NB * BS * BS, (2 * BS) ** (-0.5))
    embed_bias = normal_part(3, D, 0.1)
    head_bias = normal_part(4, PIX, 0.1)
    spec_bias = normal_part(5, L * 4 * D, 0.1)
    gain_part = jax.random.uniform(key_list[6], (L, 4, D), jnp.float32, 0.8, 1.2)
    shifts = normal_part(7, L * 4 * D, 0.1).reshape(L, 4, D)
    chooser = (jnp.arange(4) % 2 == 0)[None, :, None]
    norm_part = jnp.where(chooser, gain_part, shifts).reshape(-1)
    mlp_bias = normal_part(8, L * (FF + D), 0.1)
    padding = normal_part(9, ADAM - ADAM_RAW, 0.1)
    return jnp.concatenate([embed_part, head_part, spec_part, embed_bias, head_bias, spec_bias, norm_part, mlp_bias, padding])


def draw_mlp_weights(key, part):
    values = jnp.clip(jax.random.normal(key, (L, 2, FF, D), jnp.float32), -4.0, 4.0)
    spread = jnp.where(jnp.arange(2) == 0, D ** (-0.5), FF ** (-0.5)).astype(jnp.float32)
    return values * spread[None, :, None, None]


def plant(drawn, own_key, smallest, high):
    spot = [jax.random.randint(jax.random.fold_in(own_key, axis), (), 0, length) for axis, length in enumerate(drawn.shape)]
    longest = drawn.shape.index(max(drawn.shape))
    neighbour = spot[:longest] + [(spot[longest] + 1) % drawn.shape[longest]] + spot[longest + 1:]
    return drawn.at[tuple(spot)].set(smallest).at[tuple(neighbour)].set(high)


def block_levels(key, extent, cuts, low, top_value):
    factor_of = 1.0
    for dim, parts in cuts:
        steps = jax.random.uniform(jax.random.fold_in(jax.random.fold_in(key, 6), dim), (parts,), jnp.float32, low / len(cuts), top_value / len(cuts))
        factor_of = factor_of * jnp.repeat(jnp.exp(steps), extent[dim] // parts).reshape((-1,) + (1,) * (len(extent) - 1 - dim))
    return factor_of


def centred(rng, extent, deviation, limit, cuts=(), held_as=jnp.bfloat16):
    level = block_levels(rng, extent, cuts, -0.22, 0.18) if cuts else 1.0
    values = jax.random.normal(rng, extent, jnp.float32) * deviation * level
    return jnp.minimum(jnp.maximum(values, -limit), limit).astype(held_as)


def setup_inputs(seed: int = 0) -> dict:
    key_of = jax.random.split(jax.random.key(seed), 10)
    return {
        "pixels": centred(key_of[0], (ITEMS, NLAT, NLON, PIX), 1.0, 6.0, ((1, 8), (2, 4))),
        "targets": centred(key_of[1], (STEPS, ITEMS, NLAT, NLON, PIX), 1.0, 6.0, ((2, 8), (3, 4))),
        "mask": plant((jax.random.randint(key_of[2], (ITEMS, NLAT, NLON), 0, 4) < 3).astype(jnp.int32), jax.random.fold_in(key_of[2], 1), 0, 1),
        "lat_rows": plant(jax.random.randint(key_of[3], (NLAT,), 0, NLAT), jax.random.fold_in(key_of[3], 1), 0, NLAT - 1).astype(jnp.int32),
        "adam_params": draw_adam_params(jax.random.fold_in(key_of[9], 71), 0),
        "adam_m": centred(key_of[5], (ADAM,), (0.11e-3 * (ADAM_RAW + 2 * L * FF * D) ** -0.5), 1.7881393432617188e-07, ((0, 32),), jnp.float32),
        "adam_v": jnp.clip(jnp.exp(math.log(1.2541335835504833e-14) - 1.3862944 * jax.random.uniform(key_of[6], (ADAM,), jnp.float32) ** block_levels(key_of[6], (ADAM,), ((0, 32),), -0.2, 0.2)), 3.135333958876208e-15, 1.2541335835504833e-14),
        "mlp_weights": draw_mlp_weights(jax.random.fold_in(key_of[9], 71), 0),
        "mlp_momentum": centred(key_of[8], (L, 2, FF, D), (1e-3 * (ADAM_RAW + 2 * L * FF * D) ** -0.5), 1.430511474609375e-06, ((2, 4),), jnp.float32),
    }


@jax.custom_vjp
def low(v):
    return lax.optimization_barrier(v.astype(jnp.bfloat16)).astype(jnp.float32)

@jax.custom_vjp
def low_back(v):
    return v

def low_keep(v):
    return (low(v), None)

def low_pass(kept, grad):
    return (grad,)

def back_keep(v):
    return (v, None)

def back_low(kept, grad):
    return (low(grad),)
low.defvjp(low_keep, low_pass)
low_back.defvjp(back_keep, back_low)
HIGH_PREC = lax.Precision.HIGHEST
NORM_EPS = 1e-05
CLIP_LEVEL = 0.001
BETA_FIRST = 0.9
BETA_SECOND = 0.95
ADAM_RATE = 0.01
MUON_RATE = 0.8
DECAY_RATE = 0.05
MOMENT_KEEP = 0.95
POLY_COEF = (3.4445, -4.775, 2.0315)

def unpack(flat_params):
    layout = [(3, PIX, D), (3, D, PIX), (L, 2, 2, NB, BS, BS), (D,), (PIX,), (L, 2, 2, D), (L, 4, D), (L, FF + D)]
    pieces_out = []
    offset = 0
    for dims_now in layout:
        amount = math.prod(dims_now)
        pieces_out.append(flat_params[offset:offset + amount].reshape(dims_now))
        offset = offset + amount
    return pieces_out

def dft_table(length_all):
    series = jnp.arange(length_all, dtype=jnp.int32)
    phase = series[:, None] * series[None, :] % length_all
    angle = phase.astype(jnp.float32) * (2.0 * math.pi / length_all)
    scale_value = 1.0 / math.sqrt(length_all)
    return (jnp.cos(angle) * scale_value, jnp.sin(angle) * scale_value)

def along(matrix, values, axis_dim):
    if axis_dim == 1:
        return jnp.einsum('kn,bncd->bkcd', matrix, values, precision=HIGH_PREC)
    return jnp.einsum('kn,brnd->brkd', matrix, values, precision=HIGH_PREC)

def combine(pieces, axis_dim, sign_value, tables, real_only):
    cosine, sine_table = tables
    values = [piece_now.astype(jnp.float32) for piece_now in pieces]
    real_out = along(cosine, values[0], axis_dim)
    if len(values) > 1:
        real_out = real_out - sign_value * along(sine_table, values[1], axis_dim)
    if real_only:
        return (real_out,)
    imag_out = sign_value * along(sine_table, values[0], axis_dim)
    if len(values) > 1:
        imag_out = imag_out + along(cosine, values[1], axis_dim)
    return (real_out, imag_out)

def layer_norm(inputs, gain, shift):
    center = inputs - lax.optimization_barrier(jnp.mean(inputs, axis=-1, keepdims=True))
    variance = lax.optimization_barrier(jnp.mean(center * center, axis=-1, keepdims=True))
    return center * lax.rsqrt(variance + NORM_EPS) * gain + shift

def block_mix(pieces, weights, bias):
    shaped = [piece_now.reshape(piece_now.shape[:-1] + (NB, BS)) for piece_now in pieces]

    def multiply(left_side, right_side):
        return jnp.einsum('brcni,nio->brcno', left_side, right_side, precision=HIGH_PREC)
    real_out = multiply(shaped[0], weights[0]) - multiply(shaped[1], weights[1])
    imag_out = multiply(shaped[0], weights[1]) + multiply(shaped[1], weights[0])
    full_dims = pieces[0].shape
    return (real_out.reshape(full_dims) + bias[0], imag_out.reshape(full_dims) + bias[1])

def rounded(pieces):
    return tuple((low(low_back(piece_now)) for piece_now in pieces))

def layer_forward(state, spec_w, spec_b, norm_vals, mlp_pair, mlp_bias, lat_table, lon_table):
    normed = layer_norm(state, norm_vals[0], norm_vals[1])
    spectrum = combine((low(normed),), 2, -1.0, lon_table, False)
    spectrum = combine(rounded(spectrum), 1, -1.0, lat_table, False)
    inner = block_mix(rounded(spectrum), spec_w[0], spec_b[0])
    activated = tuple((low(jax.nn.gelu(low_back(piece_now), approximate=False)) for piece_now in inner))
    outer = block_mix(activated, spec_w[1], spec_b[1])
    spectrum = combine(rounded(outer), 1, 1.0, lat_table, False)
    spatial = combine(rounded(spectrum), 2, 1.0, lon_table, True)[0]
    mixed = state + low_back(spatial) + normed
    hidden_in = low(layer_norm(mixed, norm_vals[2], norm_vals[3]))
    before = jnp.einsum('brcd,fd->brcf', hidden_in, mlp_pair[0], precision=HIGH_PREC) + mlp_bias[:FF]
    hidden = low(jax.nn.gelu(low_back(before), approximate=False))
    result = jnp.einsum('brcf,fd->brcd', hidden, mlp_pair[1], precision=HIGH_PREC) + mlp_bias[FF:]
    return mixed + low_back(result)

def rows_conv(source, weight3, bias):
    result = bias
    for offset in range(3):
        moved = jnp.roll(source, 1 - offset, axis=1)
        result = result + jnp.einsum('brci,io->brco', moved, weight3[offset], precision=HIGH_PREC)
    return result

def forward_loss(flat_params, mlp_all, pixel_vals, target_vals, weight_map, weight_sum, tables):
    embed_w, head_w, spec_w, embed_b, head_b, spec_b, norm_params, mlp_b = unpack(low(flat_params))
    mlp_low = low(mlp_all)
    layer_fn = jax.checkpoint(layer_forward)
    current = pixel_vals
    accumulated = jnp.zeros((), jnp.float32)
    for roll_idx in range(STEPS):
        state = low_back(rows_conv(low(current), embed_w, embed_b))
        for depth_idx in range(L):
            state = layer_fn(state, spec_w[depth_idx], spec_b[depth_idx], norm_params[depth_idx], mlp_low[depth_idx], mlp_b[depth_idx], tables[0], tables[1])
        predicted = low_back(rows_conv(low(state), head_w, head_b))
        differ = predicted - target_vals[roll_idx]
        accumulated = accumulated + jnp.sum(weight_map[..., None] * differ * differ)
        current = predicted
    return accumulated / (STEPS * PIX * weight_sum)

def newton_schulz(matrices):
    ortho = matrices
    for ns_idx in range(NS_STEPS):
        square = jnp.einsum('lkfd,lkfe->lkde', ortho, ortho, precision=HIGH_PREC)
        if ns_idx == 0:
            trace_val = jnp.trace(square, axis1=2, axis2=3)
            inverse = 1.0 / (jnp.sqrt(trace_val) + 1e-07)
            ortho = ortho * inverse[:, :, None, None]
            square = square * (inverse * inverse)[:, :, None, None]
        poly = POLY_COEF[1] * square + POLY_COEF[2] * jnp.einsum('lkde,lkef->lkdf', square, square, precision=HIGH_PREC)
        ortho = POLY_COEF[0] * ortho + jnp.einsum('lkfd,lkde->lkfe', ortho, poly, precision=HIGH_PREC)
    return ortho

def reference(pixels, targets, mask, lat_rows, adam_params, adam_m, adam_v, mlp_weights, mlp_momentum):
    row_weight = jnp.sin(math.pi * (lat_rows.astype(jnp.float32) + 0.5) / NLAT)
    weight_map = row_weight[None, :, None] * mask.astype(jnp.float32)
    weight_sum = jnp.sum(weight_map)
    tables = (dft_table(NLAT), dft_table(NLON))
    pixel_vals = pixels.astype(jnp.float32)
    target_vals = targets.astype(jnp.float32)

    def objective(flat_params, mlp_all):
        return forward_loss(flat_params, mlp_all, pixel_vals, target_vals, weight_map, weight_sum, tables)
    loss_value, pullback = jax.vjp(objective, adam_params, mlp_weights)
    flat_grad, mlp_grad = pullback(jnp.ones_like(loss_value))
    grad_norm = jnp.sqrt(jnp.sum(flat_grad * flat_grad) + jnp.sum(mlp_grad * mlp_grad))
    factor = jnp.minimum(1.0, CLIP_LEVEL / (grad_norm + 1e-06))
    clipped = flat_grad * factor
    first_new = BETA_FIRST * adam_m + (1.0 - BETA_FIRST) * clipped
    second_new = BETA_SECOND * adam_v + (1.0 - BETA_SECOND) * clipped * clipped
    count_value = float(STEP_NUM)
    first_hat = first_new / (1.0 - BETA_FIRST ** count_value)
    second_hat = second_new / (1.0 - BETA_SECOND ** count_value)
    adam_new = adam_params - ADAM_RATE * (first_hat / (jnp.sqrt(second_hat) + 1e-08) + DECAY_RATE * adam_params)
    momentum_new = MOMENT_KEEP * mlp_momentum + mlp_grad * factor
    ortho = newton_schulz(momentum_new)
    mlp_new = mlp_weights * (1.0 - MUON_RATE * DECAY_RATE) - MUON_RATE * (FF / D) ** 0.5 * ortho
    return (adam_new, first_new, second_new, mlp_new, momentum_new, loss_value, grad_norm)
```

```python
import functools
import math

import jax
import ml_dtypes
import numpy as np
import jax.numpy as jnp
from jax import lax
from jax.experimental import pallas as pl
from jax.experimental.pallas import tpu as pltpu
from jax.sharding import Mesh
from jax.sharding import PartitionSpec as P

D = 768
FF = 3072
NB = 8
PIX = 1280
BS = 96
L = 2
STEPS = 2
NS_STEPS = 2
STEP_NUM = 5


HIGH_PREC = lax.Precision.HIGHEST
NORM_EPS = 1e-05
CLIP_LEVEL = 0.001
BETA_FIRST = 0.9
BETA_SECOND = 0.95
ADAM_RATE = 0.01
MUON_RATE = 0.8
DECAY_RATE = 0.05
MOMENT_KEEP = 0.95
POLY_COEF = (3.4445, -4.775, 2.0315)


def for_sending(value):

    def short(part):
        return part.astype(jnp.bfloat16) if part.dtype == jnp.float32 else part

    return jax.tree.map(short, value)


def with_halo(block, sides, width):
    for axis, dim in sides:
        count = lax.axis_size(axis)
        forward = [(i, i + 1) for i in range(count - 1)]
        forward.append((count - 1, 0))
        backward = [(target, source) for source, target in forward]
        low = lax.ppermute(
            lax.slice_in_dim(block, block.shape[dim] - width, None, axis=dim), axis, forward
        )
        high = lax.ppermute(lax.slice_in_dim(block, 0, width, axis=dim), axis, backward)
        block = jnp.concatenate([low, block, high], axis=dim)
    return block


def unpack(flat_params):
    layout = [
        (3, PIX, D),
        (3, D, PIX),
        (L, 2, 2, NB, BS, BS),
        (D,),
        (PIX,),
        (L, 2, 2, D),
        (L, 4, D),
        (L, FF + D),
    ]
    pieces_out = []
    offset = 0
    for dims_now in layout:
        amount = math.prod(dims_now)
        pieces_out.append(flat_params[offset : offset + amount].reshape(dims_now))
        offset = offset + amount
    return pieces_out


def along(matrix, values, axis_dim):
    if axis_dim == 1:
        return jnp.einsum("kn,bncd->bkcd", matrix, values, precision=HIGH_PREC)
    return jnp.einsum("kn,brnd->brkd", matrix, values, precision=HIGH_PREC)


def phase_table(out_count, in_count, length_all):
    out_index = jnp.arange(out_count, dtype=jnp.int32)
    in_index = jnp.arange(in_count, dtype=jnp.int32)
    phase = out_index[:, None] * in_index[None, :] % length_all
    angle = phase.astype(jnp.float32) * (2.0 * math.pi / length_all)
    scale_value = 1.0 / math.sqrt(length_all)
    return (jnp.cos(angle) * scale_value, jnp.sin(angle) * scale_value)


def combine(pieces, axis_dim, sign_value, tables, real_only):
    cosine, sine_table = tables
    values = [piece_now.astype(jnp.float32) for piece_now in pieces]
    real_out = along(cosine, values[0], axis_dim)
    if len(values) > 1:
        real_out = real_out - sign_value * along(sine_table, values[1], axis_dim)
    if real_only:
        return (real_out,)
    imag_out = sign_value * along(sine_table, values[0], axis_dim)
    if len(values) > 1:
        imag_out = imag_out + along(cosine, values[1], axis_dim)
    return (real_out, imag_out)


def turn_transform(pieces, axis_dim, sign_value, real_only):
    if axis_dim == 1:
        wide = jax.tree.map(
            lambda part, own: part.astype(own.dtype),
            lax.all_to_all(for_sending(pieces), "lat", split_axis=3, concat_axis=1, tiled=True),
            pieces,
        )
        length_all = wide[0].shape[1]
        result = combine(
            wide, 1, sign_value, phase_table(length_all, length_all, length_all), real_only
        )
        narrow = tuple((piece_now.astype(jnp.bfloat16) for piece_now in result))
        returned = jax.tree.map(
            lambda part, own: part.astype(own.dtype),
            lax.all_to_all(for_sending(narrow), "lat", split_axis=1, concat_axis=3, tiled=True),
            narrow,
        )
        return tuple((piece_now.astype(jnp.float32) for piece_now in returned))
    wide = jax.tree.map(
        lambda part, own: part.astype(own.dtype),
        lax.all_to_all(for_sending(pieces), "lon", split_axis=3, concat_axis=2, tiled=True),
        pieces,
    )
    length_all = wide[0].shape[2]
    result = combine(
        wide, 2, sign_value, phase_table(length_all, length_all, length_all), real_only
    )
    return jax.tree.map(
        lambda part, own: part.astype(own.dtype),
        lax.all_to_all(for_sending(result), "lon", split_axis=2, concat_axis=3, tiled=True),
        result,
    )


def transform(pieces, axis_dim, sign_value, real_only):
    return turn_transform(pieces, axis_dim, sign_value, real_only)


def to_low(pieces):
    return tuple((piece_now.astype(jnp.bfloat16) for piece_now in pieces))


def exact_gelu(values):
    return jax.nn.gelu(values, approximate=False)


def gelu_back(values, upstream):
    return jax.vjp(exact_gelu, values)[1](upstream)[0]


def norm_forward(inputs, gain, shift):
    center = inputs - jnp.mean(inputs, axis=-1, keepdims=True)
    inverse = lax.rsqrt(jnp.mean(center * center, axis=-1, keepdims=True) + NORM_EPS)
    scaled = center * inverse
    return (scaled * gain + shift, (scaled, inverse))


def norm_backward(upstream, saved, gain):
    scaled, inverse = saved
    g_gain = jnp.sum(upstream * scaled, axis=(0, 1, 2))
    g_shift = jnp.sum(upstream, axis=(0, 1, 2))
    g_scaled = upstream * gain
    g_input = inverse * (
        g_scaled
        - jnp.mean(g_scaled, axis=-1, keepdims=True)
        - scaled * jnp.mean(g_scaled * scaled, axis=-1, keepdims=True)
    )
    return (g_input, g_gain, g_shift)


def block_mix(pieces, weights, bias):
    shaped = [piece_now.reshape(piece_now.shape[:-1] + (NB, BS)) for piece_now in pieces]

    def multiply(left_side, right_side):
        return jnp.einsum(
            "brcni,nio->brcno", left_side, right_side, preferred_element_type=jnp.float32
        )

    real_out = multiply(shaped[0], weights[0]) - multiply(shaped[1], weights[1])
    imag_out = multiply(shaped[0], weights[1]) + multiply(shaped[1], weights[0])
    full_dims = pieces[0].shape
    return (
        real_out.reshape(full_dims) + bias[0].astype(jnp.float32),
        imag_out.reshape(full_dims) + bias[1].astype(jnp.float32),
    )


def block_back(grads_low, pieces, weights):
    shaped = [piece_now.reshape(piece_now.shape[:-1] + (NB, BS)) for piece_now in pieces]
    g_shaped = [grad_now.reshape(grad_now.shape[:-1] + (NB, BS)) for grad_now in grads_low]

    def back_multiply(grad_side, weight_side):
        return jnp.einsum(
            "brcno,nio->brcni", grad_side, weight_side, preferred_element_type=jnp.float32
        )

    def weight_multiply(input_side, grad_side):
        return jnp.einsum(
            "brcni,brcno->nio", input_side, grad_side, preferred_element_type=jnp.float32
        )

    g_real = back_multiply(g_shaped[0], weights[0]) + back_multiply(g_shaped[1], weights[1])
    g_imag = back_multiply(g_shaped[1], weights[0]) - back_multiply(g_shaped[0], weights[1])
    g_w_real = weight_multiply(shaped[0], g_shaped[0]) + weight_multiply(shaped[1], g_shaped[1])
    g_w_imag = weight_multiply(shaped[0], g_shaped[1]) - weight_multiply(shaped[1], g_shaped[0])
    g_bias = jnp.stack(
        [jnp.sum(grad_now.astype(jnp.float32), axis=(0, 1, 2)) for grad_now in grads_low]
    )
    full_dims = pieces[0].shape
    return (
        (g_real.reshape(full_dims), g_imag.reshape(full_dims)),
        jnp.stack([g_w_real, g_w_imag]),
        g_bias,
    )


def halo_rows(values):
    return with_halo(values, (("lat", 1),), 1)


def rows_conv(source_low, weight3, bias):
    padded = halo_rows(source_low)
    row_count = source_low.shape[1]
    window = jnp.concatenate(
        [padded[:, offset : offset + row_count] for offset in range(3)], axis=-1
    )
    flat_weight = weight3.reshape(-1, weight3.shape[-1])
    result = jnp.einsum("brci,io->brco", window, flat_weight, preferred_element_type=jnp.float32)
    return (result + bias.astype(jnp.float32), window)


def rows_back(grad_low, weight3, need_source):
    g_bias = jnp.sum(grad_low.astype(jnp.float32), axis=(0, 1, 2))
    if not need_source:
        return (g_bias, None)
    padded = halo_rows(grad_low)
    row_count = grad_low.shape[1]
    window_back = jnp.concatenate(
        [padded[:, 2 - offset : 2 - offset + row_count] for offset in range(3)], axis=-1
    )
    flipped = jnp.transpose(weight3, (0, 2, 1)).reshape(-1, weight3.shape[1])
    g_source = jnp.einsum("brco,oi->brci", window_back, flipped, preferred_element_type=jnp.float32)
    return (g_bias, g_source)


def conv_weight_grad(terms_list, weight3):
    window = jnp.concatenate([terms_now[0] for terms_now in terms_list], axis=0)
    grads_low = jnp.concatenate([terms_now[1] for terms_now in terms_list], axis=0)
    return jnp.einsum(
        "brci,brco->io", window, grads_low, preferred_element_type=jnp.float32
    ).reshape(weight3.shape)


def layer_forward(state, params_now):
    spec_w, spec_b, norm_vals, mlp_pair, mlp_bias = params_now
    normed, first_saved = norm_forward(state, norm_vals[0], norm_vals[1])
    spectrum = transform((normed.astype(jnp.bfloat16),), 2, -1.0, False)
    spectrum = transform(to_low(spectrum), 1, -1.0, False)
    mixed_in = to_low(spectrum)
    inner = block_mix(mixed_in, spec_w[0], spec_b[0])
    activated = to_low(tuple((exact_gelu(piece_now) for piece_now in inner)))
    outer = block_mix(activated, spec_w[1], spec_b[1])
    spectrum = transform(to_low(outer), 1, 1.0, False)
    spatial = transform(to_low(spectrum), 2, 1.0, True)[0]
    mixed = state + spatial + normed
    second, second_saved = norm_forward(mixed, norm_vals[2], norm_vals[3])
    hidden_in = second.astype(jnp.bfloat16)
    before = (
        jnp.einsum("brcd,fd->brcf", hidden_in, mlp_pair[0], preferred_element_type=jnp.float32)
        + mlp_bias[:FF]
    )
    hidden = exact_gelu(before).astype(jnp.bfloat16)
    result = (
        jnp.einsum("brcf,fd->brcd", hidden, mlp_pair[1], preferred_element_type=jnp.float32)
        + mlp_bias[FF:]
    )
    return (
        mixed + result,
        (first_saved, mixed_in, inner, activated, second_saved, hidden_in, before, hidden),
    )


def layer_backward(upstream, cache, params_now):
    spec_w, spec_b, norm_vals, mlp_pair, mlp_bias = params_now
    first_saved, mixed_in, inner, activated, second_saved, hidden_in, before, hidden = cache
    grad_out = upstream.astype(jnp.bfloat16)
    g_down_bias = jnp.sum(grad_out.astype(jnp.float32), axis=(0, 1, 2))
    g_hidden = jnp.einsum(
        "brcd,fd->brcf", grad_out, mlp_pair[1], preferred_element_type=jnp.float32
    )
    g_before = gelu_back(before, g_hidden).astype(jnp.bfloat16)
    g_up_bias = jnp.sum(g_before.astype(jnp.float32), axis=(0, 1, 2))
    g_second = jnp.einsum(
        "brcf,fd->brcd", g_before, mlp_pair[0], preferred_element_type=jnp.float32
    )
    g_norm_in, g_gain_two, g_shift_two = norm_backward(g_second, second_saved, norm_vals[2])
    g_mixed = upstream + g_norm_in
    g_spectrum = transform((g_mixed.astype(jnp.bfloat16),), 2, -1.0, False)
    g_outer = to_low(transform(to_low(g_spectrum), 1, -1.0, False))
    g_activated, g_w_outer, g_b_outer = block_back(g_outer, activated, spec_w[1])
    g_inner = to_low(
        tuple((gelu_back(piece_now, grad_now) for piece_now, grad_now in zip(inner, g_activated)))
    )
    g_mixed_in, g_w_inner, g_b_inner = block_back(g_inner, mixed_in, spec_w[0])
    g_spectrum = transform(to_low(g_mixed_in), 1, 1.0, False)
    g_normed = transform(to_low(g_spectrum), 2, 1.0, True)[0] + g_mixed
    g_state_norm, g_gain_one, g_shift_one = norm_backward(g_normed, first_saved, norm_vals[0])
    layer_grads = (
        jnp.stack([g_w_inner, g_w_outer]),
        jnp.stack([g_b_inner, g_b_outer]),
        jnp.stack([g_gain_one, g_shift_one, g_gain_two, g_shift_two]),
        jnp.concatenate([g_up_bias, g_down_bias]),
    )
    return (g_mixed + g_state_norm, layer_grads, (hidden, grad_out, g_before, hidden_in))


def body(pixels, targets, mask, lat_rows, adam_params, adam_m, adam_v, mlp_weights, mlp_momentum):
    flat_low = lax.all_gather(adam_params.astype(jnp.bfloat16), ("lat", "lon"), axis=0, tiled=True)
    mlp_low = lax.all_gather(mlp_weights.astype(jnp.bfloat16), "lon", axis=2, tiled=True)
    embed_w, head_w, spec_w, embed_b, head_b, spec_b, norm_params, mlp_b = unpack(flat_low)
    row_count = pixels.shape[1]
    lat_total = lax.axis_size("lat") * row_count
    row_weight = jnp.sin(math.pi * (lat_rows.astype(jnp.float32) + 0.5) / lat_total)
    weight_map = row_weight[None, :, None] * mask.astype(jnp.float32)
    weight_sum = lax.psum(jnp.sum(weight_map), ("lat", "lon"))
    loss_scale = 2.0 / (STEPS * PIX * weight_sum)

    def params_at(depth_idx):
        return (
            spec_w[depth_idx],
            spec_b[depth_idx],
            norm_params[depth_idx].astype(jnp.float32),
            mlp_low[depth_idx],
            mlp_b[depth_idx].astype(jnp.float32),
        )

    current = pixels
    saved_steps = []
    loss_local = jnp.zeros((), jnp.float32)
    for roll_idx in range(STEPS):
        state, embed_window = rows_conv(current.astype(jnp.bfloat16), embed_w, embed_b)
        caches = []
        for depth_idx in range(L):
            state, cache_now = layer_forward(state, params_at(depth_idx))
            caches.append(cache_now)
        predicted, head_window = rows_conv(state.astype(jnp.bfloat16), head_w, head_b)
        differ = predicted - targets[roll_idx].astype(jnp.float32)
        loss_local = loss_local + jnp.sum(weight_map[..., None] * differ * differ)
        saved_steps.append(
            (embed_window, caches, head_window, weight_map[..., None] * differ * loss_scale)
        )
        current = predicted
    g_embed_b = jnp.zeros(embed_b.shape, jnp.float32)
    g_head_b = jnp.zeros(head_b.shape, jnp.float32)
    head_terms = []
    embed_terms = []
    mlp_terms = [[] for unused in range(L)]
    g_layers = [None] * L
    carried = None
    for roll_idx in reversed(range(STEPS)):
        embed_window, caches, head_window, loss_grad = saved_steps[roll_idx]
        upstream = loss_grad if carried is None else loss_grad + carried
        upstream_low = upstream.astype(jnp.bfloat16)
        head_terms.append((head_window, upstream_low))
        grad_b, grad_state = rows_back(upstream_low, head_w, True)
        g_head_b = g_head_b + grad_b
        for depth_idx in reversed(range(L)):
            grad_state, layer_grads, mlp_now = layer_backward(
                grad_state, caches[depth_idx], params_at(depth_idx)
            )
            mlp_terms[depth_idx].append(mlp_now)
            if g_layers[depth_idx] is None:
                g_layers[depth_idx] = layer_grads
            else:
                g_layers[depth_idx] = jax.tree.map(jnp.add, g_layers[depth_idx], layer_grads)
        state_low = grad_state.astype(jnp.bfloat16)
        embed_terms.append((embed_window, state_low))
        grad_b, carried = rows_back(state_low, embed_w, roll_idx > 0)
        g_embed_b = g_embed_b + grad_b
    g_embed_w = conv_weight_grad(embed_terms, embed_w)
    g_head_w = conv_weight_grad(head_terms, head_w)
    mlp_grads = []
    for depth_idx in range(L):
        joined = [
            jnp.concatenate([terms_now[member] for terms_now in mlp_terms[depth_idx]], axis=0)
            for member in range(4)
        ]
        g_up = jnp.einsum("brcf,brcd->fd", joined[2], joined[3], preferred_element_type=jnp.float32)
        g_down = jnp.einsum(
            "brcf,brcd->fd", joined[0], joined[1], preferred_element_type=jnp.float32
        )
        mlp_grads.append(jnp.stack([g_up, g_down]))
    full_mlp = jnp.stack(mlp_grads)
    stacked = [
        jnp.stack([g_layers[depth_idx][member] for depth_idx in range(L)]) for member in range(4)
    ]
    flat_grad = jnp.concatenate(
        [
            g_embed_w.reshape(-1),
            g_head_w.reshape(-1),
            stacked[0].reshape(-1),
            g_embed_b,
            g_head_b,
            stacked[1].reshape(-1),
            stacked[2].reshape(-1),
            stacked[3].reshape(-1),
        ]
    )
    lon_count = lax.axis_size("lon")
    lat_count = lax.axis_size("lat")
    dev_count = lon_count * lat_count
    per_block = full_mlp.shape[2] // dev_count
    mlp_rows = (
        full_mlp.reshape(L, 2, lon_count, lat_count, per_block, D)
        .transpose(3, 2, 0, 1, 4, 5)
        .reshape(dev_count, -1)
    )
    flat_rows = flat_grad.reshape(dev_count, -1)
    flat_width = flat_rows.shape[1]
    summed = lax.psum_scatter(
        jnp.concatenate([flat_rows, mlp_rows], axis=1),
        ("lat", "lon"),
        scatter_dimension=0,
        tiled=True,
    )[0]
    flat_piece = summed[:flat_width]
    mlp_piece = summed[flat_width:].reshape(L, 2, per_block, D)
    local_square = jnp.sum(flat_piece * flat_piece) + jnp.sum(mlp_piece * mlp_piece)
    loss_total, square_sum = lax.psum(
        (loss_local / (STEPS * PIX * weight_sum), local_square), ("lat", "lon")
    )
    mlp_grad = lax.all_gather(mlp_piece.astype(jnp.bfloat16), "lat", axis=2, tiled=True).astype(
        mlp_piece.dtype
    )
    grad_norm = jnp.sqrt(square_sum)
    factor = jnp.minimum(1.0, CLIP_LEVEL / (grad_norm + 1e-06))
    clipped = flat_piece * factor
    first_new = BETA_FIRST * adam_m + (1.0 - BETA_FIRST) * clipped
    second_new = BETA_SECOND * adam_v + (1.0 - BETA_SECOND) * clipped * clipped
    count_value = float(STEP_NUM)
    first_hat = first_new / (1.0 - BETA_FIRST**count_value)
    second_hat = second_new / (1.0 - BETA_SECOND**count_value)
    adam_new = adam_params - ADAM_RATE * (
        first_hat / (jnp.sqrt(second_hat) + 1e-08) + DECAY_RATE * adam_params
    )
    momentum_new = MOMENT_KEEP * mlp_momentum + mlp_grad * factor
    ortho = momentum_new
    for ns_idx in range(NS_STEPS):
        partial_gram = jnp.einsum("lkfd,lkfe->lkde", ortho, ortho, precision=HIGH_PREC)
        square = lax.psum(partial_gram.astype(jnp.bfloat16), "lon").astype(jnp.float32)
        if ns_idx == 0:
            trace_val = jnp.trace(square, axis1=2, axis2=3)
            inverse = 1.0 / (jnp.sqrt(trace_val) + 1e-07)
            ortho = ortho * inverse[:, :, None, None]
            square = square * (inverse * inverse)[:, :, None, None]
        poly = POLY_COEF[1] * square + POLY_COEF[2] * jnp.einsum(
            "lkde,lkef->lkdf", square, square, precision=HIGH_PREC
        )
        ortho = POLY_COEF[0] * ortho + jnp.einsum(
            "lkfd,lkde->lkfe", ortho, poly, precision=HIGH_PREC
        )
    mlp_new = mlp_weights * (1.0 - MUON_RATE * DECAY_RATE) - MUON_RATE * (FF / D) ** 0.5 * ortho
    return (adam_new, first_new, second_new, mlp_new, momentum_new, loss_total, grad_norm)


ROWS = 48
COLS = 48
GROUP = 16
OWN = 3
TOK = ROWS * OWN
HALF_TOK = TOK // 2
PAIRS = 12
LANES = 128
WIDE = NB * LANES
FREQ = PAIRS * 96
NARROW = jnp.bfloat16
WINDOW = 212
EMBED_AT = 2
Z_AXES = ("zh", "zl")
EMBED_SIZE = 3 * PIX * D
SUB_AXES = ("zh", "zl", "x", "y", "c")
LAT_AXES = ("zh", "zl", "x")
LON_AXES = ("y", "c")
ITEM_AXES = ("zl", "x", "y", "c")


def shift_tables():
    table = np.zeros((3, TOK, TOK), np.float32)
    spots = np.arange(TOK)
    for offset in range(3):
        table[offset, spots, (spots + OWN * (offset - 1)) % TOK] = 1.0
    return table


def row_table():
    table = np.zeros((TOK, TOK), np.float64)
    rows = np.arange(ROWS)
    for pair in range(2 * PAIRS):
        if pair == 0:
            waves = (np.ones(ROWS), np.cos(np.pi * rows))
        else:
            angle = 2.0 * np.pi * (pair * rows % ROWS) / ROWS
            waves = (np.cos(angle), np.sin(angle))
        for part in range(2):
            for own in range(OWN):
                table[pair * 6 + part * OWN + own, rows * OWN + own] = waves[part]
    return table / math.sqrt(ROWS)


def column_tables():
    freq = np.arange(COLS)[:, None]
    table = np.zeros((2, 192, 128), np.float64)
    for source in range(GROUP):
        quad, lon = source // 4, source % 4
        for own in range(OWN):
            column = lon * 12 + quad * OWN + own
            angle = 2.0 * np.pi * (freq[:, 0] * column % COLS) / COLS
            cosine, sine = np.cos(angle), np.sin(angle)
            first, second = source * 8 + own, source * 8 + OWN + own
            table[0, 0:48, first] = cosine
            table[0, 96:144, first] = -sine
            table[0, 48:96, second] = cosine
            table[0, 144:192, second] = -sine
            table[1, 0:48, first] = cosine
            table[1, 48:96, first] = cosine
            table[1, 96:144, first] = -sine
            table[1, 144:192, first] = -sine
            table[1, 0:48, second] = -sine
            table[1, 48:96, second] = sine
            table[1, 96:144, second] = -cosine
            table[1, 144:192, second] = cosine
    return table / math.sqrt(COLS)


def spread_table():
    table = np.zeros((384, 512), np.float32)
    spots = np.arange(384)
    table[spots, spots // BS * LANES + spots % BS] = 1.0
    return table


def two_terms(table):
    high = table.astype(ml_dtypes.bfloat16)
    low = (table - high.astype(np.float64)).astype(ml_dtypes.bfloat16)
    return np.stack([high, low])


def dot(left, right):
    return lax.dot_general(left, right, (((1,), (0,)), ((), ())), preferred_element_type=jnp.float32)


def dot_nt(left, right):
    return lax.dot_general(left, right, (((1,), (1,)), ((), ())), preferred_element_type=jnp.float32)


def dot_tn(left, right):
    return lax.dot_general(left, right, (((0,), (0,)), ((), ())), preferred_element_type=jnp.float32)


def normalize(values):
    center = values - jnp.mean(values, axis=-1, keepdims=True)
    inverse = lax.rsqrt(jnp.mean(center * center, axis=-1, keepdims=True) + NORM_EPS)
    return center * inverse, inverse


def normalize_back(upstream, scaled, inverse, gain):
    inner = upstream * gain
    return inverse * (
        inner
        - jnp.mean(inner, axis=-1, keepdims=True)
        - scaled * jnp.mean(inner * scaled, axis=-1, keepdims=True)
    )


def column_sum(values):
    return jnp.sum(values, axis=0, keepdims=True)


def bell(values):
    return 0.5 * (1.0 + lax.erf(values * math.sqrt(0.5)))


def bell_slope(values, area):
    return area + values * jnp.exp(-0.5 * values * values) * (1.0 / math.sqrt(2.0 * math.pi))


def send_rows(low, spread_ref, row_ref, out_ref):
    wide = jnp.concatenate(
        [dot(low[:, :384], spread_ref[...]), dot(low[:, 384:], spread_ref[...])], axis=1
    ).astype(NARROW)
    turned = dot(row_ref[0], wide) + dot(row_ref[1], wide)
    for side in range(2):
        for block in range(NB):
            out_ref[side * NB + block] = turned[
                side * HALF_TOK : (side + 1) * HALF_TOK, block * LANES : (block + 1) * LANES
            ].astype(NARROW)


def take_rows(in_ref, spread_ref, row_back_ref):
    sides = []
    for side in range(2):
        sides.append(
            jnp.concatenate(
                [in_ref[side * NB + block].astype(jnp.float32) for block in range(NB)], axis=1
            )
        )
    wide = jnp.concatenate(sides, axis=0).astype(NARROW)
    low = jnp.concatenate(
        [dot_nt(wide[:, :512], spread_ref[...]), dot_nt(wide[:, 512:], spread_ref[...])], axis=1
    ).astype(NARROW)
    return dot(row_back_ref[0], low) + dot(row_back_ref[1], low)


def fetch(sources, held_ref, sems):
    copies = [pltpu.make_async_copy(src, held_ref.at[i], sems.at[i]) for i, src in enumerate(sources)]
    for copy in copies:
        copy.start()
    return copies


def thirds(w_ref, size):
    return [w_ref.at[pl.ds(i * size, size)] for i in range(3)]


def embed_kernel(src_ref, shift_ref, bias_ref, norm_ref, spread_ref, row_ref, w_ref,
                 state_ref, send_ref, held_ref, sems):
    copies = fetch(thirds(w_ref, PIX), held_ref, sems)
    src = src_ref[...]
    state = bias_ref[...]
    for offset in range(3):
        moved = src if offset == 1 else dot(shift_ref[offset], src).astype(NARROW)
        copies[offset].wait()
        state = state + dot(moved, held_ref[offset])
    state_ref[...] = state
    scaled, _unused = normalize(state)
    normed = scaled * norm_ref[0:1] + norm_ref[1:2]
    send_rows(normed.astype(NARROW), spread_ref, row_ref, send_ref)


def turn_columns(wide_ref, col_ref, pair):
    kind = 0 if pair == 0 else 1
    low = wide_ref[:, 6 * pair : 6 * pair + 8, :].reshape(128, 128).astype(NARROW)
    both = dot(col_ref[0, kind], low) + dot(col_ref[1, kind], low)
    return jnp.concatenate([both[:96], both[96:]], axis=1).astype(NARROW)


def back_columns(wide_ref, col_back_ref, pair, low):
    kind = 0 if pair == 0 else 1
    both = jnp.concatenate([low[:, :128], low[:, 128:]], axis=0)
    back = dot(col_back_ref[0, kind], both) + dot(col_back_ref[1, kind], both)
    wide_ref[:, 6 * pair : 6 * pair + 8, :] = back.reshape(16, 8, 128)


def spec_kernel(
    in_ref, col_ref, col_back_ref, w_ref, b_ref, out_ref, mixed_ref, wide_ref, wide_out_ref
):
    wide_ref[:, :HALF_TOK, :] = in_ref[...].astype(jnp.float32)
    wide_ref[:, HALF_TOK:, :] = jnp.zeros((16, 8, 128), jnp.float32)
    for chunk in range(4):
        pairs = range(chunk * 3, chunk * 3 + 3)
        mixed = jnp.concatenate([turn_columns(wide_ref, col_ref, pair) for pair in pairs], axis=0)
        mixed_ref[chunk * 288 : (chunk + 1) * 288, :] = mixed
        inner = dot(mixed, w_ref[0]) + b_ref[0:1]
        act = (inner * bell(inner)).astype(NARROW)
        outer = (dot(act, w_ref[1]) + b_ref[1:2]).astype(NARROW)
        for place, pair in enumerate(pairs):
            back_columns(wide_out_ref, col_back_ref, pair, outer[place * 96 : place * 96 + 96])
    out_ref[...] = wide_out_ref[:, :HALF_TOK, :].astype(NARROW)


def spec_back_kernel(
    in_ref, col_ref, col_back_ref, w_ref, b_ref, mixed_ref,
    out_ref, gw_ref, gb_ref, wide_ref, wide_out_ref,
):
    wide_ref[:, :HALF_TOK, :] = in_ref[...].astype(jnp.float32)
    wide_ref[:, HALF_TOK:, :] = jnp.zeros((16, 8, 128), jnp.float32)
    for chunk in range(4):
        pairs = range(chunk * 3, chunk * 3 + 3)
        g_outer = jnp.concatenate([turn_columns(wide_ref, col_ref, pair) for pair in pairs], axis=0)
        mixed = mixed_ref[chunk * 288 : (chunk + 1) * 288, :]
        inner = dot(mixed, w_ref[0]) + b_ref[0:1]
        area = bell(inner)
        act = (inner * area).astype(NARROW)
        g_inner = (bell_slope(inner, area) * dot_nt(g_outer, w_ref[1])).astype(NARROW)
        g_mixed = dot_nt(g_inner, w_ref[0]).astype(NARROW)
        first, second = dot_tn(mixed, g_inner), dot_tn(act, g_outer)
        sums = jnp.concatenate(
            [column_sum(g_inner.astype(jnp.float32)), column_sum(g_outer.astype(jnp.float32))], axis=0
        )
        if chunk == 0:
            gw_ref[0], gw_ref[1], gb_ref[...] = first, second, sums
        else:
            gw_ref[0] += first
            gw_ref[1] += second
            gb_ref[...] += sums
        for place, pair in enumerate(pairs):
            back_columns(wide_out_ref, col_back_ref, pair, g_mixed[place * 96 : place * 96 + 96])
    out_ref[...] = wide_out_ref[:, :HALF_TOK, :].astype(NARROW)


def mlp_kernel(has_next, in_ref, state_ref, norm_ref, next_norm_ref, up_b_ref, down_b_ref,
               spread_ref, row_ref, row_back_ref, w0_ref, w1_ref, w2_ref, w3_ref, *rest):
    held_ref, sems = rest[-2:]
    mixed_ref, hidden_in_ref, before_ref, hidden_ref, out_ref = rest[:5]
    copies = fetch((w0_ref, w1_ref, w2_ref, w3_ref), held_ref, sems)
    spatial = take_rows(in_ref, spread_ref, row_back_ref)
    state = state_ref[...]
    scaled, _unused = normalize(state)
    mixed = state + spatial + (scaled * norm_ref[0:1] + norm_ref[1:2])
    mixed_ref[...] = mixed
    again, _unused = normalize(mixed)
    hidden_in = (again * norm_ref[2:3] + norm_ref[3:4]).astype(NARROW)
    hidden_in_ref[...] = hidden_in
    out = mixed + down_b_ref[...]
    for part in range(4):
        spot = slice(part * D, (part + 1) * D)
        copies[part].wait()
        before = dot_nt(hidden_in, held_ref[part, 0]) + up_b_ref[:, spot]
        before_ref[:, spot] = before
        hidden = (before * bell(before)).astype(NARROW)
        hidden_ref[:, spot] = hidden
        out = out + dot(hidden, held_ref[part, 1])
    out_ref[...] = out
    if has_next:
        scaled, _unused = normalize(out)
        normed = scaled * next_norm_ref[0:1] + next_norm_ref[1:2]
        send_rows(normed.astype(NARROW), spread_ref, row_ref, rest[5])


def head_kernel(state_ref, shift_ref, bias_ref, target_ref, weight_ref, w_ref,
                low_ref, pred_ref, grad_ref, loss_ref, held_ref, sems):
    copies = fetch(thirds(w_ref, D), held_ref, sems)
    low = state_ref[...].astype(NARROW)
    low_ref[...] = low
    predicted = bias_ref[...]
    for offset in range(3):
        moved = low if offset == 1 else dot(shift_ref[offset], low).astype(NARROW)
        copies[offset].wait()
        predicted = predicted + dot(moved, held_ref[offset])
    pred_ref[...] = predicted.astype(NARROW)
    differ = predicted - target_ref[...].astype(jnp.float32)
    loss_ref[...] = column_sum(weight_ref[:, 0:1] * differ * differ)
    grad_ref[...] = weight_ref[:, 1:2] * differ


def head_back_kernel(grad_ref, shift_ref, w_ref, low_ref, sum_ref, out_ref, held_ref, sems):
    copies = fetch(thirds(w_ref, D), held_ref, sems)
    low = grad_ref[...].astype(NARROW)
    low_ref[...] = low
    sum_ref[...] = column_sum(low.astype(jnp.float32))
    total = None
    for offset in range(3):
        moved = low if offset == 1 else dot(shift_ref[2 - offset], low).astype(NARROW)
        copies[offset].wait()
        part = dot_nt(moved, held_ref[offset])
        total = part if total is None else total + part
    out_ref[...] = total


def embed_back_kernel(low_ref, shift_ref, add_ref, w_ref, out_ref, held_ref, sems):
    copies = fetch(thirds(w_ref, PIX), held_ref, sems)
    low = low_ref[...]
    total = add_ref[...]
    for offset in range(3):
        moved = low if offset == 1 else dot(shift_ref[2 - offset], low).astype(NARROW)
        copies[offset].wait()
        total = total + dot_nt(moved, held_ref[offset])
    out_ref[...] = total


def mlp_back_kernel(up_ref, before_ref, mixed_ref, norm_ref, spread_ref, row_ref,
                    w0_ref, w1_ref, w2_ref, w3_ref,
                    grad_out_ref, g_before_ref, g_mixed_ref, g_up_b_ref, sums_ref, send_ref,
                    held_ref, sems):
    copies = fetch((w0_ref, w1_ref, w2_ref, w3_ref), held_ref, sems)
    upstream = up_ref[...]
    grad_out = upstream.astype(NARROW)
    grad_out_ref[...] = grad_out
    sums_ref[0:1] = column_sum(grad_out.astype(jnp.float32))
    g_second = None
    for part in range(4):
        spot = slice(part * D, (part + 1) * D)
        before = before_ref[:, spot]
        slope = bell_slope(before, bell(before))
        copies[part].wait()
        g_before = (slope * dot_nt(grad_out, held_ref[part, 1])).astype(NARROW)
        g_before_ref[:, spot] = g_before
        g_up_b_ref[:, spot] = column_sum(g_before.astype(jnp.float32))
        now = dot(g_before, held_ref[part, 0])
        g_second = now if g_second is None else g_second + now
    scaled, inverse = normalize(mixed_ref[...])
    sums_ref[1:2] = column_sum(g_second * scaled)
    sums_ref[2:3] = column_sum(g_second)
    g_mixed = upstream + normalize_back(g_second, scaled, inverse, norm_ref[2:3])
    g_mixed_ref[...] = g_mixed
    send_rows(g_mixed.astype(NARROW), spread_ref, row_ref, send_ref)


def norm_back_kernel(in_ref, g_mixed_ref, state_ref, norm_ref, spread_ref, row_back_ref,
                     out_ref, low_ref, sums_ref):
    g_mixed = g_mixed_ref[...]
    g_normed = take_rows(in_ref, spread_ref, row_back_ref) + g_mixed
    scaled, inverse = normalize(state_ref[...])
    out = g_mixed + normalize_back(g_normed, scaled, inverse, norm_ref[0:1])
    out_ref[...] = out
    low = out.astype(NARROW)
    low_ref[...] = low
    sums_ref[0:1] = column_sum(g_normed * scaled)
    sums_ref[1:2] = column_sum(g_normed)
    sums_ref[2:3] = column_sum(low.astype(jnp.float32))


def muon_kernel(level_ref, momentum_ref, weight_ref, change_ref, out_ref):
    momentum = momentum_ref[...]
    ortho = POLY_COEF[0] * POLY_COEF[0] * level_ref[pl.program_id(0)] * momentum
    ortho = ortho + dot(momentum.astype(NARROW), change_ref[...])
    out_ref[...] = weight_ref[...] * (1.0 - MUON_RATE * DECAY_RATE) - MUON_RATE * (FF / D) ** 0.5 * ortho


def launch(kernel, name, out_dims, operands, far=(), far_out=False, near=(), scratch=(), limit=28):
    anywhere = pl.BlockSpec(memory_space=pl.ANY)
    local = pl.BlockSpec(memory_space=pltpu.VMEM)
    in_specs = []
    for i in range(len(operands)):
        if i in near:
            in_specs.append(pl.BlockSpec(memory_space=pltpu.SMEM))
        else:
            in_specs.append(anywhere if i in far else local)
    return pl.pallas_call(
        kernel,
        name=name,
        out_shape=[jax.ShapeDtypeStruct(dims, kind) for dims, kind in out_dims],
        in_specs=in_specs,
        out_specs=[anywhere if far_out else local for unused in out_dims],
        scratch_shapes=list(scratch),
        compiler_params=pltpu.CompilerParams(vmem_limit_bytes=limit * 1024 * 1024),
    )(*operands)


def exchange(values):
    return lax.all_to_all(values, ITEM_AXES, split_axis=0, concat_axis=0, tiled=True)


def total_over(values, axes):
    count = lax.axis_size(axes)
    spread = jnp.broadcast_to(jnp.pad(values, (0, LANES - values.shape[0])), (count, 1, LANES))
    got = lax.all_to_all(spread, axes, split_axis=0, concat_axis=0, tiled=True)
    return jnp.sum(got, axis=(0, 1))[: values.shape[0]]


KINDS = {"embed": (D, 6), "head": (PIX, 10), "rest": (LANES, 1)}


def kind_ranges(total):
    edges = (0, EMBED_SIZE, 2 * EMBED_SIZE, total)
    return dict(zip(KINDS, zip(edges[:-1], edges[1:])))


def window_pieces(index, width, total):
    found = []
    for kind, (low, high) in kind_ranges(total).items():
        begin, end = max(index * width, low), min((index + 1) * width, high)
        if begin >= end:
            continue
        row, tiles = KINDS[kind]
        first = (begin - low) // (8 * row)
        last = -(-(end - low) // (8 * row))
        found.append([kind, first, last, 0, begin, end])
    spot = {"embed": EMBED_AT, "head": 0, "rest": 0}
    kinds = [piece[0] for piece in found]
    for piece in found:
        piece[3] = spot[piece[0]]
    if kinds == ["embed", "head"]:
        used = (found[1][2] - found[1][1]) * 10
        found[0][3] = EMBED_AT + -(-(used - EMBED_AT) // 6) * 6
    if kinds == ["head", "rest"]:
        found[1][3] = (found[0][2] - found[0][1]) * 10
    for piece in found:
        assert piece[3] + (piece[2] - piece[1]) * KINDS[piece[0]][1] <= WINDOW
    return found


def form_tables(width, total, count):
    starts = {kind: np.zeros(count, np.int32) for kind in KINDS}
    lows = {kind: np.zeros(count, np.int32) for kind in KINDS}
    highs = {kind: np.zeros(count, np.int32) for kind in KINDS}
    for index in range(count):
        for kind, first, last, tile, begin, end in window_pieces(index, width, total):
            row, tiles = KINDS[kind]
            base = EMBED_AT if kind == "embed" else 0
            own = begin - kind_ranges(total)[kind][0] - first * 8 * row
            lows[kind][index] = begin - index * width
            highs[kind][index] = end - index * width
            starts[kind][index] = (tile - base) * 8 * LANES + own - lows[kind][index]
    return starts, lows, highs


def form_tiles(kind):
    if kind == "embed":
        return EMBED_AT, (WINDOW - EMBED_AT) // 6
    return (0, WINDOW // 10) if kind == "head" else (0, WINDOW)


def own_window(own, device, width, total, count):
    starts, lows, highs = form_tables(width, total, count)
    spot = jnp.arange(width, dtype=jnp.int32)
    window = jnp.zeros((WINDOW, 8, LANES), jnp.float32)
    for kind, (row, tiles) in KINDS.items():
        start, low, high = (jnp.asarray(t[kind])[device] for t in (starts, lows, highs))
        first, groups = form_tiles(kind)
        length = groups * tiles * 8 * LANES
        held = jnp.where((spot >= low) & (spot < high), own, 0.0)
        held = jnp.pad(held, (length, length))
        form = lax.dynamic_slice(held, (length - start,), (length,))
        form = form.reshape(groups, 8, tiles, LANES).transpose(0, 2, 1, 3).reshape(-1, 8, LANES)
        window = window + jnp.pad(form, ((first, WINDOW - first - groups * tiles), (0, 0), (0, 0)))
    return window.astype(NARROW)


def own_range(window, device, width, total, count):
    starts, lows, highs = form_tables(width, total, count)
    spot = jnp.arange(width, dtype=jnp.int32)
    result = jnp.zeros((width,), jnp.float32)
    for kind, (row, tiles) in KINDS.items():
        start, low, high = (jnp.asarray(t[kind])[device] for t in (starts, lows, highs))
        first, groups = form_tiles(kind)
        form = window[first : first + groups * tiles].reshape(groups, tiles, 8, LANES)
        form = jnp.pad(form.transpose(0, 2, 1, 3).reshape(-1), (width, width))
        held = lax.dynamic_slice(form, (width + start,), (width,))
        result = jnp.where((spot >= low) & (spot < high), held, result)
    return result


def join_plan(kind, width, total, count):
    pieces = []
    for index in range(count):
        for piece in window_pieces(index, width, total):
            if piece[0] == kind:
                pieces.append((index,) + tuple(piece[1:4]))
    single, double = [], []
    for place, (index, first, last, tile) in enumerate(pieces):
        if place:
            shared = pieces[place - 1][2]
            before = pieces[place - 1]
            if shared > first:
                double.append((first, shared, before[0], before[3], before[1], index, tile))
        else:
            shared = first
        follow = pieces[place + 1][1] if place + 1 < len(pieces) else last
        begin, end = max(first, shared), min(last, follow)
        if begin < end:
            single.append((begin, end, index, tile, first))
    return single, double


def join_kernel(tiles, single, double, got_ref, out_ref, left_ref, right_ref, sems, left_sems, right_sems):
    copies = []
    for place, (begin, end, index, tile, first) in enumerate(single):
        source = got_ref.at[index, pl.ds(tile + (begin - first) * tiles, (end - begin) * tiles)]
        target = out_ref.at[pl.ds(begin * tiles, (end - begin) * tiles)]
        copies.append(pltpu.make_async_copy(source, target, sems.at[place]))
    loads = []
    for place, (begin, end, before, before_tile, before_first, index, tile) in enumerate(double):
        size = (end - begin) * tiles
        source = got_ref.at[before, pl.ds(before_tile + (begin - before_first) * tiles, size)]
        loads.append(pltpu.make_async_copy(source, left_ref.at[place, pl.ds(0, size)], left_sems.at[place]))
        source = got_ref.at[index, pl.ds(tile, size)]
        loads.append(pltpu.make_async_copy(source, right_ref.at[place, pl.ds(0, size)], right_sems.at[place]))
    for copy in loads + copies:
        copy.start()
    for copy in loads:
        copy.wait()
    stores = []
    for place, (begin, end, *unused) in enumerate(double):
        size = (end - begin) * tiles
        total = left_ref[place, :size].astype(jnp.float32) + right_ref[place, :size].astype(jnp.float32)
        left_ref[place, :size] = total.astype(NARROW)
        target = out_ref.at[pl.ds(begin * tiles, size)]
        stores.append(pltpu.make_async_copy(left_ref.at[place, pl.ds(0, size)], target, left_sems.at[place]))
        stores[-1].start()
    for copy in copies + stores:
        copy.wait()


def join_windows(got, kind, width, total, count):
    row, tiles = KINDS[kind]
    low, high = kind_ranges(total)[kind]
    single, double = join_plan(kind, width, total, count)
    groups = -(-(high - low) // (8 * row))
    deep = max([(d[1] - d[0]) * tiles for d in double] + [1])
    held = pltpu.VMEM((max(len(double), 1), deep, 8, LANES), NARROW)
    sem = pltpu.SemaphoreType.DMA
    (out,) = launch(
        functools.partial(join_kernel, tiles, single, double), "join_" + kind,
        [((groups * tiles, 8, LANES), NARROW)], [got], far=(0,), far_out=True,
        scratch=(held, held, sem((max(len(single), 1),)), sem((max(len(double), 1),)), sem((max(len(double), 1),))),
    )
    return out.reshape(groups, tiles, 8, LANES).transpose(0, 2, 1, 3).reshape(groups * 8, row)


def pack_plan(width, total, count):
    plan = []
    for index in range(count):
        for kind, first, last, tile, begin, end in window_pieces(index, width, total):
            tiles = KINDS[kind][1]
            if kind == "rest":
                plan.append((index, 6, first, last - first, tile))
                continue
            size = (PIX if kind == "embed" else D) // 8
            while first < last:
                source = first // size
                stop = min(last, (source + 1) * size)
                number = source + (0 if kind == "embed" else 3)
                plan.append((index, number, (first - source * size) * tiles, (stop - first) * tiles, tile))
                tile += (stop - first) * tiles
                first = stop
    return plan


def pack_kernel(plan, place_ref, *refs):
    sources, (keep_ref, send_ref, sems) = refs[:7], refs[7:]
    x, y, c = place_ref[0], place_ref[1], place_ref[2]
    ends = []
    for number, (index, source, begin, size, tile) in enumerate(plan):
        plane, side, depth, core = index // 8, index // 4 % 2, index // 2 % 2, index % 2
        spot = (plane, (side + x) % 2, (depth + y) % 2, pl.ds(tile, size))
        from_ref = sources[source].at[pl.ds(begin, size)]
        keep = pltpu.make_async_copy(from_ref, keep_ref.at[spot], sems.at[number])
        send = pltpu.make_async_copy(from_ref, send_ref.at[spot], sems.at[number])

        @pl.when(c == core)
        def _():
            keep.start()

        @pl.when(c != core)
        def _():
            send.start()

        ends.append(keep)
    for copy in ends:
        copy.wait()


def tiles_of(values):
    rows, columns = values.shape
    split = values.reshape(rows // 8, 8, columns // LANES, LANES)
    return split.transpose(0, 2, 1, 3).reshape(-1, 8, LANES)


def swap(values, axis):
    return lax.ppermute(values, axis, [(0, 1), (1, 0)])


def add_low(left, right):
    return (left.astype(jnp.float32) + right.astype(jnp.float32)).astype(NARROW)


def chip_sum(kept, x_dim, y_dim, cut_dim):
    half = kept.shape[cut_dim] // 2

    def side(values, dim, which):
        return lax.index_in_dim(values, which, dim, keepdims=True)

    parts = []
    for start, order in ((0, ((x_dim, "x"), (y_dim, "y"))), (half, ((y_dim, "y"), (x_dim, "x")))):
        value = lax.slice_in_dim(kept, start, start + half, axis=cut_dim)
        for dim, axis in order:
            value = add_low(side(value, dim, 0), swap(side(value, dim, 1), axis))
        parts.append(value)
    return jnp.concatenate(parts, axis=cut_dim)


def line_sum(parts, owners):
    plane = lax.axis_index(Z_AXES)

    def pick(number):
        return lax.dynamic_index_in_dim(
            parts, jnp.clip(number - owners[0], 0, len(owners) - 1), 0, keepdims=False
        )

    total = pick(plane).astype(jnp.float32)
    for mirror in (False, True):
        here = 3 - plane if mirror else plane
        moving = None
        for step in (1, 2, 3):
            pairs = []
            for spot in range(3):
                number = 4 - step + spot
                owner = 3 - number if mirror else number
                if number > 3 or owner not in owners:
                    continue
                pairs.append((3 - spot, 2 - spot) if mirror else (spot, spot + 1))
            if not pairs:
                continue
            number = 4 - step + here
            value = pick(3 - number if mirror else number)
            if moving is not None:
                value = add_low(value, moving)
            moving = lax.ppermute(value, Z_AXES, pairs)
        total = total + moving.astype(jnp.float32)
    return total


def plane_sum(values):
    rows = values.shape[0]
    core = lax.axis_index("c")
    halves = values.reshape(2, rows // 2, values.shape[1])
    kept = lax.dynamic_index_in_dim(halves, core, 0, keepdims=False)
    sent = lax.dynamic_index_in_dim(halves, 1 - core, 0, keepdims=False).astype(NARROW)
    kept = kept + swap(sent, "c").astype(jnp.float32)
    quarter = rows // 4
    parts = []
    for start, order in ((0, ("x", "y")), (quarter, ("y", "x"))):
        value = kept[start : start + quarter]
        for axis in order:
            low = value.astype(NARROW)
            value = low.astype(jnp.float32) + swap(low, axis).astype(jnp.float32)
        parts.append(value)
    mine = jnp.concatenate(parts, axis=0).astype(NARROW)
    other = swap(mine, "c")
    first = jnp.where(core == 0, mine, other)
    second = jnp.where(core == 0, other, mine)
    return jnp.concatenate([first, second], axis=0).astype(jnp.float32)


def line_gather(own):
    plane = lax.axis_index(Z_AXES)
    below, above = [], []
    value = own
    for step in (1, 2, 3):
        value = lax.ppermute(value, Z_AXES, [(i, i + 1) for i in range(step - 1, 3)])
        below.append(value)
    value = own
    for step in (1, 2, 3):
        value = lax.ppermute(value, Z_AXES, [(i, i - 1) for i in range(1, 5 - step)])
        above.append(value)
    stack = jnp.stack(below[::-1] + [own] + above)
    return lax.dynamic_slice_in_dim(stack, 3 - plane, 4, 0)


def unpack_rest(rest):
    found = []
    offset = 0
    for dims in ((L, 2, 2, NB, BS, BS), (D,), (PIX,), (L, 2, 2, D), (L, 4, D), (L, FF + D)):
        amount = math.prod(dims)
        found.append(rest[offset : offset + amount].reshape(dims))
        offset += amount
    return found


def fast_body(pixels, targets, mask, lat_rows, adam_params, adam_m, adam_v, mlp_weights, mlp_momentum):
    lat_index, lon_index = lax.axis_index(LAT_AXES), lax.axis_index(LON_AXES)
    device = lax.axis_index(SUB_AXES)
    devices = lax.axis_size(SUB_AXES)
    width = adam_params.shape[0]
    total = width * devices
    low_side = lax.axis_index("zl") == 0
    x, y, c = lax.axis_index("x"), lax.axis_index("y"), lax.axis_index("c")
    block = lax.axis_index(("x", "y", "c"))
    shifts = jnp.asarray(shift_tables(), NARROW)
    row_fwd = jnp.asarray(two_terms(row_table()))
    row_back = jnp.asarray(two_terms(row_table().T))
    col_fwd = jnp.asarray(two_terms(column_tables()))
    col_back = jnp.asarray(two_terms(column_tables().transpose(0, 2, 1)))
    col_fwd = jnp.where(low_side, col_fwd, col_fwd[:, 1:2])
    col_back = jnp.where(low_side, col_back, col_back[:, 1:2])
    spread = jnp.asarray(spread_table(), NARROW)

    def to_items(values):
        rest = values.shape[4:]
        lead, items, rows, cols = values.shape[:4]
        split = values.reshape((lead, items, rows, 4, OWN) + rest)
        order = (1, 3, 0, 2, 4) + tuple(range(5, 5 + len(rest)))
        packed = split.transpose(order).reshape((items * 4, lead * rows * OWN) + rest)
        got = lax.all_to_all(packed, LAT_AXES, split_axis=0, concat_axis=0, tiled=True)
        got = got.reshape((items * 4, lead, rows * OWN) + rest)
        return jnp.moveaxis(got, 1, 0).reshape((lead, TOK) + rest)

    windows = lax.all_gather(own_window(adam_params, device, width, total, devices), SUB_AXES)
    turned_w = jnp.roll(mlp_weights, mlp_weights.shape[2] // 2, axis=2)
    mlp_own = jnp.where(x == 0, mlp_weights, turned_w).astype(NARROW)
    mlp_low = []
    for depth in range(L):
        own = mlp_own[depth]
        if depth:
            own, windows = lax.optimization_barrier((own, windows))
        across_y = swap(own, "y")
        mlp_low.append((own, across_y, swap(own, "c"), swap(across_y, "c")))
    source = to_items(pixels[None])[0]
    wanted = to_items(targets)
    row_weight = jnp.sin(math.pi * (lat_rows.astype(jnp.float32) + 0.5) / ROWS)
    weight_local = row_weight[None, :, None] * mask.astype(jnp.float32)
    weights = to_items(weight_local[None])[0]
    weight_sum = total_over(jnp.sum(weight_local)[None], SUB_AXES)[0]
    loss_scale = 2.0 / (STEPS * PIX * weight_sum)
    weight_pair = jnp.stack([weights, weights * loss_scale], axis=1)

    embed_w = join_windows(windows, "embed", width, total, devices)
    head_w = join_windows(windows, "head", width, total, devices)
    rest = join_windows(windows, "rest", width, total, devices).reshape(-1)
    spec_w, embed_b, head_b, spec_b, norm_params, mlp_b = unpack_rest(rest)
    embed_b, head_b = embed_b.astype(jnp.float32)[None], head_b.astype(jnp.float32)[None]
    norms = norm_params.astype(jnp.float32)
    mlp_b = mlp_b.astype(jnp.float32)

    def by_place(values):
        values = jnp.where(y == 0, values, values[:, ::-1])
        values = jnp.where(c == 0, values, values[:, :, ::-1])
        return jnp.where(x == 0, values, values[:, :, :, ::-1])

    up_b = by_place(mlp_b[:, :FF].reshape(L, 2, 2, 2, -1)).transpose(0, 2, 1, 3, 4).reshape(L, 1, FF)
    down_b = mlp_b[:, None, FF:]
    gap = LANES - BS
    own_w = lax.dynamic_index_in_dim(spec_w, block, 3, keepdims=False)
    own_w = jnp.pad(own_w, ((0, 0),) * 3 + ((0, gap), (0, gap)))
    real, imag = own_w[:, :, 0], own_w[:, :, 1]
    pair_w = jnp.concatenate(
        [jnp.concatenate([real, imag], axis=-1), jnp.concatenate([-imag, real], axis=-1)], axis=-2
    )
    own_b = lax.dynamic_slice_in_dim(spec_b, block * BS, BS, 3).astype(jnp.float32)
    pair_b = jnp.pad(own_b, ((0, 0),) * 3 + ((0, gap),)).reshape(L, 2, 2 * LANES)

    f32 = jnp.float32
    payload = ((GROUP, HALF_TOK, LANES), NARROW)
    state_f32 = ((TOK, D), f32)
    wide = pltpu.VMEM((GROUP, HALF_TOK + 8, LANES), f32)
    sem = pltpu.SemaphoreType.DMA
    held_mlp = (pltpu.VMEM((4, 2, D, D), NARROW), sem((4,)))
    held_embed = (pltpu.VMEM((3, PIX, D), NARROW), sem((3,)))
    held_head = (pltpu.VMEM((3, D, PIX), NARROW), sem((3,)))

    current = source
    saved = []
    loss_sums = []
    for roll_idx in range(STEPS):
        state, sent = launch(
            embed_kernel, "embed", [state_f32, payload],
            [current, shifts, embed_b, norms[0], spread, row_fwd, embed_w], far=(6,),
            scratch=held_embed,
        )
        layers = []
        for depth in range(L):
            got = exchange(sent)
            out, mixed_in = launch(
                spec_kernel, "spec", [payload, ((FREQ, 2 * LANES), NARROW)],
                [got, col_fwd, col_back, pair_w[depth], pair_b[depth]], scratch=(wide, wide),
            )
            got = exchange(out)
            has_next = depth + 1 < L
            outs = [state_f32, ((TOK, D), NARROW), ((TOK, FF), f32), ((TOK, FF), NARROW), state_f32]
            results = launch(
                functools.partial(mlp_kernel, has_next), "mlp", outs + [payload] * has_next,
                [got, state, norms[depth], norms[min(depth + 1, L - 1)], up_b[depth], down_b[depth],
                 spread, row_fwd, row_back, *mlp_low[depth]], far=(9, 10, 11, 12), scratch=held_mlp,
            )
            layers.append((state, mixed_in) + tuple(results[:4]))
            state = results[4]
            if has_next:
                sent = results[5]
        low, predicted, loss_grad, loss_part = launch(
            head_kernel, "head",
            [((TOK, D), NARROW), ((TOK, PIX), NARROW), ((TOK, PIX), f32), ((1, PIX), f32)],
            [state, shifts, head_b, wanted[roll_idx], weight_pair, head_w], far=(5,),
            scratch=held_head,
        )
        loss_sums.append(loss_part)
        saved.append((current, layers, low, loss_grad))
        current = predicted

    rows_own = mlp_momentum.shape[2] // 2
    half_ff = FF // 2

    def joined(terms, member):
        return jnp.concatenate([now[member] for now in terms], axis=0)

    def mlp_sends(depth):
        g_before, hidden_in, hidden, grad_out = (joined(mlp_terms[depth], m) for m in range(4))
        pairs = ((g_before, hidden_in), (hidden, grad_out))
        return pairs, [swap(dot_tn(a[:, half_ff:], b).astype(NARROW), "c") for a, b in pairs]

    def mlp_chip(pairs, got):
        kept = [
            (dot_tn(a[:, :half_ff], b) + sent.astype(f32)).astype(NARROW)
            for (a, b), sent in zip(pairs, got)
        ]
        kept = jnp.stack(kept).reshape(2, 2, 2, rows_own, D)
        return chip_sum(kept, 2, 1, 3).reshape(2, rows_own, D)

    def mlp_line(depth, kept):
        return line_sum(kept, [2 * depth, 2 * depth + 1])

    head_terms, embed_terms = [], []
    mlp_terms = [[] for unused in range(L)]
    spec_terms = [[] for unused in range(L)]
    sum_terms = [[] for unused in range(L)]
    head_sums, embed_sums = [], []
    upstream = None
    for roll_idx in reversed(range(STEPS)):
        current, layers, low, loss_grad = saved[roll_idx]
        upstream = loss_grad if upstream is None else upstream
        upstream_low, head_sum, grad_state = launch(
            head_back_kernel, "head_back",
            [((TOK, PIX), NARROW), ((1, PIX), f32), state_f32], [upstream, shifts, head_w],
            far=(2,), scratch=held_head,
        )
        head_terms.append((low, upstream_low))
        head_sums.append(head_sum)
        for depth in reversed(range(L)):
            state, mixed_in, mixed, hidden_in, before, hidden = layers[depth]
            grad_out, g_before, g_mixed, g_up_b, sums_two, sent = launch(
                mlp_back_kernel, "mlp_back",
                [((TOK, D), NARROW), ((TOK, FF), NARROW), state_f32, ((1, FF), f32), ((3, D), f32),
                 payload],
                [grad_state, before, mixed, norms[depth], spread, row_fwd, *mlp_low[depth]],
                far=(6, 7, 8, 9), scratch=held_mlp,
            )
            got = exchange(sent)
            if roll_idx == 0 and depth == 0:
                last_chip, got = lax.optimization_barrier((mlp_chip(*last_sends), got))
            out, g_pair, g_pair_b = launch(
                spec_back_kernel, "spec_back",
                [payload, ((2, 2 * LANES, 2 * LANES), f32), ((2, 2 * LANES), f32)],
                [got, col_fwd, col_back, pair_w[depth], pair_b[depth], mixed_in],
                scratch=(wide, wide),
            )
            got = exchange(out)
            if roll_idx == 0 and depth == 0:
                mlp_second, got = lax.optimization_barrier((mlp_line(L - 1, last_chip), got))
            grad_state, state_low, sums_one = launch(
                norm_back_kernel, "norm_back", [state_f32, ((TOK, D), NARROW), ((3, D), f32)],
                [got, g_mixed, state, norms[depth], spread, row_back],
            )
            mlp_terms[depth].append((g_before, hidden_in, hidden, grad_out))
            if roll_idx == 0 and depth == L - 1:
                pairs, sends = mlp_sends(depth)
                grad_state, *sends = lax.optimization_barrier((grad_state, *sends))
                last_sends = (pairs, sends)
            spec_terms[depth].append((g_pair, g_pair_b))
            sum_terms[depth].append((sums_one, sums_two, g_up_b))
        embed_terms.append((current, state_low))
        embed_sums.append(sums_one[2])
        if roll_idx:
            (upstream,) = launch(
                embed_back_kernel, "embed_back", [((TOK, PIX), f32)],
                [state_low, shifts, saved[roll_idx - 1][3], embed_w], far=(3,), scratch=held_embed,
            )

    mlp_first = mlp_line(0, mlp_chip(*mlp_sends(0)))
    mlp_mine = jnp.where(lax.axis_index("zh") == 0, mlp_first, mlp_second)

    def moved_pair(values, amount):
        return jnp.concatenate([jnp.roll(now, amount, axis=0) for now in values], axis=0)

    embed_src = joined(embed_terms, 0)
    head_up = joined(head_terms, 1)
    g_embed = [
        dot_tn(embed_src, moved_pair([now[1] for now in embed_terms], OWN * (o - 1))).astype(NARROW)
        for o in range(3)
    ]
    g_head = [
        dot_tn(moved_pair([now[0] for now in head_terms], -OWN * (o - 1)), head_up).astype(NARROW)
        for o in range(3)
    ]
    g_spec, g_spec_b, g_norm, g_mlp_b = [], [], [], []
    for depth in range(L):
        pair_sum = sum(now[0] for now in spec_terms[depth]).reshape(2, 2, LANES, 2, LANES)
        pair_sum = pair_sum[:, :, :BS, :, :BS]
        g_real = pair_sum[:, 0, :, 0] + pair_sum[:, 1, :, 1]
        g_imag = pair_sum[:, 0, :, 1] - pair_sum[:, 1, :, 0]
        g_spec.append(jnp.stack([g_real, g_imag], axis=1))
        g_spec_b.append(sum(now[1] for now in spec_terms[depth]).reshape(2, 2, LANES)[:, :, :BS])
        one = sum(now[0] for now in sum_terms[depth])
        two = sum(now[1] for now in sum_terms[depth])
        g_norm.append(jnp.stack([one[0], one[1], two[1], two[2]]))
        up_sum = sum(now[2] for now in sum_terms[depth]).reshape(1, 2, 2, 2, -1)
        up_sum = by_place(up_sum.transpose(0, 2, 1, 3, 4)).reshape(-1)
        g_mlp_b.append(jnp.concatenate([up_sum, two[0]]))
    full_spec = jnp.zeros((L, 2, 2, NB, BS, BS), NARROW)
    full_spec = lax.dynamic_update_slice_in_dim(
        full_spec, jnp.stack(g_spec).astype(NARROW)[:, :, :, None], block, 3
    )
    full_spec_b = lax.dynamic_update_slice_in_dim(
        jnp.zeros((L, 2, 2, D), f32), jnp.stack(g_spec_b), block * BS, 3
    )
    small = jnp.concatenate(
        [sum(embed_sums), sum(head_sums)[0], full_spec_b.reshape(-1),
         jnp.stack(g_norm).reshape(-1), jnp.stack(g_mlp_b).reshape(-1)]
    ).astype(NARROW)
    rest_grad = jnp.concatenate([full_spec.reshape(-1), small])
    rest_grad = jnp.pad(rest_grad, (0, -rest_grad.shape[0] % (8 * LANES))).reshape(-1, 8, LANES)
    plan = pack_plan(width, total, devices)
    window_set = ((4, 2, 2, WINDOW, 8, LANES), NARROW)
    kept, sent = launch(
        functools.partial(pack_kernel, plan), "pack", [window_set, window_set],
        [jnp.stack([x, y, c])] + [tiles_of(g) for g in g_embed + g_head] + [rest_grad],
        near=(0,), far_out=True, scratch=(sem((len(plan),)),), limit=8,
    )
    kept = chip_sum(add_low(kept, swap(sent, "c")), 1, 2, 3).reshape(4, WINDOW, 8, LANES)
    flat_piece = own_range(line_sum(kept, [0, 1, 2, 3]), device, width, total, devices)
    local = jnp.stack(
        [jnp.sum(flat_piece * flat_piece) + jnp.sum(mlp_mine * mlp_mine),
         sum(jnp.sum(now) for now in loss_sums)]
    )
    square_sum, loss_total = total_over(local, SUB_AXES)
    loss_total = loss_total / (STEPS * PIX * weight_sum)
    grad_norm = jnp.sqrt(square_sum)
    factor = jnp.minimum(1.0, CLIP_LEVEL / (grad_norm + 1e-06))

    mlp_grad = lax.all_gather(mlp_mine.astype(NARROW), LAT_AXES, axis=0, tiled=True)
    mlp_grad = mlp_grad.reshape(mlp_momentum.shape).astype(f32)
    momentum_new = MOMENT_KEEP * mlp_momentum + mlp_grad * factor

    held = mlp_momentum.reshape(2 * L * 2, rows_own, D)
    held = lax.dynamic_index_in_dim(held, lat_index, 0, keepdims=False)
    mine_new = MOMENT_KEEP * held + mlp_mine * factor
    high = lax.Precision.HIGH
    gram = plane_sum(lax.dot_general(mine_new, mine_new, (((0,), (0,)), ((), ())), precision=high))
    inverse = 1.0 / (jnp.sqrt(jnp.trace(gram)) + 1e-07)
    lead, mid, last = POLY_COEF
    square = gram * (inverse * inverse)
    mul = functools.partial(jnp.dot, precision=high)
    poly_one = mid * square + last * mul(square, square)
    turned = mul(square, poly_one)
    square_two = lead * lead * square + 2.0 * lead * turned + mul(turned, poly_one)
    poly_two = mid * square_two + last * mul(square_two, square_two)
    change = lead * (poly_one + poly_two) + mul(poly_one, poly_two)
    level_high = inverse.astype(NARROW)
    level_mid = (inverse - level_high.astype(f32)).astype(NARROW)
    level_low = (inverse - level_high.astype(f32) - level_mid.astype(f32)).astype(NARROW)
    extra = jnp.zeros((8, D), NARROW)
    extra = extra.at[0, 0].set(level_high).at[0, 1].set(level_mid).at[0, 2].set(level_low)
    change = lax.dynamic_slice_in_dim((change * inverse).astype(NARROW), c * (D // 2), D // 2, 0)
    gathered = line_gather(jnp.concatenate([change, extra], axis=0))
    levels = jnp.sum(gathered[:, D // 2, :3].astype(f32), axis=-1)
    gathered = gathered[:, : D // 2]
    other = swap(gathered, "c")
    changes = jnp.concatenate(
        [jnp.where(c == 0, gathered, other), jnp.where(c == 0, other, gathered)], axis=1
    )
    (mlp_new,) = pl.pallas_call(
        muon_kernel,
        name="muon",
        grid=(2 * L, 2),
        out_shape=[jax.ShapeDtypeStruct((2 * L, D, D), f32)],
        in_specs=[pl.BlockSpec(memory_space=pltpu.SMEM)]
        + [pl.BlockSpec((None, rows_own, D), lambda m, h: (m, h, 0))] * 2
        + [pl.BlockSpec((None, D, D), lambda m, h: (m, 0, 0))],
        out_specs=[pl.BlockSpec((None, rows_own, D), lambda m, h: (m, h, 0))],
        compiler_params=pltpu.CompilerParams(vmem_limit_bytes=28 * 1024 * 1024),
    )(levels, momentum_new.reshape(2 * L, D, D), mlp_weights.reshape(2 * L, D, D), changes)
    mlp_new = mlp_new.reshape(mlp_weights.shape)

    clipped = flat_piece * factor
    first_new = BETA_FIRST * adam_m + (1.0 - BETA_FIRST) * clipped
    second_new = BETA_SECOND * adam_v + (1.0 - BETA_SECOND) * clipped * clipped
    count_value = float(STEP_NUM)
    first_hat = first_new / (1.0 - BETA_FIRST**count_value)
    second_hat = second_new / (1.0 - BETA_SECOND**count_value)
    adam_new = adam_params - ADAM_RATE * (
        first_hat / (jnp.sqrt(second_hat) + 1e-08) + DECAY_RATE * adam_params
    )
    return (adam_new, first_new, second_new, mlp_new, momentum_new, loss_total, grad_norm)


def solution(mesh):
    if tuple(mesh.shape.items()) == (("lat", 8), ("lon", 4)):
        fine = Mesh(mesh.devices.reshape(2, 2, 2, 2, 2), SUB_AXES)
        return placed(fast_body, fine, LAT_AXES, LON_AXES)
    return placed(body, mesh, ("lat",), ("lon",))


def placed(step, mesh, lat, lon):
    flat = P(lat + lon)
    halves = P(None, None, lon, None)
    return jax.shard_map(
        step,
        mesh=mesh,
        in_specs=(
            P(None, lat, lon, None),
            P(None, None, lat, lon, None),
            P(None, lat, lon),
            P(lat),
            flat,
            flat,
            flat,
            halves,
            halves,
        ),
        out_specs=(flat, flat, flat, halves, halves, P(), P()),
        check_vma=False,
    )
```

```python
import functools
import math

import jax
import ml_dtypes
import numpy as np
import jax.numpy as jnp
from jax import lax
from jax.experimental import pallas as pl
from jax.experimental.pallas import tpu as pltpu
from jax.sharding import Mesh
from jax.sharding import PartitionSpec as P

D = 768
FF = 3072
NB = 8
PIX = 1280
BS = 96
L = 2
STEPS = 2
NS_STEPS = 2
STEP_NUM = 5


HIGH_PREC = lax.Precision.HIGHEST
NORM_EPS = 1e-05
CLIP_LEVEL = 0.001
BETA_FIRST = 0.9
BETA_SECOND = 0.95
ADAM_RATE = 0.01
MUON_RATE = 0.8
DECAY_RATE = 0.05
MOMENT_KEEP = 0.95
POLY_COEF = (3.4445, -4.775, 2.0315)


def for_sending(value):

    def short(part):
        return part.astype(jnp.bfloat16) if part.dtype == jnp.float32 else part

    return jax.tree.map(short, value)


def with_halo(block, sides, width):
    for axis, dim in sides:
        count = lax.axis_size(axis)
        forward = [(i, i + 1) for i in range(count - 1)]
        forward.append((count - 1, 0))
        backward = [(target, source) for source, target in forward]
        low = lax.ppermute(
            lax.slice_in_dim(block, block.shape[dim] - width, None, axis=dim), axis, forward
        )
        high = lax.ppermute(lax.slice_in_dim(block, 0, width, axis=dim), axis, backward)
        block = jnp.concatenate([low, block, high], axis=dim)
    return block


def unpack(flat_params):
    layout = [
        (3, PIX, D),
        (3, D, PIX),
        (L, 2, 2, NB, BS, BS),
        (D,),
        (PIX,),
        (L, 2, 2, D),
        (L, 4, D),
        (L, FF + D),
    ]
    pieces_out = []
    offset = 0
    for dims_now in layout:
        amount = math.prod(dims_now)
        pieces_out.append(flat_params[offset : offset + amount].reshape(dims_now))
        offset = offset + amount
    return pieces_out


def along(matrix, values, axis_dim):
    if axis_dim == 1:
        return jnp.einsum("kn,bncd->bkcd", matrix, values, precision=HIGH_PREC)
    return jnp.einsum("kn,brnd->brkd", matrix, values, precision=HIGH_PREC)


def phase_table(out_count, in_count, length_all):
    out_index = jnp.arange(out_count, dtype=jnp.int32)
    in_index = jnp.arange(in_count, dtype=jnp.int32)
    phase = out_index[:, None] * in_index[None, :] % length_all
    angle = phase.astype(jnp.float32) * (2.0 * math.pi / length_all)
    scale_value = 1.0 / math.sqrt(length_all)
    return (jnp.cos(angle) * scale_value, jnp.sin(angle) * scale_value)


def combine(pieces, axis_dim, sign_value, tables, real_only):
    cosine, sine_table = tables
    values = [piece_now.astype(jnp.float32) for piece_now in pieces]
    real_out = along(cosine, values[0], axis_dim)
    if len(values) > 1:
        real_out = real_out - sign_value * along(sine_table, values[1], axis_dim)
    if real_only:
        return (real_out,)
    imag_out = sign_value * along(sine_table, values[0], axis_dim)
    if len(values) > 1:
        imag_out = imag_out + along(cosine, values[1], axis_dim)
    return (real_out, imag_out)


def turn_transform(pieces, axis_dim, sign_value, real_only):
    if axis_dim == 1:
        wide = jax.tree.map(
            lambda part, own: part.astype(own.dtype),
            lax.all_to_all(for_sending(pieces), "lat", split_axis=3, concat_axis=1, tiled=True),
            pieces,
        )
        length_all = wide[0].shape[1]
        result = combine(
            wide, 1, sign_value, phase_table(length_all, length_all, length_all), real_only
        )
        narrow = tuple((piece_now.astype(jnp.bfloat16) for piece_now in result))
        returned = jax.tree.map(
            lambda part, own: part.astype(own.dtype),
            lax.all_to_all(for_sending(narrow), "lat", split_axis=1, concat_axis=3, tiled=True),
            narrow,
        )
        return tuple((piece_now.astype(jnp.float32) for piece_now in returned))
    wide = jax.tree.map(
        lambda part, own: part.astype(own.dtype),
        lax.all_to_all(for_sending(pieces), "lon", split_axis=3, concat_axis=2, tiled=True),
        pieces,
    )
    length_all = wide[0].shape[2]
    result = combine(
        wide, 2, sign_value, phase_table(length_all, length_all, length_all), real_only
    )
    return jax.tree.map(
        lambda part, own: part.astype(own.dtype),
        lax.all_to_all(for_sending(result), "lon", split_axis=2, concat_axis=3, tiled=True),
        result,
    )


def transform(pieces, axis_dim, sign_value, real_only):
    return turn_transform(pieces, axis_dim, sign_value, real_only)


def to_low(pieces):
    return tuple((piece_now.astype(jnp.bfloat16) for piece_now in pieces))


def exact_gelu(values):
    return jax.nn.gelu(values, approximate=False)


def gelu_back(values, upstream):
    return jax.vjp(exact_gelu, values)[1](upstream)[0]


def norm_forward(inputs, gain, shift):
    center = inputs - jnp.mean(inputs, axis=-1, keepdims=True)
    inverse = lax.rsqrt(jnp.mean(center * center, axis=-1, keepdims=True) + NORM_EPS)
    scaled = center * inverse
    return (scaled * gain + shift, (scaled, inverse))


def norm_backward(upstream, saved, gain):
    scaled, inverse = saved
    g_gain = jnp.sum(upstream * scaled, axis=(0, 1, 2))
    g_shift = jnp.sum(upstream, axis=(0, 1, 2))
    g_scaled = upstream * gain
    g_input = inverse * (
        g_scaled
        - jnp.mean(g_scaled, axis=-1, keepdims=True)
        - scaled * jnp.mean(g_scaled * scaled, axis=-1, keepdims=True)
    )
    return (g_input, g_gain, g_shift)


def block_mix(pieces, weights, bias):
    shaped = [piece_now.reshape(piece_now.shape[:-1] + (NB, BS)) for piece_now in pieces]

    def multiply(left_side, right_side):
        return jnp.einsum(
            "brcni,nio->brcno", left_side, right_side, preferred_element_type=jnp.float32
        )

    real_out = multiply(shaped[0], weights[0]) - multiply(shaped[1], weights[1])
    imag_out = multiply(shaped[0], weights[1]) + multiply(shaped[1], weights[0])
    full_dims = pieces[0].shape
    return (
        real_out.reshape(full_dims) + bias[0].astype(jnp.float32),
        imag_out.reshape(full_dims) + bias[1].astype(jnp.float32),
    )


def block_back(grads_low, pieces, weights):
    shaped = [piece_now.reshape(piece_now.shape[:-1] + (NB, BS)) for piece_now in pieces]
    g_shaped = [grad_now.reshape(grad_now.shape[:-1] + (NB, BS)) for grad_now in grads_low]

    def back_multiply(grad_side, weight_side):
        return jnp.einsum(
            "brcno,nio->brcni", grad_side, weight_side, preferred_element_type=jnp.float32
        )

    def weight_multiply(input_side, grad_side):
        return jnp.einsum(
            "brcni,brcno->nio", input_side, grad_side, preferred_element_type=jnp.float32
        )

    g_real = back_multiply(g_shaped[0], weights[0]) + back_multiply(g_shaped[1], weights[1])
    g_imag = back_multiply(g_shaped[1], weights[0]) - back_multiply(g_shaped[0], weights[1])
    g_w_real = weight_multiply(shaped[0], g_shaped[0]) + weight_multiply(shaped[1], g_shaped[1])
    g_w_imag = weight_multiply(shaped[0], g_shaped[1]) - weight_multiply(shaped[1], g_shaped[0])
    g_bias = jnp.stack(
        [jnp.sum(grad_now.astype(jnp.float32), axis=(0, 1, 2)) for grad_now in grads_low]
    )
    full_dims = pieces[0].shape
    return (
        (g_real.reshape(full_dims), g_imag.reshape(full_dims)),
        jnp.stack([g_w_real, g_w_imag]),
        g_bias,
    )


def halo_rows(values):
    return with_halo(values, (("lat", 1),), 1)


def rows_conv(source_low, weight3, bias):
    padded = halo_rows(source_low)
    row_count = source_low.shape[1]
    window = jnp.concatenate(
        [padded[:, offset : offset + row_count] for offset in range(3)], axis=-1
    )
    flat_weight = weight3.reshape(-1, weight3.shape[-1])
    result = jnp.einsum("brci,io->brco", window, flat_weight, preferred_element_type=jnp.float32)
    return (result + bias.astype(jnp.float32), window)


def rows_back(grad_low, weight3, need_source):
    g_bias = jnp.sum(grad_low.astype(jnp.float32), axis=(0, 1, 2))
    if not need_source:
        return (g_bias, None)
    padded = halo_rows(grad_low)
    row_count = grad_low.shape[1]
    window_back = jnp.concatenate(
        [padded[:, 2 - offset : 2 - offset + row_count] for offset in range(3)], axis=-1
    )
    flipped = jnp.transpose(weight3, (0, 2, 1)).reshape(-1, weight3.shape[1])
    g_source = jnp.einsum("brco,oi->brci", window_back, flipped, preferred_element_type=jnp.float32)
    return (g_bias, g_source)


def conv_weight_grad(terms_list, weight3):
    window = jnp.concatenate([terms_now[0] for terms_now in terms_list], axis=0)
    grads_low = jnp.concatenate([terms_now[1] for terms_now in terms_list], axis=0)
    return jnp.einsum(
        "brci,brco->io", window, grads_low, preferred_element_type=jnp.float32
    ).reshape(weight3.shape)


def layer_forward(state, params_now):
    spec_w, spec_b, norm_vals, mlp_pair, mlp_bias = params_now
    normed, first_saved = norm_forward(state, norm_vals[0], norm_vals[1])
    spectrum = transform((normed.astype(jnp.bfloat16),), 2, -1.0, False)
    spectrum = transform(to_low(spectrum), 1, -1.0, False)
    mixed_in = to_low(spectrum)
    inner = block_mix(mixed_in, spec_w[0], spec_b[0])
    activated = to_low(tuple((exact_gelu(piece_now) for piece_now in inner)))
    outer = block_mix(activated, spec_w[1], spec_b[1])
    spectrum = transform(to_low(outer), 1, 1.0, False)
    spatial = transform(to_low(spectrum), 2, 1.0, True)[0]
    mixed = state + spatial + normed
    second, second_saved = norm_forward(mixed, norm_vals[2], norm_vals[3])
    hidden_in = second.astype(jnp.bfloat16)
    before = (
        jnp.einsum("brcd,fd->brcf", hidden_in, mlp_pair[0], preferred_element_type=jnp.float32)
        + mlp_bias[:FF]
    )
    hidden = exact_gelu(before).astype(jnp.bfloat16)
    result = (
        jnp.einsum("brcf,fd->brcd", hidden, mlp_pair[1], preferred_element_type=jnp.float32)
        + mlp_bias[FF:]
    )
    return (
        mixed + result,
        (first_saved, mixed_in, inner, activated, second_saved, hidden_in, before, hidden),
    )


def layer_backward(upstream, cache, params_now):
    spec_w, spec_b, norm_vals, mlp_pair, mlp_bias = params_now
    first_saved, mixed_in, inner, activated, second_saved, hidden_in, before, hidden = cache
    grad_out = upstream.astype(jnp.bfloat16)
    g_down_bias = jnp.sum(grad_out.astype(jnp.float32), axis=(0, 1, 2))
    g_hidden = jnp.einsum(
        "brcd,fd->brcf", grad_out, mlp_pair[1], preferred_element_type=jnp.float32
    )
    g_before = gelu_back(before, g_hidden).astype(jnp.bfloat16)
    g_up_bias = jnp.sum(g_before.astype(jnp.float32), axis=(0, 1, 2))
    g_second = jnp.einsum(
        "brcf,fd->brcd", g_before, mlp_pair[0], preferred_element_type=jnp.float32
    )
    g_norm_in, g_gain_two, g_shift_two = norm_backward(g_second, second_saved, norm_vals[2])
    g_mixed = upstream + g_norm_in
    g_spectrum = transform((g_mixed.astype(jnp.bfloat16),), 2, -1.0, False)
    g_outer = to_low(transform(to_low(g_spectrum), 1, -1.0, False))
    g_activated, g_w_outer, g_b_outer = block_back(g_outer, activated, spec_w[1])
    g_inner = to_low(
        tuple((gelu_back(piece_now, grad_now) for piece_now, grad_now in zip(inner, g_activated)))
    )
    g_mixed_in, g_w_inner, g_b_inner = block_back(g_inner, mixed_in, spec_w[0])
    g_spectrum = transform(to_low(g_mixed_in), 1, 1.0, False)
    g_normed = transform(to_low(g_spectrum), 2, 1.0, True)[0] + g_mixed
    g_state_norm, g_gain_one, g_shift_one = norm_backward(g_normed, first_saved, norm_vals[0])
    layer_grads = (
        jnp.stack([g_w_inner, g_w_outer]),
        jnp.stack([g_b_inner, g_b_outer]),
        jnp.stack([g_gain_one, g_shift_one, g_gain_two, g_shift_two]),
        jnp.concatenate([g_up_bias, g_down_bias]),
    )
    return (g_mixed + g_state_norm, layer_grads, (hidden, grad_out, g_before, hidden_in))


def body(pixels, targets, mask, lat_rows, adam_params, adam_m, adam_v, mlp_weights, mlp_momentum):
    flat_low = lax.all_gather(adam_params.astype(jnp.bfloat16), ("lat", "lon"), axis=0, tiled=True)
    mlp_low = lax.all_gather(mlp_weights.astype(jnp.bfloat16), "lon", axis=2, tiled=True)
    embed_w, head_w, spec_w, embed_b, head_b, spec_b, norm_params, mlp_b = unpack(flat_low)
    row_count = pixels.shape[1]
    lat_total = lax.axis_size("lat") * row_count
    row_weight = jnp.sin(math.pi * (lat_rows.astype(jnp.float32) + 0.5) / lat_total)
    weight_map = row_weight[None, :, None] * mask.astype(jnp.float32)
    weight_sum = lax.psum(jnp.sum(weight_map), ("lat", "lon"))
    loss_scale = 2.0 / (STEPS * PIX * weight_sum)

    def params_at(depth_idx):
        return (
            spec_w[depth_idx],
            spec_b[depth_idx],
            norm_params[depth_idx].astype(jnp.float32),
            mlp_low[depth_idx],
            mlp_b[depth_idx].astype(jnp.float32),
        )

    current = pixels
    saved_steps = []
    loss_local = jnp.zeros((), jnp.float32)
    for roll_idx in range(STEPS):
        state, embed_window = rows_conv(current.astype(jnp.bfloat16), embed_w, embed_b)
        caches = []
        for depth_idx in range(L):
            state, cache_now = layer_forward(state, params_at(depth_idx))
            caches.append(cache_now)
        predicted, head_window = rows_conv(state.astype(jnp.bfloat16), head_w, head_b)
        differ = predicted - targets[roll_idx].astype(jnp.float32)
        loss_local = loss_local + jnp.sum(weight_map[..., None] * differ * differ)
        saved_steps.append(
            (embed_window, caches, head_window, weight_map[..., None] * differ * loss_scale)
        )
        current = predicted
    g_embed_b = jnp.zeros(embed_b.shape, jnp.float32)
    g_head_b = jnp.zeros(head_b.shape, jnp.float32)
    head_terms = []
    embed_terms = []
    mlp_terms = [[] for unused in range(L)]
    g_layers = [None] * L
    carried = None
    for roll_idx in reversed(range(STEPS)):
        embed_window, caches, head_window, loss_grad = saved_steps[roll_idx]
        upstream = loss_grad if carried is None else loss_grad + carried
        upstream_low = upstream.astype(jnp.bfloat16)
        head_terms.append((head_window, upstream_low))
        grad_b, grad_state = rows_back(upstream_low, head_w, True)
        g_head_b = g_head_b + grad_b
        for depth_idx in reversed(range(L)):
            grad_state, layer_grads, mlp_now = layer_backward(
                grad_state, caches[depth_idx], params_at(depth_idx)
            )
            mlp_terms[depth_idx].append(mlp_now)
            if g_layers[depth_idx] is None:
                g_layers[depth_idx] = layer_grads
            else:
                g_layers[depth_idx] = jax.tree.map(jnp.add, g_layers[depth_idx], layer_grads)
        state_low = grad_state.astype(jnp.bfloat16)
        embed_terms.append((embed_window, state_low))
        grad_b, carried = rows_back(state_low, embed_w, roll_idx > 0)
        g_embed_b = g_embed_b + grad_b
    g_embed_w = conv_weight_grad(embed_terms, embed_w)
    g_head_w = conv_weight_grad(head_terms, head_w)
    mlp_grads = []
    for depth_idx in range(L):
        joined = [
            jnp.concatenate([terms_now[member] for terms_now in mlp_terms[depth_idx]], axis=0)
            for member in range(4)
        ]
        g_up = jnp.einsum("brcf,brcd->fd", joined[2], joined[3], preferred_element_type=jnp.float32)
        g_down = jnp.einsum(
            "brcf,brcd->fd", joined[0], joined[1], preferred_element_type=jnp.float32
        )
        mlp_grads.append(jnp.stack([g_up, g_down]))
    full_mlp = jnp.stack(mlp_grads)
    stacked = [
        jnp.stack([g_layers[depth_idx][member] for depth_idx in range(L)]) for member in range(4)
    ]
    flat_grad = jnp.concatenate(
        [
            g_embed_w.reshape(-1),
            g_head_w.reshape(-1),
            stacked[0].reshape(-1),
            g_embed_b,
            g_head_b,
            stacked[1].reshape(-1),
            stacked[2].reshape(-1),
            stacked[3].reshape(-1),
        ]
    )
    lon_count = lax.axis_size("lon")
    lat_count = lax.axis_size("lat")
    dev_count = lon_count * lat_count
    per_block = full_mlp.shape[2] // dev_count
    mlp_rows = (
        full_mlp.reshape(L, 2, lon_count, lat_count, per_block, D)
        .transpose(3, 2, 0, 1, 4, 5)
        .reshape(dev_count, -1)
    )
    flat_rows = flat_grad.reshape(dev_count, -1)
    flat_width = flat_rows.shape[1]
    summed = lax.psum_scatter(
        jnp.concatenate([flat_rows, mlp_rows], axis=1),
        ("lat", "lon"),
        scatter_dimension=0,
        tiled=True,
    )[0]
    flat_piece = summed[:flat_width]
    mlp_piece = summed[flat_width:].reshape(L, 2, per_block, D)
    local_square = jnp.sum(flat_piece * flat_piece) + jnp.sum(mlp_piece * mlp_piece)
    loss_total, square_sum = lax.psum(
        (loss_local / (STEPS * PIX * weight_sum), local_square), ("lat", "lon")
    )
    mlp_grad = lax.all_gather(mlp_piece.astype(jnp.bfloat16), "lat", axis=2, tiled=True).astype(
        mlp_piece.dtype
    )
    grad_norm = jnp.sqrt(square_sum)
    factor = jnp.minimum(1.0, CLIP_LEVEL / (grad_norm + 1e-06))
    clipped = flat_piece * factor
    first_new = BETA_FIRST * adam_m + (1.0 - BETA_FIRST) * clipped
    second_new = BETA_SECOND * adam_v + (1.0 - BETA_SECOND) * clipped * clipped
    count_value = float(STEP_NUM)
    first_hat = first_new / (1.0 - BETA_FIRST**count_value)
    second_hat = second_new / (1.0 - BETA_SECOND**count_value)
    adam_new = adam_params - ADAM_RATE * (
        first_hat / (jnp.sqrt(second_hat) + 1e-08) + DECAY_RATE * adam_params
    )
    momentum_new = MOMENT_KEEP * mlp_momentum + mlp_grad * factor
    ortho = momentum_new
    for ns_idx in range(NS_STEPS):
        partial_gram = jnp.einsum("lkfd,lkfe->lkde", ortho, ortho, precision=HIGH_PREC)
        square = lax.psum(partial_gram.astype(jnp.bfloat16), "lon").astype(jnp.float32)
        if ns_idx == 0:
            trace_val = jnp.trace(square, axis1=2, axis2=3)
            inverse = 1.0 / (jnp.sqrt(trace_val) + 1e-07)
            ortho = ortho * inverse[:, :, None, None]
            square = square * (inverse * inverse)[:, :, None, None]
        poly = POLY_COEF[1] * square + POLY_COEF[2] * jnp.einsum(
            "lkde,lkef->lkdf", square, square, precision=HIGH_PREC
        )
        ortho = POLY_COEF[0] * ortho + jnp.einsum(
            "lkfd,lkde->lkfe", ortho, poly, precision=HIGH_PREC
        )
    mlp_new = mlp_weights * (1.0 - MUON_RATE * DECAY_RATE) - MUON_RATE * (FF / D) ** 0.5 * ortho
    return (adam_new, first_new, second_new, mlp_new, momentum_new, loss_total, grad_norm)


ROWS = 48
COLS = 48
GROUP = 16
OWN = 3
TOK = ROWS * OWN
HALF_TOK = TOK // 2
PAIRS = 12
LANES = 128
WIDE = NB * LANES
FREQ = PAIRS * 96
NARROW = jnp.bfloat16
WINDOW = 212
EMBED_AT = 2
Z_AXES = ("zh", "zl")
EMBED_SIZE = 3 * PIX * D
SUB_AXES = ("zh", "zl", "x", "y", "c")
LAT_AXES = ("zh", "zl", "x")
LON_AXES = ("y", "c")
ITEM_AXES = ("zl", "x", "y", "c")


def shift_tables():
    table = np.zeros((3, TOK, TOK), np.float32)
    spots = np.arange(TOK)
    for offset in range(3):
        table[offset, spots, (spots + OWN * (offset - 1)) % TOK] = 1.0
    return table


def row_table():
    table = np.zeros((TOK, TOK), np.float64)
    rows = np.arange(ROWS)
    for pair in range(2 * PAIRS):
        if pair == 0:
            waves = (np.ones(ROWS), np.cos(np.pi * rows))
        else:
            angle = 2.0 * np.pi * (pair * rows % ROWS) / ROWS
            waves = (np.cos(angle), np.sin(angle))
        for part in range(2):
            for own in range(OWN):
                table[pair * 6 + part * OWN + own, rows * OWN + own] = waves[part]
    return table / math.sqrt(ROWS)


def column_tables():
    freq = np.arange(COLS)[:, None]
    table = np.zeros((2, 192, 128), np.float64)
    for source in range(GROUP):
        quad, lon = source // 4, source % 4
        for own in range(OWN):
            column = lon * 12 + quad * OWN + own
            angle = 2.0 * np.pi * (freq[:, 0] * column % COLS) / COLS
            cosine, sine = np.cos(angle), np.sin(angle)
            first, second = source * 8 + own, source * 8 + OWN + own
            table[0, 0:48, first] = cosine
            table[0, 96:144, first] = -sine
            table[0, 48:96, second] = cosine
            table[0, 144:192, second] = -sine
            table[1, 0:48, first] = cosine
            table[1, 48:96, first] = cosine
            table[1, 96:144, first] = -sine
            table[1, 144:192, first] = -sine
            table[1, 0:48, second] = -sine
            table[1, 48:96, second] = sine
            table[1, 96:144, second] = -cosine
            table[1, 144:192, second] = cosine
    return table / math.sqrt(COLS)


def spread_table():
    table = np.zeros((384, 512), np.float32)
    spots = np.arange(384)
    table[spots, spots // BS * LANES + spots % BS] = 1.0
    return table


def two_terms(table):
    high = table.astype(ml_dtypes.bfloat16)
    low = (table - high.astype(np.float64)).astype(ml_dtypes.bfloat16)
    return np.stack([high, low])


def dot(left, right):
    return lax.dot_general(left, right, (((1,), (0,)), ((), ())), preferred_element_type=jnp.float32)


def dot_nt(left, right):
    return lax.dot_general(left, right, (((1,), (1,)), ((), ())), preferred_element_type=jnp.float32)


def dot_tn(left, right):
    return lax.dot_general(left, right, (((0,), (0,)), ((), ())), preferred_element_type=jnp.float32)


def normalize(values):
    center = values - jnp.mean(values, axis=-1, keepdims=True)
    inverse = lax.rsqrt(jnp.mean(center * center, axis=-1, keepdims=True) + NORM_EPS)
    return center * inverse, inverse


def normalize_back(upstream, scaled, inverse, gain):
    inner = upstream * gain
    return inverse * (
        inner
        - jnp.mean(inner, axis=-1, keepdims=True)
        - scaled * jnp.mean(inner * scaled, axis=-1, keepdims=True)
    )


def column_sum(values):
    return jnp.sum(values, axis=0, keepdims=True)


def bell(values):
    return 0.5 * (1.0 + lax.erf(values * math.sqrt(0.5)))


def bell_slope(values, area):
    return area + values * jnp.exp(-0.5 * values * values) * (1.0 / math.sqrt(2.0 * math.pi))


def send_rows(low, spread_ref, row_ref, out_ref):
    wide = jnp.concatenate(
        [dot(low[:, :384], spread_ref[...]), dot(low[:, 384:], spread_ref[...])], axis=1
    ).astype(NARROW)
    turned = dot(row_ref[0], wide) + dot(row_ref[1], wide)
    for side in range(2):
        for block in range(NB):
            out_ref[side * NB + block] = turned[
                side * HALF_TOK : (side + 1) * HALF_TOK, block * LANES : (block + 1) * LANES
            ].astype(NARROW)


def take_rows(in_ref, spread_ref, row_back_ref):
    sides = []
    for side in range(2):
        sides.append(
            jnp.concatenate(
                [in_ref[side * NB + block].astype(jnp.float32) for block in range(NB)], axis=1
            )
        )
    wide = jnp.concatenate(sides, axis=0).astype(NARROW)
    low = jnp.concatenate(
        [dot_nt(wide[:, :512], spread_ref[...]), dot_nt(wide[:, 512:], spread_ref[...])], axis=1
    ).astype(NARROW)
    return dot(row_back_ref[0], low) + dot(row_back_ref[1], low)


def fetch(sources, held_ref, sems):
    copies = [pltpu.make_async_copy(src, held_ref.at[i], sems.at[i]) for i, src in enumerate(sources)]
    for copy in copies:
        copy.start()
    return copies


def thirds(w_ref, size):
    return [w_ref[i * size : (i + 1) * size] for i in range(3)]


def embed_kernel(src_ref, shift_ref, bias_ref, norm_ref, spread_ref, row_ref, w_ref,
                 state_ref, send_ref):
    src = src_ref[...]
    state = bias_ref[...]
    for offset, weight in enumerate(thirds(w_ref, PIX)):
        moved = src if offset == 1 else dot(shift_ref[offset], src).astype(NARROW)
        state = state + dot(moved, weight)
    state_ref[...] = state
    scaled, _unused = normalize(state)
    normed = scaled * norm_ref[0:1] + norm_ref[1:2]
    send_rows(normed.astype(NARROW), spread_ref, row_ref, send_ref)


def turn_columns(wide_ref, col_ref, pair):
    kind = 0 if pair == 0 else 1
    low = wide_ref[:, 6 * pair : 6 * pair + 8, :].reshape(128, 128).astype(NARROW)
    both = dot(col_ref[0, kind], low) + dot(col_ref[1, kind], low)
    return jnp.concatenate([both[:96], both[96:]], axis=1).astype(NARROW)


def back_columns(wide_ref, col_back_ref, pair, low):
    kind = 0 if pair == 0 else 1
    both = jnp.concatenate([low[:, :128], low[:, 128:]], axis=0)
    back = dot(col_back_ref[0, kind], both) + dot(col_back_ref[1, kind], both)
    wide_ref[:, 6 * pair : 6 * pair + 8, :] = back.reshape(16, 8, 128)


def spec_kernel(
    in_ref, col_ref, col_back_ref, w_ref, b_ref, out_ref, mixed_ref, wide_ref, wide_out_ref
):
    wide_ref[:, :HALF_TOK, :] = in_ref[...].astype(jnp.float32)
    wide_ref[:, HALF_TOK:, :] = jnp.zeros((16, 8, 128), jnp.float32)
    for chunk in range(4):
        pairs = range(chunk * 3, chunk * 3 + 3)
        mixed = jnp.concatenate([turn_columns(wide_ref, col_ref, pair) for pair in pairs], axis=0)
        mixed_ref[chunk * 288 : (chunk + 1) * 288, :] = mixed
        inner = dot(mixed, w_ref[0]) + b_ref[0:1]
        act = (inner * bell(inner)).astype(NARROW)
        outer = (dot(act, w_ref[1]) + b_ref[1:2]).astype(NARROW)
        for place, pair in enumerate(pairs):
            back_columns(wide_out_ref, col_back_ref, pair, outer[place * 96 : place * 96 + 96])
    out_ref[...] = wide_out_ref[:, :HALF_TOK, :].astype(NARROW)


def spec_back_kernel(
    in_ref, col_ref, col_back_ref, w_ref, b_ref, mixed_ref,
    out_ref, gw_ref, gb_ref, wide_ref, wide_out_ref,
):
    wide_ref[:, :HALF_TOK, :] = in_ref[...].astype(jnp.float32)
    wide_ref[:, HALF_TOK:, :] = jnp.zeros((16, 8, 128), jnp.float32)
    for chunk in range(4):
        pairs = range(chunk * 3, chunk * 3 + 3)
        g_outer = jnp.concatenate([turn_columns(wide_ref, col_ref, pair) for pair in pairs], axis=0)
        mixed = mixed_ref[chunk * 288 : (chunk + 1) * 288, :]
        inner = dot(mixed, w_ref[0]) + b_ref[0:1]
        area = bell(inner)
        act = (inner * area).astype(NARROW)
        g_inner = (bell_slope(inner, area) * dot_nt(g_outer, w_ref[1])).astype(NARROW)
        g_mixed = dot_nt(g_inner, w_ref[0]).astype(NARROW)
        first, second = dot_tn(mixed, g_inner), dot_tn(act, g_outer)
        sums = jnp.concatenate(
            [column_sum(g_inner.astype(jnp.float32)), column_sum(g_outer.astype(jnp.float32))], axis=0
        )
        if chunk == 0:
            gw_ref[0], gw_ref[1], gb_ref[...] = first, second, sums
        else:
            gw_ref[0] += first
            gw_ref[1] += second
            gb_ref[...] += sums
        for place, pair in enumerate(pairs):
            back_columns(wide_out_ref, col_back_ref, pair, g_mixed[place * 96 : place * 96 + 96])
    out_ref[...] = wide_out_ref[:, :HALF_TOK, :].astype(NARROW)


def mlp_kernel(has_next, in_ref, state_ref, norm_ref, next_norm_ref, up_b_ref, down_b_ref,
               spread_ref, row_ref, row_back_ref, w0_ref, w1_ref, w2_ref, w3_ref, *rest):
    held_ref, sems = rest[-2:]
    mixed_ref, hidden_in_ref, before_ref, hidden_ref, out_ref = rest[:5]
    copies = fetch((w0_ref, w1_ref, w2_ref, w3_ref), held_ref, sems)
    spatial = take_rows(in_ref, spread_ref, row_back_ref)
    state = state_ref[...]
    scaled, _unused = normalize(state)
    mixed = state + spatial + (scaled * norm_ref[0:1] + norm_ref[1:2])
    mixed_ref[...] = mixed
    again, _unused = normalize(mixed)
    hidden_in = (again * norm_ref[2:3] + norm_ref[3:4]).astype(NARROW)
    hidden_in_ref[...] = hidden_in
    out = mixed + down_b_ref[...]
    for part in range(4):
        spot = slice(part * D, (part + 1) * D)
        copies[part].wait()
        before = dot_nt(hidden_in, held_ref[part, 0]) + up_b_ref[:, spot]
        before_ref[:, spot] = before
        hidden = (before * bell(before)).astype(NARROW)
        hidden_ref[:, spot] = hidden
        out = out + dot(hidden, held_ref[part, 1])
    out_ref[...] = out
    if has_next:
        scaled, _unused = normalize(out)
        normed = scaled * next_norm_ref[0:1] + next_norm_ref[1:2]
        send_rows(normed.astype(NARROW), spread_ref, row_ref, rest[5])


def head_kernel(state_ref, shift_ref, bias_ref, target_ref, weight_ref, w_ref,
                low_ref, pred_ref, grad_ref, loss_ref):
    low = state_ref[...].astype(NARROW)
    low_ref[...] = low
    predicted = bias_ref[...]
    for offset, weight in enumerate(thirds(w_ref, D)):
        moved = low if offset == 1 else dot(shift_ref[offset], low).astype(NARROW)
        predicted = predicted + dot(moved, weight)
    pred_ref[...] = predicted.astype(NARROW)
    differ = predicted - target_ref[...].astype(jnp.float32)
    loss_ref[...] = column_sum(weight_ref[:, 0:1] * differ * differ)
    grad_ref[...] = weight_ref[:, 1:2] * differ


def head_back_kernel(grad_ref, shift_ref, w_ref, low_ref, sum_ref, out_ref):
    low = grad_ref[...].astype(NARROW)
    low_ref[...] = low
    sum_ref[...] = column_sum(low.astype(jnp.float32))
    total = None
    for offset, weight in enumerate(thirds(w_ref, D)):
        moved = low if offset == 1 else dot(shift_ref[2 - offset], low).astype(NARROW)
        part = dot_nt(moved, weight)
        total = part if total is None else total + part
    out_ref[...] = total


def embed_back_kernel(low_ref, shift_ref, add_ref, w_ref, out_ref):
    low = low_ref[...]
    total = add_ref[...]
    for offset, weight in enumerate(thirds(w_ref, PIX)):
        moved = low if offset == 1 else dot(shift_ref[2 - offset], low).astype(NARROW)
        total = total + dot_nt(moved, weight)
    out_ref[...] = total


def mlp_back_kernel(up_ref, before_ref, mixed_ref, norm_ref, spread_ref, row_ref,
                    w0_ref, w1_ref, w2_ref, w3_ref,
                    grad_out_ref, g_before_ref, g_mixed_ref, g_up_b_ref, sums_ref, send_ref,
                    held_ref, sems):
    copies = fetch((w0_ref, w1_ref, w2_ref, w3_ref), held_ref, sems)
    upstream = up_ref[...]
    grad_out = upstream.astype(NARROW)
    grad_out_ref[...] = grad_out
    sums_ref[0:1] = column_sum(grad_out.astype(jnp.float32))
    g_second = None
    for part in range(4):
        spot = slice(part * D, (part + 1) * D)
        before = before_ref[:, spot]
        slope = bell_slope(before, bell(before))
        copies[part].wait()
        g_before = (slope * dot_nt(grad_out, held_ref[part, 1])).astype(NARROW)
        g_before_ref[:, spot] = g_before
        g_up_b_ref[:, spot] = column_sum(g_before.astype(jnp.float32))
        now = dot(g_before, held_ref[part, 0])
        g_second = now if g_second is None else g_second + now
    scaled, inverse = normalize(mixed_ref[...])
    sums_ref[1:2] = column_sum(g_second * scaled)
    sums_ref[2:3] = column_sum(g_second)
    g_mixed = upstream + normalize_back(g_second, scaled, inverse, norm_ref[2:3])
    g_mixed_ref[...] = g_mixed
    send_rows(g_mixed.astype(NARROW), spread_ref, row_ref, send_ref)


def norm_back_kernel(in_ref, g_mixed_ref, state_ref, norm_ref, spread_ref, row_back_ref,
                     out_ref, low_ref, sums_ref):
    g_mixed = g_mixed_ref[...]
    g_normed = take_rows(in_ref, spread_ref, row_back_ref) + g_mixed
    scaled, inverse = normalize(state_ref[...])
    out = g_mixed + normalize_back(g_normed, scaled, inverse, norm_ref[0:1])
    out_ref[...] = out
    low = out.astype(NARROW)
    low_ref[...] = low
    sums_ref[0:1] = column_sum(g_normed * scaled)
    sums_ref[1:2] = column_sum(g_normed)
    sums_ref[2:3] = column_sum(low.astype(jnp.float32))


def narrow_kernel(place_ref, in_ref, out_ref):
    out_ref[...] = in_ref[...].astype(NARROW)


def own_quarters(weights, place):
    size = weights.shape[1] // 4

    def from_spot(m, q, place_ref):
        return (m, (q // 2 + place_ref[0]) % 2 * 2 + (q % 2 + place_ref[1]) % 2, 0)

    return pl.pallas_call(
        narrow_kernel,
        name="narrow",
        out_shape=jax.ShapeDtypeStruct(weights.shape, NARROW),
        grid_spec=pltpu.PrefetchScalarGridSpec(
            num_scalar_prefetch=1,
            grid=(weights.shape[0], 4),
            in_specs=[pl.BlockSpec((None, size, D), from_spot)],
            out_specs=pl.BlockSpec((None, size, D), lambda m, q, place_ref: (m, q, 0)),
        ),
    )(place, weights)


def muon_kernel(level_ref, momentum_ref, weight_ref, change_ref, out_ref):
    momentum = momentum_ref[...]
    ortho = POLY_COEF[0] * POLY_COEF[0] * level_ref[pl.program_id(0)] * momentum
    ortho = ortho + dot(momentum.astype(NARROW), change_ref[...])
    out_ref[...] = weight_ref[...] * (1.0 - MUON_RATE * DECAY_RATE) - MUON_RATE * (FF / D) ** 0.5 * ortho


def launch(kernel, name, out_dims, operands, far=(), far_out=False, near=(), scratch=(), limit=16):
    anywhere = pl.BlockSpec(memory_space=pltpu.HBM)
    local = pl.BlockSpec(memory_space=pltpu.VMEM)
    in_specs = []
    for i in range(len(operands)):
        if i in near:
            in_specs.append(pl.BlockSpec(memory_space=pltpu.SMEM))
        else:
            in_specs.append(anywhere if i in far else local)
    return pl.pallas_call(
        kernel,
        name=name,
        out_shape=[jax.ShapeDtypeStruct(dims, kind) for dims, kind in out_dims],
        in_specs=in_specs,
        out_specs=[anywhere if far_out else local for unused in out_dims],
        scratch_shapes=list(scratch),
        compiler_params=pltpu.CompilerParams(vmem_limit_bytes=limit * 1024 * 1024),
    )(*operands)


def exchange(values):
    return lax.all_to_all(values, ITEM_AXES, split_axis=0, concat_axis=0, tiled=True)


def total_over(values, axes):
    count = lax.axis_size(axes)
    spread = jnp.broadcast_to(jnp.pad(values, (0, LANES - values.shape[0])), (count, 1, LANES))
    got = lax.all_to_all(spread, axes, split_axis=0, concat_axis=0, tiled=True)
    return jnp.sum(got, axis=(0, 1))[: values.shape[0]]


KINDS = {"embed": (D, 6), "head": (PIX, 10), "rest": (LANES, 1)}


def kind_ranges(total):
    edges = (0, EMBED_SIZE, 2 * EMBED_SIZE, total)
    return dict(zip(KINDS, zip(edges[:-1], edges[1:])))


def window_pieces(index, width, total):
    found = []
    for kind, (low, high) in kind_ranges(total).items():
        begin, end = max(index * width, low), min((index + 1) * width, high)
        if begin >= end:
            continue
        row, tiles = KINDS[kind]
        first = (begin - low) // (8 * row)
        last = -(-(end - low) // (8 * row))
        found.append([kind, first, last, 0, begin, end])
    spot = {"embed": EMBED_AT, "head": 0, "rest": 0}
    kinds = [piece[0] for piece in found]
    for piece in found:
        piece[3] = spot[piece[0]]
    if kinds == ["embed", "head"]:
        used = (found[1][2] - found[1][1]) * 10
        found[0][3] = EMBED_AT + -(-(used - EMBED_AT) // 6) * 6
    if kinds == ["head", "rest"]:
        found[1][3] = (found[0][2] - found[0][1]) * 10
    for piece in found:
        assert piece[3] + (piece[2] - piece[1]) * KINDS[piece[0]][1] <= WINDOW
    return found


def form_range(kind, device, width, total, count):
    row, tiles = KINDS[kind]
    base, edge = kind_ranges(total)[kind]
    origin = device * width
    low = jnp.clip(base - origin, 0, width)
    high = jnp.clip(edge - origin, 0, width)
    inside = jnp.maximum(origin - base, 0)
    start = inside % (8 * row) - low
    first = EMBED_AT if kind == "embed" else 0
    for index in range(count):
        for piece in window_pieces(index, width, total):
            if piece[0] == kind and piece[3] != first:
                start = start + jnp.where(device == index, (piece[3] - first) * 8 * LANES, 0)
    return start, low, high


def form_tiles(kind):
    if kind == "embed":
        return EMBED_AT, (WINDOW - EMBED_AT) // 6
    return (0, WINDOW // 10) if kind == "head" else (0, WINDOW)


def own_window(own, device, width, total, count):
    spot = jnp.arange(width, dtype=jnp.int32)
    window = jnp.zeros((WINDOW, 8, LANES), jnp.float32)
    for kind, (row, tiles) in KINDS.items():
        start, low, high = form_range(kind, device, width, total, count)
        first, groups = form_tiles(kind)
        length = groups * tiles * 8 * LANES
        held = jnp.where((spot >= low) & (spot < high), own, 0.0)
        held = jnp.pad(held, (length, length))
        form = lax.dynamic_slice(held, (length - start,), (length,))
        form = form.reshape(groups, 8, tiles, LANES).transpose(0, 2, 1, 3).reshape(-1, 8, LANES)
        window = window + jnp.pad(form, ((first, WINDOW - first - groups * tiles), (0, 0), (0, 0)))
    return window


def own_range(window, device, width, total, count):
    spot = jnp.arange(width, dtype=jnp.int32)
    result = jnp.zeros((width,), jnp.float32)
    for kind, (row, tiles) in KINDS.items():
        start, low, high = form_range(kind, device, width, total, count)
        first, groups = form_tiles(kind)
        form = window[first : first + groups * tiles].reshape(groups, tiles, 8, LANES)
        form = jnp.pad(form.transpose(0, 2, 1, 3).reshape(-1), (width, width))
        held = lax.dynamic_slice(form, (width + start,), (width,))
        result = jnp.where((spot >= low) & (spot < high), held, result)
    return result


def join_plan(kind, width, total, count):
    pieces = []
    for index in range(count):
        for piece in window_pieces(index, width, total):
            if piece[0] == kind:
                pieces.append((index,) + tuple(piece[1:4]))
    single, double = [], []
    for place, (index, first, last, tile) in enumerate(pieces):
        if place:
            shared = pieces[place - 1][2]
            before = pieces[place - 1]
            if shared > first:
                double.append((first, shared, before[0], before[3], before[1], index, tile))
        else:
            shared = first
        follow = pieces[place + 1][1] if place + 1 < len(pieces) else last
        begin, end = max(first, shared), min(last, follow)
        if begin < end:
            single.append((begin, end, index, tile, first))
    return single, double


def join_kernel(tiles, single, double, got_ref, out_ref, left_ref, right_ref, sems, left_sems, right_sems):
    copies = []
    for place, (begin, end, index, tile, first) in enumerate(single):
        source = got_ref.at[index, pl.ds(tile + (begin - first) * tiles, (end - begin) * tiles)]
        target = out_ref.at[pl.ds(begin * tiles, (end - begin) * tiles)]
        copies.append(pltpu.make_async_copy(source, target, sems.at[place]))
    loads = []
    for place, (begin, end, before, before_tile, before_first, index, tile) in enumerate(double):
        size = (end - begin) * tiles
        source = got_ref.at[before, pl.ds(before_tile + (begin - before_first) * tiles, size)]
        loads.append(pltpu.make_async_copy(source, left_ref.at[place, pl.ds(0, size)], left_sems.at[place]))
        source = got_ref.at[index, pl.ds(tile, size)]
        loads.append(pltpu.make_async_copy(source, right_ref.at[place, pl.ds(0, size)], right_sems.at[place]))
    for copy in loads + copies:
        copy.start()
    for copy in loads:
        copy.wait()
    stores = []
    for place, (begin, end, *unused) in enumerate(double):
        size = (end - begin) * tiles
        total = left_ref[place, :size].astype(jnp.float32) + right_ref[place, :size].astype(jnp.float32)
        left_ref[place, :size] = total.astype(NARROW)
        target = out_ref.at[pl.ds(begin * tiles, size)]
        stores.append(pltpu.make_async_copy(left_ref.at[place, pl.ds(0, size)], target, left_sems.at[place]))
        stores[-1].start()
    for copy in copies + stores:
        copy.wait()


def join_windows(got, kind, width, total, count):
    row, tiles = KINDS[kind]
    low, high = kind_ranges(total)[kind]
    single, double = join_plan(kind, width, total, count)
    groups = -(-(high - low) // (8 * row))
    deep = max([(d[1] - d[0]) * tiles for d in double] + [1])
    held = pltpu.VMEM((max(len(double), 1), deep, 8, LANES), NARROW)
    sem = pltpu.SemaphoreType.DMA
    (out,) = launch(
        functools.partial(join_kernel, tiles, single, double), "join_" + kind,
        [((groups * tiles, 8, LANES), NARROW)], [got], far=(0,),
        scratch=(held, held, sem((max(len(single), 1),)), sem((max(len(double), 1),)), sem((max(len(double), 1),))),
        limit=50,
    )
    return out.reshape(groups, tiles, 8, LANES).transpose(0, 2, 1, 3).reshape(groups * 8, row)


def pack_plan(width, total, count):
    plan = []
    for index in range(count):
        for kind, first, last, tile, begin, end in window_pieces(index, width, total):
            tiles = KINDS[kind][1]
            if kind == "rest":
                plan.append((index, 6, first, last - first, tile))
                continue
            size = (PIX if kind == "embed" else D) // 8
            while first < last:
                source = first // size
                stop = min(last, (source + 1) * size)
                number = source + (0 if kind == "embed" else 3)
                plan.append((index, number, (first - source * size) * tiles, (stop - first) * tiles, tile))
                tile += (stop - first) * tiles
                first = stop
    return plan


def pack_kernel(plan, place_ref, *refs):
    sources, (keep_ref, send_ref, sems) = refs[:7], refs[7:]
    x, y, c = place_ref[0], place_ref[1], place_ref[2]
    ends = []
    for number, (index, source, begin, size, tile) in enumerate(plan):
        plane, side, depth, core = index // 8, index // 4 % 2, index // 2 % 2, index % 2
        spot = (plane, (side + x) % 2, (depth + y) % 2, pl.ds(tile, size))
        from_ref = sources[source].at[pl.ds(begin, size)]
        keep = pltpu.make_async_copy(from_ref, keep_ref.at[spot], sems.at[number])
        send = pltpu.make_async_copy(from_ref, send_ref.at[spot], sems.at[number])

        @pl.when(c == core)
        def _():
            keep.start()

        @pl.when(c != core)
        def _():
            send.start()

        ends.append(keep)
    for copy in ends:
        copy.wait()


def tiles_of(values):
    rows, columns = values.shape
    split = values.reshape(rows // 8, 8, columns // LANES, LANES)
    return split.transpose(0, 2, 1, 3).reshape(-1, 8, LANES)


def swap(values, axis):
    return lax.ppermute(values, axis, [(0, 1), (1, 0)])


def add_low(*values):
    return sum(v.astype(jnp.float32) for v in values).astype(NARROW)


def side(values, dim, which):
    return lax.index_in_dim(values, which, dim, keepdims=True)


def chip_halves(kept, x_dim, y_dim, cut_dim):
    half = kept[0].shape[cut_dim] // 2
    ways = ((x_dim, "x"), (y_dim, "y"))
    return [
        ([lax.slice_in_dim(v, start, start + half, axis=cut_dim) for v in kept], order)
        for start, order in ((0, ways), (half, ways[::-1]))
    ]


def chip_stage(halves, stage):
    result = []
    for values, order in halves:
        dim, axis = order[stage]
        got = swap(add_low(*(side(v, dim, 1) for v in values)), axis)
        result.append(([add_low(got, *(side(v, dim, 0) for v in values))], order))
    return result


def chip_join(halves, cut_dim):
    return jnp.concatenate([values[0] for values, order in halves], axis=cut_dim)


def held_back(halves, *others):
    flat = [values[0] for values, order in halves]
    flat, others = lax.optimization_barrier((flat, others))
    return [([v], order) for v, (unused, order) in zip(flat, halves)], *others


def line_sum(parts, owners):
    plane = lax.axis_index(Z_AXES)

    def pick(number):
        return lax.dynamic_index_in_dim(
            parts, jnp.clip(number - owners[0], 0, len(owners) - 1), 0, keepdims=False
        )

    total = pick(plane).astype(jnp.float32)
    for mirror in (False, True):
        here = 3 - plane if mirror else plane
        moving = None
        for step in (1, 2, 3):
            pairs = []
            for spot in range(3):
                number = 4 - step + spot
                owner = 3 - number if mirror else number
                if number > 3 or owner not in owners:
                    continue
                pairs.append((3 - spot, 2 - spot) if mirror else (spot, spot + 1))
            if not pairs:
                continue
            number = 4 - step + here
            value = pick(3 - number if mirror else number)
            if moving is not None:
                value = add_low(value, moving)
            moving = lax.ppermute(value, Z_AXES, pairs)
        total = total + moving.astype(jnp.float32)
    return total


def plane_sum(values):
    rows = values.shape[0]
    core = lax.axis_index("c")
    halves = values.reshape(2, rows // 2, values.shape[1])
    kept = lax.dynamic_index_in_dim(halves, core, 0, keepdims=False)
    sent = lax.dynamic_index_in_dim(halves, 1 - core, 0, keepdims=False).astype(NARROW)
    kept = kept + swap(sent, "c").astype(jnp.float32)
    quarter = rows // 4
    parts = []
    for start, order in ((0, ("x", "y")), (quarter, ("y", "x"))):
        value = kept[start : start + quarter]
        for axis in order:
            low = value.astype(NARROW)
            value = low.astype(jnp.float32) + swap(low, axis).astype(jnp.float32)
        parts.append(value)
    mine = jnp.concatenate(parts, axis=0).astype(NARROW)
    other = swap(mine, "c")
    first = jnp.where(core == 0, mine, other)
    second = jnp.where(core == 0, other, mine)
    return jnp.concatenate([first, second], axis=0).astype(jnp.float32)


def line_gather(own):
    plane = lax.axis_index(Z_AXES)
    below, above = [], []
    value = own
    for step in (1, 2, 3):
        value = lax.ppermute(value, Z_AXES, [(i, i + 1) for i in range(step - 1, 3)])
        below.append(value)
    value = own
    for step in (1, 2, 3):
        value = lax.ppermute(value, Z_AXES, [(i, i - 1) for i in range(1, 5 - step)])
        above.append(value)
    stack = jnp.stack(below[::-1] + [own] + above)
    return lax.dynamic_slice_in_dim(stack, 3 - plane, 4, 0)


def unpack_rest(rest):
    found = []
    offset = 0
    for dims in ((D,), (PIX,), (L, 2, 2, D), (L, 4, D), (L, FF + D)):
        amount = math.prod(dims)
        found.append(rest[offset : offset + amount].reshape(dims))
        offset += amount
    return found


def fast_body(pixels, targets, mask, lat_rows, adam_params, adam_m, adam_v, mlp_weights, mlp_momentum):
    lat_index, lon_index = lax.axis_index(LAT_AXES), lax.axis_index(LON_AXES)
    device = lax.axis_index(SUB_AXES)
    devices = lax.axis_size(SUB_AXES)
    width = adam_params.shape[0]
    total = width * devices
    low_side = lax.axis_index("zl") == 0
    x, y, c = lax.axis_index("x"), lax.axis_index("y"), lax.axis_index("c")
    block = lax.axis_index(("x", "y", "c"))
    shifts = jnp.asarray(shift_tables(), NARROW)
    row_fwd = jnp.asarray(two_terms(row_table()))
    row_back = jnp.asarray(two_terms(row_table().T))
    col_fwd = jnp.asarray(two_terms(column_tables()))
    col_back = jnp.asarray(two_terms(column_tables().transpose(0, 2, 1)))
    col_fwd = jnp.where(low_side, col_fwd, col_fwd[:, 1:2])
    col_back = jnp.where(low_side, col_back, col_back[:, 1:2])
    spread = jnp.asarray(spread_table(), NARROW)

    def to_items(values):
        rest = values.shape[4:]
        lead, items, rows, cols = values.shape[:4]
        split = values.reshape((lead, items, rows, 4, OWN) + rest)
        order = (1, 3, 0, 2, 4) + tuple(range(5, 5 + len(rest)))
        packed = split.transpose(order).reshape((items * 4, lead * rows * OWN) + rest)
        got = lax.all_to_all(packed, LAT_AXES, split_axis=0, concat_axis=0, tiled=True)
        got = got.reshape((items * 4, lead, rows * OWN) + rest)
        return jnp.moveaxis(got, 1, 0).reshape((lead, TOK) + rest)

    own = own_window(adam_params, device, width, total, devices).astype(NARROW)
    windows = lax.all_gather(own, SUB_AXES)
    own_mask = own_window(jnp.ones((width,), jnp.float32), device, width, total, devices)
    zl = lax.axis_index("zl")
    mlp_low = []
    for depth in range(L):
        own = own_quarters(mlp_weights[depth], jnp.stack([x, zl])).reshape(2, 4, D // 4, D)
        first = swap(own[:, 0], "y")
        second = swap(first, "x")
        others = swap(jnp.stack([first, second]), "zl")
        across_y = jnp.stack([first, others[0], second, others[1]], axis=1)
        four = (own, across_y, swap(own, "c"), swap(across_y, "c"))
        mlp_low.append([chunk.reshape(2, D, D) for chunk in four])
    source = to_items(pixels[None])[0]
    wanted = to_items(targets)
    row_weight = jnp.sin(math.pi * (lat_rows.astype(jnp.float32) + 0.5) / ROWS)
    weight_local = row_weight[None, :, None] * mask.astype(jnp.float32)
    weights = to_items(weight_local[None])[0]
    weight_sum = total_over(jnp.sum(weight_local)[None], SUB_AXES)[0]
    loss_scale = 2.0 / (STEPS * PIX * weight_sum)
    weight_pair = jnp.stack([weights, weights * loss_scale], axis=1)

    embed_w = join_windows(windows, "embed", width, total, devices)
    head_w = join_windows(windows, "head", width, total, devices)
    rest = join_windows(windows, "rest", width, total, devices)
    spec_rows = L * 4 * NB * BS * BS // LANES
    spec_w = rest[:spec_rows].reshape(L, 2, 2, NB, BS, BS)
    embed_b, head_b, spec_b, norm_params, mlp_b = unpack_rest(rest[spec_rows:].reshape(-1))
    embed_b, head_b = embed_b.astype(jnp.float32)[None], head_b.astype(jnp.float32)[None]
    norms = norm_params.astype(jnp.float32)
    mlp_b = mlp_b.astype(jnp.float32)

    def by_place(values):
        for dim, side in ((1, y), (2, c), (3, x), (4, zl)):
            values = jnp.where(side == 0, values, jnp.flip(values, dim))
        return values

    up_b = by_place(mlp_b[:, :FF].reshape(L, 2, 2, 2, 2, -1)).transpose(0, 2, 1, 3, 4, 5)
    up_b = up_b.reshape(L, 1, FF)
    down_b = mlp_b[:, None, FF:]
    gap = LANES - BS
    own_w = lax.dynamic_index_in_dim(spec_w, block, 3, keepdims=False)
    own_w = jnp.pad(own_w, ((0, 0),) * 3 + ((0, gap), (0, gap)))
    real, imag = own_w[:, :, 0], own_w[:, :, 1]
    pair_w = jnp.concatenate(
        [jnp.concatenate([real, imag], axis=-1), jnp.concatenate([-imag, real], axis=-1)], axis=-2
    )
    own_b = lax.dynamic_slice_in_dim(spec_b, block * BS, BS, 3).astype(jnp.float32)
    pair_b = jnp.pad(own_b, ((0, 0),) * 3 + ((0, gap),)).reshape(L, 2, 2 * LANES)

    f32 = jnp.float32
    payload = ((GROUP, HALF_TOK, LANES), NARROW)
    state_f32 = ((TOK, D), f32)
    wide = pltpu.VMEM((GROUP, HALF_TOK + 8, LANES), f32)
    sem = pltpu.SemaphoreType.DMA
    held_mlp = (pltpu.VMEM((4, 2, D, D), NARROW), sem((4,)))

    current = source
    saved = []
    loss_sums = []
    for roll_idx in range(STEPS):
        state, sent = launch(
            embed_kernel, "embed", [state_f32, payload],
            [current, shifts, embed_b, norms[0], spread, row_fwd, embed_w],
        )
        layers = []
        for depth in range(L):
            got = exchange(sent)
            out, mixed_in = launch(
                spec_kernel, "spec", [payload, ((FREQ, 2 * LANES), NARROW)],
                [got, col_fwd, col_back, pair_w[depth], pair_b[depth]], scratch=(wide, wide),
            )
            got = exchange(out)
            has_next = depth + 1 < L
            outs = [state_f32, ((TOK, D), NARROW), ((TOK, FF), f32), ((TOK, FF), NARROW), state_f32]
            results = launch(
                functools.partial(mlp_kernel, has_next), "mlp", outs + [payload] * has_next,
                [got, state, norms[depth], norms[min(depth + 1, L - 1)], up_b[depth], down_b[depth],
                 spread, row_fwd, row_back, *mlp_low[depth]], far=(9, 10, 11, 12), scratch=held_mlp, limit=26,
            )
            layers.append((state, mixed_in) + tuple(results[:4]))
            state = results[4]
            if has_next:
                sent = results[5]
        low, predicted, loss_grad, loss_part = launch(
            head_kernel, "head",
            [((TOK, D), NARROW), ((TOK, PIX), NARROW), ((TOK, PIX), f32), ((1, PIX), f32)],
            [state, shifts, head_b, wanted[roll_idx], weight_pair, head_w],
        )
        loss_sums.append(loss_part)
        saved.append((current, layers, low, loss_grad))
        current = predicted

    rows_own = mlp_momentum.shape[2] // 2
    half_ff = FF // 2

    def joined(terms, member):
        return jnp.concatenate([now[member] for now in terms], axis=0)

    def mlp_sends(depth):
        g_before, hidden_in, hidden, grad_out = (joined(mlp_terms[depth], m) for m in range(4))
        pairs = ((g_before, hidden_in), (hidden, grad_out))
        return pairs, [swap(dot_tn(a[:, half_ff:], b).astype(NARROW), "c") for a, b in pairs]

    def mlp_kept(pairs, got):
        kept = [
            (dot_tn(a[:, :half_ff], b) + sent.astype(f32)).astype(NARROW)
            for (a, b), sent in zip(pairs, got)
        ]
        return jnp.stack(kept).reshape(2, 2, 2, rows_own, D)

    def mlp_joined(halves):
        halves = chip_join(halves, 3).reshape(2, 2, rows_own // 2, D)
        halves = jnp.where(zl == 0, halves, jnp.flip(halves, 1))
        return halves.reshape(2, rows_own, D)

    head_terms, embed_terms = [], []
    mlp_terms = [[] for unused in range(L)]
    spec_terms = [[] for unused in range(L)]
    sum_terms = [[] for unused in range(L)]
    head_sums, embed_sums = [], []
    upstream = None
    for roll_idx in reversed(range(STEPS)):
        current, layers, low, loss_grad = saved[roll_idx]
        upstream = loss_grad if upstream is None else upstream
        upstream_low, head_sum, grad_state = launch(
            head_back_kernel, "head_back",
            [((TOK, PIX), NARROW), ((1, PIX), f32), state_f32], [upstream, shifts, head_w],
        )
        head_terms.append((low, upstream_low))
        head_sums.append(head_sum)
        for depth in reversed(range(L)):
            state, mixed_in, mixed, hidden_in, before, hidden = layers[depth]
            grad_out, g_before, g_mixed, g_up_b, sums_two, sent = launch(
                mlp_back_kernel, "mlp_back",
                [((TOK, D), NARROW), ((TOK, FF), NARROW), state_f32, ((1, FF), f32), ((3, D), f32),
                 payload],
                [grad_state, before, mixed, norms[depth], spread, row_fwd, *mlp_low[depth]],
                far=(6, 7, 8, 9), scratch=held_mlp, limit=26,
            )
            mlp_terms[depth].append((g_before, hidden_in, hidden, grad_out))
            got = exchange(sent)
            if roll_idx == 0 and depth == L - 1:
                last_sends = mlp_sends(depth)
                last_kept, got = lax.optimization_barrier((mlp_kept(*last_sends), got))
                last_halves = chip_halves([last_kept], 2, 1, 3)
            if roll_idx == 0 and depth == 0:
                last_halves, got = held_back(chip_stage(last_halves, 1), got)
            out, g_pair, g_pair_b = launch(
                spec_back_kernel, "spec_back",
                [payload, ((2, 2 * LANES, 2 * LANES), f32), ((2, 2 * LANES), f32)],
                [got, col_fwd, col_back, pair_w[depth], pair_b[depth], mixed_in],
                scratch=(wide, wide),
            )
            got = exchange(out)
            if roll_idx == 0 and depth == L - 1:
                last_halves, got = held_back(chip_stage(last_halves, 0), got)
            grad_state, state_low, sums_one = launch(
                norm_back_kernel, "norm_back", [state_f32, ((TOK, D), NARROW), ((3, D), f32)],
                [got, g_mixed, state, norms[depth], spread, row_back],
            )
            spec_terms[depth].append((g_pair, g_pair_b))
            sum_terms[depth].append((sums_one, sums_two, g_up_b))
        embed_terms.append((current, state_low))
        embed_sums.append(sums_one[2])
        if roll_idx:
            (upstream,) = launch(
                embed_back_kernel, "embed_back", [((TOK, PIX), f32)],
                [state_low, shifts, saved[roll_idx - 1][3], embed_w],
            )

    pairs, sends = mlp_sends(0)
    first_halves = chip_halves([mlp_kept(pairs, sends)], 2, 1, 3)
    first_halves = chip_stage(chip_stage(first_halves, 0), 1)
    chips = jnp.concatenate([mlp_joined(first_halves), mlp_joined(last_halves)], axis=0)

    def moved_pair(values, amount):
        return jnp.concatenate([jnp.roll(now, amount, axis=0) for now in values], axis=0)

    embed_src = joined(embed_terms, 0)
    head_up = joined(head_terms, 1)
    g_embed = [
        dot_tn(embed_src, moved_pair([now[1] for now in embed_terms], OWN * (o - 1))).astype(NARROW)
        for o in range(3)
    ]
    g_head = [
        dot_tn(moved_pair([now[0] for now in head_terms], -OWN * (o - 1)), head_up).astype(NARROW)
        for o in range(3)
    ]
    g_spec, g_spec_b, g_norm, g_mlp_b = [], [], [], []
    for depth in range(L):
        pair_sum = sum(now[0] for now in spec_terms[depth]).reshape(2, 2, LANES, 2, LANES)
        pair_sum = pair_sum[:, :, :BS, :, :BS]
        g_real = pair_sum[:, 0, :, 0] + pair_sum[:, 1, :, 1]
        g_imag = pair_sum[:, 0, :, 1] - pair_sum[:, 1, :, 0]
        g_spec.append(jnp.stack([g_real, g_imag], axis=1))
        g_spec_b.append(sum(now[1] for now in spec_terms[depth]).reshape(2, 2, LANES)[:, :, :BS])
        one = sum(now[0] for now in sum_terms[depth])
        two = sum(now[1] for now in sum_terms[depth])
        g_norm.append(jnp.stack([one[0], one[1], two[1], two[2]]))
        up_sum = sum(now[2] for now in sum_terms[depth]).reshape(1, 2, 2, 2, 2, -1)
        up_sum = by_place(up_sum.transpose(0, 2, 1, 3, 4, 5)).reshape(-1)
        g_mlp_b.append(jnp.concatenate([up_sum, two[0]]))
    full_spec = jnp.zeros((L, 2, 2, NB, BS, BS), NARROW)
    full_spec = lax.dynamic_update_slice_in_dim(
        full_spec, jnp.stack(g_spec).astype(NARROW)[:, :, :, None], block, 3
    )
    full_spec_b = lax.dynamic_update_slice_in_dim(
        jnp.zeros((L, 2, 2, D), f32), jnp.stack(g_spec_b), block * BS, 3
    )
    small = jnp.concatenate(
        [sum(embed_sums), sum(head_sums)[0], full_spec_b.reshape(-1),
         jnp.stack(g_norm).reshape(-1), jnp.stack(g_mlp_b).reshape(-1)]
    ).astype(NARROW)
    rest_grad = jnp.concatenate([full_spec.reshape(-1), small])
    rest_grad = jnp.pad(rest_grad, (0, -rest_grad.shape[0] % (8 * LANES))).reshape(-1, 8, LANES)
    plan = pack_plan(width, total, devices)
    window_set = ((4, 2, 2, WINDOW, 8, LANES), NARROW)
    rest_grad, *sends = lax.optimization_barrier((rest_grad, *sends))
    kept, sent = launch(
        functools.partial(pack_kernel, plan), "pack", [window_set, window_set],
        [jnp.stack([x, y, c])] + [tiles_of(g) for g in g_embed + g_head] + [rest_grad],
        near=(0,), far_out=True, scratch=(sem((len(plan),)),), limit=8,
    )
    halves = chip_stage(chip_halves([kept, swap(sent, "c")], 1, 2, 3), 0)
    halves = chip_stage(halves, 1)
    mlp_mine = line_sum(chips, [0, 1, 2, 3])
    flat_window = line_sum(chip_join(halves, 3).reshape(4, WINDOW, 8, LANES), [0, 1, 2, 3])
    flat_piece = own_range(flat_window, device, width, total, devices)
    local = jnp.stack(
        [jnp.sum(jnp.where(own_mask > 0, flat_window * flat_window, 0.0)) + jnp.sum(mlp_mine * mlp_mine),
         sum(jnp.sum(now) for now in loss_sums)]
    )
    square_sum, loss_total = total_over(local, SUB_AXES)
    loss_total = loss_total / (STEPS * PIX * weight_sum)
    grad_norm = jnp.sqrt(square_sum)
    factor = jnp.minimum(1.0, CLIP_LEVEL / (grad_norm + 1e-06))

    mlp_grad = lax.all_gather(mlp_mine.astype(NARROW), LAT_AXES, axis=0, tiled=True)

    held = mlp_momentum.reshape(2 * L * 2, rows_own, D)
    held = lax.dynamic_index_in_dim(held, lat_index, 0, keepdims=False)
    mine_new = MOMENT_KEEP * held + mlp_mine * factor
    high = lax.Precision.HIGH
    gram = plane_sum(lax.dot_general(mine_new, mine_new, (((0,), (0,)), ((), ())), precision=high))
    inverse = 1.0 / (jnp.sqrt(jnp.trace(gram)) + 1e-07)
    lead, mid, last = POLY_COEF
    square = gram * (inverse * inverse)
    mul = functools.partial(jnp.dot, precision=high)
    poly_one = mid * square + last * mul(square, square)
    turned = mul(square, poly_one)
    square_two = lead * lead * square + 2.0 * lead * turned + mul(turned, poly_one)
    poly_two = mid * square_two + last * mul(square_two, square_two)
    change = lead * (poly_one + poly_two) + mul(poly_one, poly_two)
    level_high = inverse.astype(NARROW)
    level_mid = (inverse - level_high.astype(f32)).astype(NARROW)
    level_low = (inverse - level_high.astype(f32) - level_mid.astype(f32)).astype(NARROW)
    extra = jnp.zeros((8, D), NARROW)
    extra = extra.at[0, 0].set(level_high).at[0, 1].set(level_mid).at[0, 2].set(level_low)
    change = lax.dynamic_slice_in_dim((change * inverse).astype(NARROW), c * (D // 2), D // 2, 0)
    packed = jnp.concatenate([change, extra], axis=0)
    packed, mlp_grad = lax.optimization_barrier((packed, mlp_grad))
    gathered = line_gather(packed)
    mlp_grad = mlp_grad.reshape(mlp_momentum.shape).astype(f32)
    momentum_new = MOMENT_KEEP * mlp_momentum + mlp_grad * factor
    levels = jnp.sum(gathered[:, D // 2, :3].astype(f32), axis=-1)
    gathered = gathered[:, : D // 2]
    other = swap(gathered, "c")
    changes = jnp.concatenate(
        [jnp.where(c == 0, gathered, other), jnp.where(c == 0, other, gathered)], axis=1
    )
    (mlp_new,) = pl.pallas_call(
        muon_kernel,
        name="muon",
        grid=(2 * L, 2),
        out_shape=[jax.ShapeDtypeStruct((2 * L, D, D), f32)],
        in_specs=[pl.BlockSpec(memory_space=pltpu.SMEM)]
        + [pl.BlockSpec((None, rows_own, D), lambda m, h: (m, h, 0))] * 2
        + [pl.BlockSpec((None, D, D), lambda m, h: (m, 0, 0))],
        out_specs=[pl.BlockSpec((None, rows_own, D), lambda m, h: (m, h, 0))],
        compiler_params=pltpu.CompilerParams(vmem_limit_bytes=28 * 1024 * 1024),
    )(levels, momentum_new.reshape(2 * L, D, D), mlp_weights.reshape(2 * L, D, D), changes)
    mlp_new = mlp_new.reshape(mlp_weights.shape)

    clipped = flat_piece * factor
    first_new = BETA_FIRST * adam_m + (1.0 - BETA_FIRST) * clipped
    second_new = BETA_SECOND * adam_v + (1.0 - BETA_SECOND) * clipped * clipped
    count_value = float(STEP_NUM)
    first_hat = first_new / (1.0 - BETA_FIRST**count_value)
    second_hat = second_new / (1.0 - BETA_SECOND**count_value)
    adam_new = adam_params - ADAM_RATE * (
        first_hat / (jnp.sqrt(second_hat) + 1e-08) + DECAY_RATE * adam_params
    )
    return (adam_new, first_new, second_new, mlp_new, momentum_new, loss_total, grad_norm)


def solution(mesh):
    if tuple(mesh.shape.items()) == (("lat", 8), ("lon", 4)):
        fine = Mesh(mesh.devices.reshape(2, 2, 2, 2, 2), SUB_AXES)
        return placed(fast_body, fine, LAT_AXES, LON_AXES)
    return placed(body, mesh, ("lat",), ("lon",))


def placed(step, mesh, lat, lon):
    flat = P(lat + lon)
    halves = P(None, None, lon, None)
    return jax.shard_map(
        step,
        mesh=mesh,
        in_specs=(
            P(None, lat, lon, None),
            P(None, None, lat, lon, None),
            P(None, lat, lon),
            P(lat),
            flat,
            flat,
            flat,
            halves,
            halves,
        ),
        out_specs=(flat, flat, flat, halves, halves, P(), P()),
        check_vma=False,
    )
```

```python
import functools
import math

import jax
import ml_dtypes
import numpy as np
import jax.numpy as jnp
from jax import lax
from jax.experimental import pallas as pl
from jax.experimental.pallas import tpu as pltpu
from jax.sharding import Mesh
from jax.sharding import PartitionSpec as P

D = 768
FF = 3072
NB = 8
PIX = 1280
BS = 96
L = 2
STEPS = 2
NS_STEPS = 2
STEP_NUM = 5


HIGH_PREC = lax.Precision.HIGHEST
NORM_EPS = 1e-05
CLIP_LEVEL = 0.001
BETA_FIRST = 0.9
BETA_SECOND = 0.95
ADAM_RATE = 0.01
MUON_RATE = 0.8
DECAY_RATE = 0.05
MOMENT_KEEP = 0.95
POLY_COEF = (3.4445, -4.775, 2.0315)


def for_sending(value):

    def short(part):
        return part.astype(jnp.bfloat16) if part.dtype == jnp.float32 else part

    return jax.tree.map(short, value)


def with_halo(block, sides, width):
    for axis, dim in sides:
        count = lax.axis_size(axis)
        forward = [(i, i + 1) for i in range(count - 1)]
        forward.append((count - 1, 0))
        backward = [(target, source) for source, target in forward]
        low = lax.ppermute(
            lax.slice_in_dim(block, block.shape[dim] - width, None, axis=dim), axis, forward
        )
        high = lax.ppermute(lax.slice_in_dim(block, 0, width, axis=dim), axis, backward)
        block = jnp.concatenate([low, block, high], axis=dim)
    return block


def unpack(flat_params):
    layout = [
        (3, PIX, D),
        (3, D, PIX),
        (L, 2, 2, NB, BS, BS),
        (D,),
        (PIX,),
        (L, 2, 2, D),
        (L, 4, D),
        (L, FF + D),
    ]
    pieces_out = []
    offset = 0
    for dims_now in layout:
        amount = math.prod(dims_now)
        pieces_out.append(flat_params[offset : offset + amount].reshape(dims_now))
        offset = offset + amount
    return pieces_out


def along(matrix, values, axis_dim):
    if axis_dim == 1:
        return jnp.einsum("kn,bncd->bkcd", matrix, values, precision=HIGH_PREC)
    return jnp.einsum("kn,brnd->brkd", matrix, values, precision=HIGH_PREC)


def phase_table(out_count, in_count, length_all):
    out_index = jnp.arange(out_count, dtype=jnp.int32)
    in_index = jnp.arange(in_count, dtype=jnp.int32)
    phase = out_index[:, None] * in_index[None, :] % length_all
    angle = phase.astype(jnp.float32) * (2.0 * math.pi / length_all)
    scale_value = 1.0 / math.sqrt(length_all)
    return (jnp.cos(angle) * scale_value, jnp.sin(angle) * scale_value)


def combine(pieces, axis_dim, sign_value, tables, real_only):
    cosine, sine_table = tables
    values = [piece_now.astype(jnp.float32) for piece_now in pieces]
    real_out = along(cosine, values[0], axis_dim)
    if len(values) > 1:
        real_out = real_out - sign_value * along(sine_table, values[1], axis_dim)
    if real_only:
        return (real_out,)
    imag_out = sign_value * along(sine_table, values[0], axis_dim)
    if len(values) > 1:
        imag_out = imag_out + along(cosine, values[1], axis_dim)
    return (real_out, imag_out)


def turn_transform(pieces, axis_dim, sign_value, real_only):
    if axis_dim == 1:
        wide = jax.tree.map(
            lambda part, own: part.astype(own.dtype),
            lax.all_to_all(for_sending(pieces), "lat", split_axis=3, concat_axis=1, tiled=True),
            pieces,
        )
        length_all = wide[0].shape[1]
        result = combine(
            wide, 1, sign_value, phase_table(length_all, length_all, length_all), real_only
        )
        narrow = tuple((piece_now.astype(jnp.bfloat16) for piece_now in result))
        returned = jax.tree.map(
            lambda part, own: part.astype(own.dtype),
            lax.all_to_all(for_sending(narrow), "lat", split_axis=1, concat_axis=3, tiled=True),
            narrow,
        )
        return tuple((piece_now.astype(jnp.float32) for piece_now in returned))
    wide = jax.tree.map(
        lambda part, own: part.astype(own.dtype),
        lax.all_to_all(for_sending(pieces), "lon", split_axis=3, concat_axis=2, tiled=True),
        pieces,
    )
    length_all = wide[0].shape[2]
    result = combine(
        wide, 2, sign_value, phase_table(length_all, length_all, length_all), real_only
    )
    return jax.tree.map(
        lambda part, own: part.astype(own.dtype),
        lax.all_to_all(for_sending(result), "lon", split_axis=2, concat_axis=3, tiled=True),
        result,
    )


def transform(pieces, axis_dim, sign_value, real_only):
    return turn_transform(pieces, axis_dim, sign_value, real_only)


def to_low(pieces):
    return tuple((piece_now.astype(jnp.bfloat16) for piece_now in pieces))


def exact_gelu(values):
    return jax.nn.gelu(values, approximate=False)


def gelu_back(values, upstream):
    return jax.vjp(exact_gelu, values)[1](upstream)[0]


def norm_forward(inputs, gain, shift):
    center = inputs - jnp.mean(inputs, axis=-1, keepdims=True)
    inverse = lax.rsqrt(jnp.mean(center * center, axis=-1, keepdims=True) + NORM_EPS)
    scaled = center * inverse
    return (scaled * gain + shift, (scaled, inverse))


def norm_backward(upstream, saved, gain):
    scaled, inverse = saved
    g_gain = jnp.sum(upstream * scaled, axis=(0, 1, 2))
    g_shift = jnp.sum(upstream, axis=(0, 1, 2))
    g_scaled = upstream * gain
    g_input = inverse * (
        g_scaled
        - jnp.mean(g_scaled, axis=-1, keepdims=True)
        - scaled * jnp.mean(g_scaled * scaled, axis=-1, keepdims=True)
    )
    return (g_input, g_gain, g_shift)


def block_mix(pieces, weights, bias):
    shaped = [piece_now.reshape(piece_now.shape[:-1] + (NB, BS)) for piece_now in pieces]

    def multiply(left_side, right_side):
        return jnp.einsum(
            "brcni,nio->brcno", left_side, right_side, preferred_element_type=jnp.float32
        )

    real_out = multiply(shaped[0], weights[0]) - multiply(shaped[1], weights[1])
    imag_out = multiply(shaped[0], weights[1]) + multiply(shaped[1], weights[0])
    full_dims = pieces[0].shape
    return (
        real_out.reshape(full_dims) + bias[0].astype(jnp.float32),
        imag_out.reshape(full_dims) + bias[1].astype(jnp.float32),
    )


def block_back(grads_low, pieces, weights):
    shaped = [piece_now.reshape(piece_now.shape[:-1] + (NB, BS)) for piece_now in pieces]
    g_shaped = [grad_now.reshape(grad_now.shape[:-1] + (NB, BS)) for grad_now in grads_low]

    def back_multiply(grad_side, weight_side):
        return jnp.einsum(
            "brcno,nio->brcni", grad_side, weight_side, preferred_element_type=jnp.float32
        )

    def weight_multiply(input_side, grad_side):
        return jnp.einsum(
            "brcni,brcno->nio", input_side, grad_side, preferred_element_type=jnp.float32
        )

    g_real = back_multiply(g_shaped[0], weights[0]) + back_multiply(g_shaped[1], weights[1])
    g_imag = back_multiply(g_shaped[1], weights[0]) - back_multiply(g_shaped[0], weights[1])
    g_w_real = weight_multiply(shaped[0], g_shaped[0]) + weight_multiply(shaped[1], g_shaped[1])
    g_w_imag = weight_multiply(shaped[0], g_shaped[1]) - weight_multiply(shaped[1], g_shaped[0])
    g_bias = jnp.stack(
        [jnp.sum(grad_now.astype(jnp.float32), axis=(0, 1, 2)) for grad_now in grads_low]
    )
    full_dims = pieces[0].shape
    return (
        (g_real.reshape(full_dims), g_imag.reshape(full_dims)),
        jnp.stack([g_w_real, g_w_imag]),
        g_bias,
    )


def halo_rows(values):
    return with_halo(values, (("lat", 1),), 1)


def rows_conv(source_low, weight3, bias):
    padded = halo_rows(source_low)
    row_count = source_low.shape[1]
    window = jnp.concatenate(
        [padded[:, offset : offset + row_count] for offset in range(3)], axis=-1
    )
    flat_weight = weight3.reshape(-1, weight3.shape[-1])
    result = jnp.einsum("brci,io->brco", window, flat_weight, preferred_element_type=jnp.float32)
    return (result + bias.astype(jnp.float32), window)


def rows_back(grad_low, weight3, need_source):
    g_bias = jnp.sum(grad_low.astype(jnp.float32), axis=(0, 1, 2))
    if not need_source:
        return (g_bias, None)
    padded = halo_rows(grad_low)
    row_count = grad_low.shape[1]
    window_back = jnp.concatenate(
        [padded[:, 2 - offset : 2 - offset + row_count] for offset in range(3)], axis=-1
    )
    flipped = jnp.transpose(weight3, (0, 2, 1)).reshape(-1, weight3.shape[1])
    g_source = jnp.einsum("brco,oi->brci", window_back, flipped, preferred_element_type=jnp.float32)
    return (g_bias, g_source)


def conv_weight_grad(terms_list, weight3):
    window = jnp.concatenate([terms_now[0] for terms_now in terms_list], axis=0)
    grads_low = jnp.concatenate([terms_now[1] for terms_now in terms_list], axis=0)
    return jnp.einsum(
        "brci,brco->io", window, grads_low, preferred_element_type=jnp.float32
    ).reshape(weight3.shape)


def layer_forward(state, params_now):
    spec_w, spec_b, norm_vals, mlp_pair, mlp_bias = params_now
    normed, first_saved = norm_forward(state, norm_vals[0], norm_vals[1])
    spectrum = transform((normed.astype(jnp.bfloat16),), 2, -1.0, False)
    spectrum = transform(to_low(spectrum), 1, -1.0, False)
    mixed_in = to_low(spectrum)
    inner = block_mix(mixed_in, spec_w[0], spec_b[0])
    activated = to_low(tuple((exact_gelu(piece_now) for piece_now in inner)))
    outer = block_mix(activated, spec_w[1], spec_b[1])
    spectrum = transform(to_low(outer), 1, 1.0, False)
    spatial = transform(to_low(spectrum), 2, 1.0, True)[0]
    mixed = state + spatial + normed
    second, second_saved = norm_forward(mixed, norm_vals[2], norm_vals[3])
    hidden_in = second.astype(jnp.bfloat16)
    before = (
        jnp.einsum("brcd,fd->brcf", hidden_in, mlp_pair[0], preferred_element_type=jnp.float32)
        + mlp_bias[:FF]
    )
    hidden = exact_gelu(before).astype(jnp.bfloat16)
    result = (
        jnp.einsum("brcf,fd->brcd", hidden, mlp_pair[1], preferred_element_type=jnp.float32)
        + mlp_bias[FF:]
    )
    return (
        mixed + result,
        (first_saved, mixed_in, inner, activated, second_saved, hidden_in, before, hidden),
    )


def layer_backward(upstream, cache, params_now):
    spec_w, spec_b, norm_vals, mlp_pair, mlp_bias = params_now
    first_saved, mixed_in, inner, activated, second_saved, hidden_in, before, hidden = cache
    grad_out = upstream.astype(jnp.bfloat16)
    g_down_bias = jnp.sum(grad_out.astype(jnp.float32), axis=(0, 1, 2))
    g_hidden = jnp.einsum(
        "brcd,fd->brcf", grad_out, mlp_pair[1], preferred_element_type=jnp.float32
    )
    g_before = gelu_back(before, g_hidden).astype(jnp.bfloat16)
    g_up_bias = jnp.sum(g_before.astype(jnp.float32), axis=(0, 1, 2))
    g_second = jnp.einsum(
        "brcf,fd->brcd", g_before, mlp_pair[0], preferred_element_type=jnp.float32
    )
    g_norm_in, g_gain_two, g_shift_two = norm_backward(g_second, second_saved, norm_vals[2])
    g_mixed = upstream + g_norm_in
    g_spectrum = transform((g_mixed.astype(jnp.bfloat16),), 2, -1.0, False)
    g_outer = to_low(transform(to_low(g_spectrum), 1, -1.0, False))
    g_activated, g_w_outer, g_b_outer = block_back(g_outer, activated, spec_w[1])
    g_inner = to_low(
        tuple((gelu_back(piece_now, grad_now) for piece_now, grad_now in zip(inner, g_activated)))
    )
    g_mixed_in, g_w_inner, g_b_inner = block_back(g_inner, mixed_in, spec_w[0])
    g_spectrum = transform(to_low(g_mixed_in), 1, 1.0, False)
    g_normed = transform(to_low(g_spectrum), 2, 1.0, True)[0] + g_mixed
    g_state_norm, g_gain_one, g_shift_one = norm_backward(g_normed, first_saved, norm_vals[0])
    layer_grads = (
        jnp.stack([g_w_inner, g_w_outer]),
        jnp.stack([g_b_inner, g_b_outer]),
        jnp.stack([g_gain_one, g_shift_one, g_gain_two, g_shift_two]),
        jnp.concatenate([g_up_bias, g_down_bias]),
    )
    return (g_mixed + g_state_norm, layer_grads, (hidden, grad_out, g_before, hidden_in))


def body(pixels, targets, mask, lat_rows, adam_params, adam_m, adam_v, mlp_weights, mlp_momentum):
    flat_low = lax.all_gather(adam_params.astype(jnp.bfloat16), ("lat", "lon"), axis=0, tiled=True)
    mlp_low = lax.all_gather(mlp_weights.astype(jnp.bfloat16), "lon", axis=2, tiled=True)
    embed_w, head_w, spec_w, embed_b, head_b, spec_b, norm_params, mlp_b = unpack(flat_low)
    row_count = pixels.shape[1]
    lat_total = lax.axis_size("lat") * row_count
    row_weight = jnp.sin(math.pi * (lat_rows.astype(jnp.float32) + 0.5) / lat_total)
    weight_map = row_weight[None, :, None] * mask.astype(jnp.float32)
    weight_sum = lax.psum(jnp.sum(weight_map), ("lat", "lon"))
    loss_scale = 2.0 / (STEPS * PIX * weight_sum)

    def params_at(depth_idx):
        return (
            spec_w[depth_idx],
            spec_b[depth_idx],
            norm_params[depth_idx].astype(jnp.float32),
            mlp_low[depth_idx],
            mlp_b[depth_idx].astype(jnp.float32),
        )

    current = pixels
    saved_steps = []
    loss_local = jnp.zeros((), jnp.float32)
    for roll_idx in range(STEPS):
        state, embed_window = rows_conv(current.astype(jnp.bfloat16), embed_w, embed_b)
        caches = []
        for depth_idx in range(L):
            state, cache_now = layer_forward(state, params_at(depth_idx))
            caches.append(cache_now)
        predicted, head_window = rows_conv(state.astype(jnp.bfloat16), head_w, head_b)
        differ = predicted - targets[roll_idx].astype(jnp.float32)
        loss_local = loss_local + jnp.sum(weight_map[..., None] * differ * differ)
        saved_steps.append(
            (embed_window, caches, head_window, weight_map[..., None] * differ * loss_scale)
        )
        current = predicted
    g_embed_b = jnp.zeros(embed_b.shape, jnp.float32)
    g_head_b = jnp.zeros(head_b.shape, jnp.float32)
    head_terms = []
    embed_terms = []
    mlp_terms = [[] for unused in range(L)]
    g_layers = [None] * L
    carried = None
    for roll_idx in reversed(range(STEPS)):
        embed_window, caches, head_window, loss_grad = saved_steps[roll_idx]
        upstream = loss_grad if carried is None else loss_grad + carried
        upstream_low = upstream.astype(jnp.bfloat16)
        head_terms.append((head_window, upstream_low))
        grad_b, grad_state = rows_back(upstream_low, head_w, True)
        g_head_b = g_head_b + grad_b
        for depth_idx in reversed(range(L)):
            grad_state, layer_grads, mlp_now = layer_backward(
                grad_state, caches[depth_idx], params_at(depth_idx)
            )
            mlp_terms[depth_idx].append(mlp_now)
            if g_layers[depth_idx] is None:
                g_layers[depth_idx] = layer_grads
            else:
                g_layers[depth_idx] = jax.tree.map(jnp.add, g_layers[depth_idx], layer_grads)
        state_low = grad_state.astype(jnp.bfloat16)
        embed_terms.append((embed_window, state_low))
        grad_b, carried = rows_back(state_low, embed_w, roll_idx > 0)
        g_embed_b = g_embed_b + grad_b
    g_embed_w = conv_weight_grad(embed_terms, embed_w)
    g_head_w = conv_weight_grad(head_terms, head_w)
    mlp_grads = []
    for depth_idx in range(L):
        joined = [
            jnp.concatenate([terms_now[member] for terms_now in mlp_terms[depth_idx]], axis=0)
            for member in range(4)
        ]
        g_up = jnp.einsum("brcf,brcd->fd", joined[2], joined[3], preferred_element_type=jnp.float32)
        g_down = jnp.einsum(
            "brcf,brcd->fd", joined[0], joined[1], preferred_element_type=jnp.float32
        )
        mlp_grads.append(jnp.stack([g_up, g_down]))
    full_mlp = jnp.stack(mlp_grads)
    stacked = [
        jnp.stack([g_layers[depth_idx][member] for depth_idx in range(L)]) for member in range(4)
    ]
    flat_grad = jnp.concatenate(
        [
            g_embed_w.reshape(-1),
            g_head_w.reshape(-1),
            stacked[0].reshape(-1),
            g_embed_b,
            g_head_b,
            stacked[1].reshape(-1),
            stacked[2].reshape(-1),
            stacked[3].reshape(-1),
        ]
    )
    lon_count = lax.axis_size("lon")
    lat_count = lax.axis_size("lat")
    dev_count = lon_count * lat_count
    per_block = full_mlp.shape[2] // dev_count
    mlp_rows = (
        full_mlp.reshape(L, 2, lon_count, lat_count, per_block, D)
        .transpose(3, 2, 0, 1, 4, 5)
        .reshape(dev_count, -1)
    )
    flat_rows = flat_grad.reshape(dev_count, -1)
    flat_width = flat_rows.shape[1]
    summed = lax.psum_scatter(
        jnp.concatenate([flat_rows, mlp_rows], axis=1),
        ("lat", "lon"),
        scatter_dimension=0,
        tiled=True,
    )[0]
    flat_piece = summed[:flat_width]
    mlp_piece = summed[flat_width:].reshape(L, 2, per_block, D)
    local_square = jnp.sum(flat_piece * flat_piece) + jnp.sum(mlp_piece * mlp_piece)
    loss_total, square_sum = lax.psum(
        (loss_local / (STEPS * PIX * weight_sum), local_square), ("lat", "lon")
    )
    mlp_grad = lax.all_gather(mlp_piece.astype(jnp.bfloat16), "lat", axis=2, tiled=True).astype(
        mlp_piece.dtype
    )
    grad_norm = jnp.sqrt(square_sum)
    factor = jnp.minimum(1.0, CLIP_LEVEL / (grad_norm + 1e-06))
    clipped = flat_piece * factor
    first_new = BETA_FIRST * adam_m + (1.0 - BETA_FIRST) * clipped
    second_new = BETA_SECOND * adam_v + (1.0 - BETA_SECOND) * clipped * clipped
    count_value = float(STEP_NUM)
    first_hat = first_new / (1.0 - BETA_FIRST**count_value)
    second_hat = second_new / (1.0 - BETA_SECOND**count_value)
    adam_new = adam_params - ADAM_RATE * (
        first_hat / (jnp.sqrt(second_hat) + 1e-08) + DECAY_RATE * adam_params
    )
    momentum_new = MOMENT_KEEP * mlp_momentum + mlp_grad * factor
    ortho = momentum_new
    for ns_idx in range(NS_STEPS):
        partial_gram = jnp.einsum("lkfd,lkfe->lkde", ortho, ortho, precision=HIGH_PREC)
        square = lax.psum(partial_gram.astype(jnp.bfloat16), "lon").astype(jnp.float32)
        if ns_idx == 0:
            trace_val = jnp.trace(square, axis1=2, axis2=3)
            inverse = 1.0 / (jnp.sqrt(trace_val) + 1e-07)
            ortho = ortho * inverse[:, :, None, None]
            square = square * (inverse * inverse)[:, :, None, None]
        poly = POLY_COEF[1] * square + POLY_COEF[2] * jnp.einsum(
            "lkde,lkef->lkdf", square, square, precision=HIGH_PREC
        )
        ortho = POLY_COEF[0] * ortho + jnp.einsum(
            "lkfd,lkde->lkfe", ortho, poly, precision=HIGH_PREC
        )
    mlp_new = mlp_weights * (1.0 - MUON_RATE * DECAY_RATE) - MUON_RATE * (FF / D) ** 0.5 * ortho
    return (adam_new, first_new, second_new, mlp_new, momentum_new, loss_total, grad_norm)


ROWS = 48
COLS = 48
GROUP = 16
OWN = 3
TOK = ROWS * OWN
HALF_TOK = TOK // 2
PAIRS = 12
LANES = 128
WIDE = NB * LANES
FREQ = PAIRS * 96
NARROW = jnp.bfloat16
WINDOW = 212
MLP_LIMIT = 26
WINDOW_CUTS = (0, 72, 142, WINDOW)
MLP_CUTS = (0, 128, 256, 384)
EMBED_AT = 2
Z_AXES = ("zh", "zl")
EMBED_SIZE = 3 * PIX * D
SUB_AXES = ("zh", "zl", "x", "y", "c")
LAT_AXES = ("zh", "zl", "x")
LON_AXES = ("y", "c")
ITEM_AXES = ("zl", "x", "y", "c")


def shift_tables():
    table = np.zeros((3, TOK, TOK), np.float32)
    spots = np.arange(TOK)
    for offset in range(3):
        table[offset, spots, (spots + OWN * (offset - 1)) % TOK] = 1.0
    return table


def row_table():
    table = np.zeros((TOK, TOK), np.float64)
    rows = np.arange(ROWS)
    for pair in range(2 * PAIRS):
        if pair == 0:
            waves = (np.ones(ROWS), np.cos(np.pi * rows))
        else:
            angle = 2.0 * np.pi * (pair * rows % ROWS) / ROWS
            waves = (np.cos(angle), np.sin(angle))
        for part in range(2):
            for own in range(OWN):
                table[pair * 6 + part * OWN + own, rows * OWN + own] = waves[part]
    return table / math.sqrt(ROWS)


def column_tables():
    freq = np.arange(COLS)[:, None]
    table = np.zeros((2, 192, 128), np.float64)
    for source in range(GROUP):
        quad, lon = source // 4, source % 4
        for own in range(OWN):
            column = lon * 12 + quad * OWN + own
            angle = 2.0 * np.pi * (freq[:, 0] * column % COLS) / COLS
            cosine, sine = np.cos(angle), np.sin(angle)
            first, second = source * 8 + own, source * 8 + OWN + own
            table[0, 0:48, first] = cosine
            table[0, 96:144, first] = -sine
            table[0, 48:96, second] = cosine
            table[0, 144:192, second] = -sine
            table[1, 0:48, first] = cosine
            table[1, 48:96, first] = cosine
            table[1, 96:144, first] = -sine
            table[1, 144:192, first] = -sine
            table[1, 0:48, second] = -sine
            table[1, 48:96, second] = sine
            table[1, 96:144, second] = -cosine
            table[1, 144:192, second] = cosine
    return table / math.sqrt(COLS)


def spread_table():
    table = np.zeros((384, 512), np.float32)
    spots = np.arange(384)
    table[spots, spots // BS * LANES + spots % BS] = 1.0
    return table


def two_terms(table):
    high = table.astype(ml_dtypes.bfloat16)
    low = (table - high.astype(np.float64)).astype(ml_dtypes.bfloat16)
    return np.stack([high, low])


def dot(left, right):
    return lax.dot_general(left, right, (((1,), (0,)), ((), ())), preferred_element_type=jnp.float32)


def dot_nt(left, right):
    return lax.dot_general(left, right, (((1,), (1,)), ((), ())), preferred_element_type=jnp.float32)


def dot_tn(left, right):
    return lax.dot_general(left, right, (((0,), (0,)), ((), ())), preferred_element_type=jnp.float32)


def normalize(values):
    center = values - jnp.mean(values, axis=-1, keepdims=True)
    inverse = lax.rsqrt(jnp.mean(center * center, axis=-1, keepdims=True) + NORM_EPS)
    return center * inverse, inverse


def normalize_back(upstream, scaled, inverse, gain):
    inner = upstream * gain
    return inverse * (
        inner
        - jnp.mean(inner, axis=-1, keepdims=True)
        - scaled * jnp.mean(inner * scaled, axis=-1, keepdims=True)
    )


def column_sum(values):
    return jnp.sum(values, axis=0, keepdims=True)


def bell(values):
    return 0.5 * (1.0 + lax.erf(values * math.sqrt(0.5)))


def bell_slope(values, area):
    return area + values * jnp.exp(-0.5 * values * values) * (1.0 / math.sqrt(2.0 * math.pi))


def send_rows(low, spread_ref, row_ref, out_ref):
    wide = jnp.concatenate(
        [dot(low[:, :384], spread_ref[...]), dot(low[:, 384:], spread_ref[...])], axis=1
    ).astype(NARROW)
    turned = dot(row_ref[0], wide) + dot(row_ref[1], wide)
    for side in range(2):
        for block in range(NB):
            out_ref[side * NB + block] = turned[
                side * HALF_TOK : (side + 1) * HALF_TOK, block * LANES : (block + 1) * LANES
            ].astype(NARROW)


def take_rows(in_ref, spread_ref, row_back_ref):
    sides = []
    for side in range(2):
        sides.append(
            jnp.concatenate(
                [in_ref[side * NB + block].astype(jnp.float32) for block in range(NB)], axis=1
            )
        )
    wide = jnp.concatenate(sides, axis=0).astype(NARROW)
    low = jnp.concatenate(
        [dot_nt(wide[:, :512], spread_ref[...]), dot_nt(wide[:, 512:], spread_ref[...])], axis=1
    ).astype(NARROW)
    return dot(row_back_ref[0], low) + dot(row_back_ref[1], low)


def fetch(sources, held_ref, sems):
    copies = [pltpu.make_async_copy(src, held_ref.at[i], sems.at[i]) for i, src in enumerate(sources)]
    for copy in copies:
        copy.start()
    return copies


def thirds(w_ref, size):
    return [w_ref[i * size : (i + 1) * size] for i in range(3)]


def embed_kernel(src_ref, shift_ref, bias_ref, norm_ref, spread_ref, row_ref, w_ref,
                 state_ref, send_ref):
    src = src_ref[...]
    state = bias_ref[...]
    for offset, weight in enumerate(thirds(w_ref, PIX)):
        moved = src if offset == 1 else dot(shift_ref[offset], src).astype(NARROW)
        state = state + dot(moved, weight)
    state_ref.put(state)
    scaled, _unused = normalize(state)
    normed = scaled * norm_ref[0:1] + norm_ref[1:2]
    send_rows(normed.astype(NARROW), spread_ref, row_ref, send_ref)


def turn_columns(wide_ref, col_ref, pair):
    kind = 0 if pair == 0 else 1
    low = wide_ref[:, 6 * pair : 6 * pair + 8, :].reshape(128, 128).astype(NARROW)
    both = dot(col_ref[0, kind], low) + dot(col_ref[1, kind], low)
    return jnp.concatenate([both[:96], both[96:]], axis=1).astype(NARROW)


def back_columns(wide_ref, col_back_ref, pair, low):
    kind = 0 if pair == 0 else 1
    both = jnp.concatenate([low[:, :128], low[:, 128:]], axis=0)
    back = dot(col_back_ref[0, kind], both) + dot(col_back_ref[1, kind], both)
    wide_ref[:, 6 * pair : 6 * pair + 8, :] = back.reshape(16, 8, 128)


def spec_kernel(
    in_ref, col_ref, col_back_ref, w_ref, b_ref, out_ref, mixed_ref, wide_ref, wide_out_ref
):
    wide_ref[:, :HALF_TOK, :] = in_ref[...].astype(jnp.float32)
    wide_ref[:, HALF_TOK:, :] = jnp.zeros((16, 8, 128), jnp.float32)
    for chunk in range(4):
        pairs = range(chunk * 3, chunk * 3 + 3)
        mixed = jnp.concatenate([turn_columns(wide_ref, col_ref, pair) for pair in pairs], axis=0)
        mixed_ref.put(mixed, slice(chunk * 288, (chunk + 1) * 288), slice(None))
        inner = dot(mixed, w_ref[0]) + b_ref[0:1]
        act = (inner * bell(inner)).astype(NARROW)
        outer = (dot(act, w_ref[1]) + b_ref[1:2]).astype(NARROW)
        for place, pair in enumerate(pairs):
            back_columns(wide_out_ref, col_back_ref, pair, outer[place * 96 : place * 96 + 96])
    out_ref[...] = wide_out_ref[:, :HALF_TOK, :].astype(NARROW)


def spec_back_kernel(
    in_ref, col_ref, col_back_ref, w_ref, b_ref, mixed_ref,
    out_ref, gw_ref, gb_ref, wide_ref, wide_out_ref,
):
    wide_ref[:, :HALF_TOK, :] = in_ref[...].astype(jnp.float32)
    wide_ref[:, HALF_TOK:, :] = jnp.zeros((16, 8, 128), jnp.float32)
    for chunk in range(4):
        pairs = range(chunk * 3, chunk * 3 + 3)
        g_outer = jnp.concatenate([turn_columns(wide_ref, col_ref, pair) for pair in pairs], axis=0)
        mixed = mixed_ref()[chunk * 288 : (chunk + 1) * 288, :]
        inner = dot(mixed, w_ref[0]) + b_ref[0:1]
        area = bell(inner)
        act = (inner * area).astype(NARROW)
        g_inner = (bell_slope(inner, area) * dot_nt(g_outer, w_ref[1])).astype(NARROW)
        g_mixed = dot_nt(g_inner, w_ref[0]).astype(NARROW)
        first, second = dot_tn(mixed, g_inner), dot_tn(act, g_outer)
        sums = jnp.concatenate(
            [column_sum(g_inner.astype(jnp.float32)), column_sum(g_outer.astype(jnp.float32))], axis=0
        )
        if chunk == 0:
            gw_ref[0], gw_ref[1], gb_ref[...] = first, second, sums
        else:
            gw_ref[0] += first
            gw_ref[1] += second
            gb_ref[...] += sums
        for place, pair in enumerate(pairs):
            back_columns(wide_out_ref, col_back_ref, pair, g_mixed[place * 96 : place * 96 + 96])
    out_ref[...] = wide_out_ref[:, :HALF_TOK, :].astype(NARROW)


def mlp_kernel(has_next, in_ref, state_ref, norm_ref, next_norm_ref, up_b_ref, down_b_ref,
               spread_ref, row_ref, row_back_ref, w0_ref, w1_ref, w2_ref, w3_ref, *rest):
    held_ref, sems = rest[-2:]
    mixed_ref, hidden_in_ref, before_ref, hidden_ref, out_ref = rest[:5]
    copies = fetch((w0_ref, w1_ref, w2_ref, w3_ref), held_ref, sems)
    spatial = take_rows(in_ref, spread_ref, row_back_ref)
    state = state_ref()[...]
    scaled, _unused = normalize(state)
    mixed = state + spatial + (scaled * norm_ref[0:1] + norm_ref[1:2])
    mixed_ref.put(mixed)
    again, _unused = normalize(mixed)
    hidden_in = (again * norm_ref[2:3] + norm_ref[3:4]).astype(NARROW)
    hidden_in_ref.put(hidden_in)
    out = mixed + down_b_ref[...]
    for part in range(4):
        spot = slice(part * D, (part + 1) * D)
        copies[part].wait()
        before = dot_nt(hidden_in, held_ref[part, 0]) + up_b_ref[:, spot]
        before_ref.put(before, slice(None), spot)
        hidden = (before * bell(before)).astype(NARROW)
        hidden_ref.put(hidden, slice(None), spot)
        out = out + dot(hidden, held_ref[part, 1])
    out_ref.put(out)
    if has_next:
        scaled, _unused = normalize(out)
        normed = scaled * next_norm_ref[0:1] + next_norm_ref[1:2]
        send_rows(normed.astype(NARROW), spread_ref, row_ref, rest[5])


def head_kernel(state_ref, shift_ref, bias_ref, target_ref, weight_ref, w_ref,
                low_ref, pred_ref, grad_ref, loss_ref):
    low = state_ref()[...].astype(NARROW)
    low_ref.put(low)
    predicted = bias_ref[...]
    for offset, weight in enumerate(thirds(w_ref, D)):
        moved = low if offset == 1 else dot(shift_ref[offset], low).astype(NARROW)
        predicted = predicted + dot(moved, weight)
    pred_ref[...] = predicted.astype(NARROW)
    differ = predicted - target_ref()[...].astype(jnp.float32)
    grad_ref.put(weight_ref[:, 1:2] * differ)
    loss_ref[...] = column_sum(weight_ref[:, 0:1] * differ * differ)


def head_back_kernel(grad_ref, shift_ref, w_ref, low_ref, sum_ref, out_ref):
    low = grad_ref()[...].astype(NARROW)
    low_ref.put(low)
    sum_ref[...] = column_sum(low.astype(jnp.float32))
    total = None
    for offset, weight in enumerate(thirds(w_ref, D)):
        moved = low if offset == 1 else dot(shift_ref[2 - offset], low).astype(NARROW)
        part = dot_nt(moved, weight)
        total = part if total is None else total + part
    out_ref[...] = total


def embed_back_kernel(low_ref, shift_ref, add_ref, w_ref, out_ref):
    low = low_ref[...]
    total = None
    for offset, weight in enumerate(thirds(w_ref, PIX)):
        moved = low if offset == 1 else dot(shift_ref[2 - offset], low).astype(NARROW)
        part = dot_nt(moved, weight)
        total = part if total is None else total + part
    out_ref.put(add_ref()[...] + total)


def mlp_back_kernel(up_ref, before_ref, mixed_ref, norm_ref, spread_ref, row_ref,
                    w0_ref, w1_ref, w2_ref, w3_ref,
                    grad_out_ref, g_before_ref, g_mixed_ref, g_up_b_ref, sums_ref, send_ref,
                    held_ref, sems):
    copies = fetch((w0_ref, w1_ref, w2_ref, w3_ref), held_ref, sems)
    upstream = up_ref[...]
    grad_out = upstream.astype(NARROW)
    grad_out_ref.put(grad_out)
    sums_ref[0:1] = column_sum(grad_out.astype(jnp.float32))
    g_second = None
    for part in range(4):
        spot = slice(part * D, (part + 1) * D)
        before = before_ref()[:, spot]
        slope = bell_slope(before, bell(before))
        copies[part].wait()
        g_before = (slope * dot_nt(grad_out, held_ref[part, 1])).astype(NARROW)
        g_before_ref.put(g_before, slice(None), spot)
        g_up_b_ref[:, spot] = column_sum(g_before.astype(jnp.float32))
        now = dot(g_before, held_ref[part, 0])
        g_second = now if g_second is None else g_second + now
    scaled, inverse = normalize(mixed_ref()[...])
    sums_ref[1:2] = column_sum(g_second * scaled)
    sums_ref[2:3] = column_sum(g_second)
    g_mixed = upstream + normalize_back(g_second, scaled, inverse, norm_ref[2:3])
    g_mixed_ref.put(g_mixed)
    send_rows(g_mixed.astype(NARROW), spread_ref, row_ref, send_ref)


def norm_back_kernel(in_ref, g_mixed_ref, state_ref, norm_ref, spread_ref, row_back_ref,
                     out_ref, low_ref, sums_ref):
    g_normed = take_rows(in_ref, spread_ref, row_back_ref)
    g_mixed = g_mixed_ref()[...]
    g_normed = g_normed + g_mixed
    scaled, inverse = normalize(state_ref()[...])
    out = g_mixed + normalize_back(g_normed, scaled, inverse, norm_ref[0:1])
    out_ref[...] = out
    low = out.astype(NARROW)
    low_ref[...] = low
    sums_ref[0:1] = column_sum(g_normed * scaled)
    sums_ref[1:2] = column_sum(g_normed)
    sums_ref[2:3] = column_sum(low.astype(jnp.float32))


def narrow_kernel(place_ref, in_ref, out_ref):
    out_ref[...] = in_ref[...].astype(NARROW)


def own_quarters(weights, depth, place):
    size = weights.shape[2] // 4

    def from_spot(m, q, place_ref):
        return (depth, m, (q // 2 + place_ref[0]) % 2 * 2 + q % 2, 0)

    return pl.pallas_call(
        narrow_kernel,
        name="narrow",
        out_shape=jax.ShapeDtypeStruct((2, 2, 2, size, D), NARROW),
        grid_spec=pltpu.PrefetchScalarGridSpec(
            num_scalar_prefetch=1,
            grid=(2, 4),
            in_specs=[pl.BlockSpec((None, None, size, D), from_spot)],
            out_specs=pl.BlockSpec(
                (None, None, None, size, D), lambda m, q, place_ref: (m, q // 2, q % 2, 0, 0)
            ),
        ),
    )(place, weights)


def muon_kernel(level_ref, momentum_ref, weight_ref, change_ref, out_ref):
    momentum = momentum_ref[...]
    ortho = POLY_COEF[0] * POLY_COEF[0] * level_ref[pl.program_id(0)] * momentum
    ortho = ortho + dot(momentum.astype(NARROW), change_ref[...])
    out_ref[...] = weight_ref[...] * (1.0 - MUON_RATE * DECAY_RATE) - MUON_RATE * (FF / D) ** 0.5 * ortho


class Coming:
    def __init__(self, far_ref, held_ref, sem):
        self.held, self.copy = held_ref, pltpu.make_async_copy(far_ref, held_ref, sem)
        self.copy.start()

    def __call__(self):
        if self.copy is not None:
            self.copy.wait()
        self.copy = None
        return self.held


class Going:
    def __init__(self, far_ref, held_ref, sems):
        self.far, self.held, self.sems, self.copies = far_ref, held_ref, sems, []

    def put(self, value, *spot):
        if spot:
            self.held[spot] = value
            source, target = self.held.at[spot], self.far.at[spot]
        else:
            self.held[...] = value
            source, target = self.held, self.far
        copy = pltpu.make_async_copy(source, target, self.sems.at[len(self.copies)])
        copy.start()
        self.copies.append(copy)


PIECES = 4


def launch(kernel, name, out_dims, operands, far=(), far_out=False, near=(), scratch=(), limit=16,
           coming=(), going=()):
    anywhere = pl.BlockSpec(memory_space=pltpu.HBM)
    local = pl.BlockSpec(memory_space=pltpu.VMEM)
    in_specs = []
    for i in range(len(operands)):
        if i in near:
            in_specs.append(pl.BlockSpec(memory_space=pltpu.SMEM))
        else:
            in_specs.append(anywhere if i in far or i in coming else local)
    sem = pltpu.SemaphoreType.DMA
    staged = [pltpu.VMEM(operands[i].shape, operands[i].dtype) for i in coming]
    staged += [pltpu.VMEM(*out_dims[i]) for i in going]
    staged += [sem((len(coming),))] * bool(coming) + [sem((PIECES,))] * len(going)
    ins, outs = len(operands), len(out_dims)

    def body(*refs):
        refs, rest = list(refs[: ins + outs]), refs[ins + outs :]
        held, rest = rest[: len(staged)], rest[len(staged) :]
        tail = len(coming) + len(going)
        for number, i in enumerate(coming):
            refs[i] = Coming(refs[i], held[number], held[tail].at[number])
        sent = []
        for number, i in enumerate(going):
            sems = held[tail + bool(coming) + number]
            refs[ins + i] = Going(refs[ins + i], held[len(coming) + number], sems)
            sent.append(refs[ins + i])
        kernel(*refs, *rest)
        for way in sent:
            for copy in way.copies:
                copy.wait()

    operands = [
        pltpu.with_memory_space_constraint(a, pltpu.HBM) if i in far or i in coming else a
        for i, a in enumerate(operands)
    ]
    out_shape = [
        pltpu.HBM(*dims) if far_out or i in going else jax.ShapeDtypeStruct(*dims)
        for i, dims in enumerate(out_dims)
    ]
    return pl.pallas_call(
        body,
        name=name,
        out_shape=out_shape,
        in_specs=in_specs,
        out_specs=[anywhere if far_out or i in going else local for i in range(outs)],
        scratch_shapes=staged + list(scratch),
        compiler_params=pltpu.CompilerParams(vmem_limit_bytes=limit * 1024 * 1024),
    )(*operands)


def exchange(values):
    return lax.all_to_all(values, ITEM_AXES, split_axis=0, concat_axis=0, tiled=True)


def total_over(values, axes):
    count = lax.axis_size(axes)
    spread = jnp.broadcast_to(jnp.pad(values, (0, LANES - values.shape[0])), (count, 1, LANES))
    got = lax.all_to_all(spread, axes, split_axis=0, concat_axis=0, tiled=True)
    return jnp.sum(got, axis=(0, 1))[: values.shape[0]]


KINDS = {"embed": (D, 6), "head": (PIX, 10), "rest": (LANES, 1)}


def kind_ranges(total):
    edges = (0, EMBED_SIZE, 2 * EMBED_SIZE, total)
    return dict(zip(KINDS, zip(edges[:-1], edges[1:])))


def window_pieces(index, width, total):
    found = []
    for kind, (low, high) in kind_ranges(total).items():
        begin, end = max(index * width, low), min((index + 1) * width, high)
        if begin >= end:
            continue
        row, tiles = KINDS[kind]
        first = (begin - low) // (8 * row)
        last = -(-(end - low) // (8 * row))
        found.append([kind, first, last, 0, begin, end])
    spot = {"embed": EMBED_AT, "head": 0, "rest": 0}
    kinds = [piece[0] for piece in found]
    for piece in found:
        piece[3] = spot[piece[0]]
    if kinds == ["embed", "head"]:
        used = (found[1][2] - found[1][1]) * 10
        found[0][3] = EMBED_AT + -(-(used - EMBED_AT) // 6) * 6
    if kinds == ["head", "rest"]:
        found[1][3] = (found[0][2] - found[0][1]) * 10
    for piece in found:
        assert piece[3] + (piece[2] - piece[1]) * KINDS[piece[0]][1] <= WINDOW
    return found


def form_range(kind, device, width, total, count):
    row, tiles = KINDS[kind]
    base, edge = kind_ranges(total)[kind]
    origin = device * width
    low = jnp.clip(base - origin, 0, width)
    high = jnp.clip(edge - origin, 0, width)
    inside = jnp.maximum(origin - base, 0)
    start = inside % (8 * row) - low
    first = EMBED_AT if kind == "embed" else 0
    for index in range(count):
        for piece in window_pieces(index, width, total):
            if piece[0] == kind and piece[3] != first:
                start = start + jnp.where(device == index, (piece[3] - first) * 8 * LANES, 0)
    return start, low, high


def form_tiles(kind):
    if kind == "embed":
        return EMBED_AT, (WINDOW - EMBED_AT) // 6
    return (0, WINDOW // 10) if kind == "head" else (0, WINDOW)


def own_window(own, device, width, total, count):
    spot = jnp.arange(width, dtype=jnp.int32)
    window = jnp.zeros((WINDOW, 8, LANES), jnp.float32)
    for kind, (row, tiles) in KINDS.items():
        start, low, high = form_range(kind, device, width, total, count)
        first, groups = form_tiles(kind)
        length = groups * tiles * 8 * LANES
        held = jnp.where((spot >= low) & (spot < high), own, 0.0)
        held = jnp.pad(held, (length, length))
        form = lax.dynamic_slice(held, (length - start,), (length,))
        form = form.reshape(groups, 8, tiles, LANES).transpose(0, 2, 1, 3).reshape(-1, 8, LANES)
        window = window + jnp.pad(form, ((first, WINDOW - first - groups * tiles), (0, 0), (0, 0)))
    return window


def own_range(window, device, width, total, count):
    spot = jnp.arange(width, dtype=jnp.int32)
    result = jnp.zeros((width,), jnp.float32)
    for kind, (row, tiles) in KINDS.items():
        start, low, high = form_range(kind, device, width, total, count)
        first, groups = form_tiles(kind)
        form = window[first : first + groups * tiles].reshape(groups, tiles, 8, LANES)
        form = jnp.pad(form.transpose(0, 2, 1, 3).reshape(-1), (width, width))
        held = lax.dynamic_slice(form, (width + start,), (width,))
        result = jnp.where((spot >= low) & (spot < high), held, result)
    return result


def gather_windows(own, *early):
    value, *early = lax.optimization_barrier((jnp.stack([own, swap(own, "zh")]), *early))
    thirds = []
    ways = ["x", "y", "zl"]
    for i in range(3):
        part = value[:, WINDOW_CUTS[i] : WINDOW_CUTS[i + 1]]
        for axis in ways[i:] + ways[:i]:
            part = jnp.stack([part, swap(part, axis)])
        thirds.append((part, swap(part, "c")))
    return thirds, *early


def join_plan(kind, width, total, count):
    tiles = KINDS[kind][1]
    pieces = []
    for index in range(count):
        for piece in window_pieces(index, width, total):
            if piece[0] == kind:
                pieces.append((index, piece[1] * tiles, piece[2] * tiles, piece[3]))
    single, double = [], []
    for spot, (index, first, last, tile) in enumerate(pieces):
        begin, end = first, last
        if spot and pieces[spot - 1][2] > first:
            before, before_first, begin, before_tile = pieces[spot - 1]
            double.append((first, begin - first, before, before_tile + first - before_first, index, tile))
        if spot + 1 < len(pieces):
            end = min(last, pieces[spot + 1][1])
        if begin < end:
            single.append((begin, end - begin, index, tile + begin - first))
    return single, double


def by_thirds(size, tile):
    found = []
    for third in range(3):
        begin, end = max(tile, WINDOW_CUTS[third]), min(tile + size, WINDOW_CUTS[third + 1])
        if begin < end:
            found.append((third, begin - WINDOW_CUTS[third], end - begin, begin - tile))
    return found


def join_kernel(single, double, place_ref, *refs):
    sources, (out_ref, left_ref, right_ref, sems) = refs[:6], refs[6:]
    own = [place_ref[i] for i in range(5)]
    count = 0

    def start(index, size, tile, target_ref, at):
        nonlocal count
        rel = {
            axis: (index // unit + spot) % 2
            for axis, unit, spot in zip(SUB_AXES, (16, 8, 4, 2, 1), own)
        }
        ways = ["x", "y", "zl"]
        ends = []
        for third, begin, amount, offset in by_thirds(size, tile):
            spots = [rel[axis] for axis in (ways[third:] + ways[:third])[::-1]] + [rel["zh"]]
            sources_now = sources[2 * third : 2 * third + 2]
            copies = [
                pltpu.make_async_copy(
                    ref.at[(*spots, pl.ds(begin, amount))],
                    target_ref.at[pl.ds(at + offset, amount)],
                    sems.at[count],
                )
                for ref in sources_now
            ]
            count += 1

            @pl.when(rel["c"] == 0)
            def _():
                copies[0].start()

            @pl.when(rel["c"] == 1)
            def _():
                copies[1].start()

            ends.append(copies[0])
        return ends

    edges = []
    for spot, (begin, size, before, before_tile, index, tile) in enumerate(double):
        edges += start(before, size, before_tile, left_ref.at[spot], 0)
        edges += start(index, size, tile, right_ref.at[spot], 0)
    ends = []
    for begin, size, index, tile in single:
        ends += start(index, size, tile, out_ref, begin)
    for copy in edges:
        copy.wait()
    for spot, (begin, size, *unused) in enumerate(double):
        both = left_ref[spot, :size].astype(jnp.float32) + right_ref[spot, :size].astype(jnp.float32)
        out_ref[begin : begin + size] = both.astype(NARROW)
    for copy in ends:
        copy.wait()


def join_windows(thirds, place, kind, width, total, count):
    row, tiles = KINDS[kind]
    low, high = kind_ranges(total)[kind]
    single, double = join_plan(kind, width, total, count)
    groups = -(-(high - low) // (8 * row))
    amount = sum(len(by_thirds(size, tile)) for begin, size, index, tile in single)
    for begin, size, before, before_tile, index, tile in double:
        amount += len(by_thirds(size, before_tile)) + len(by_thirds(size, tile))
    held = pltpu.VMEM((max(len(double), 1), max([d[1] for d in double] + [1]), 8, LANES), NARROW)
    (out,) = launch(
        functools.partial(join_kernel, single, double), "join_" + kind,
        [((groups * tiles, 8, LANES), NARROW)], [place] + [ref for pair in thirds for ref in pair],
        near=(0,), far=tuple(range(1, 7)), scratch=(held, held, pltpu.SemaphoreType.DMA((amount,))),
    )
    return out.reshape(groups, tiles, 8, LANES).transpose(0, 2, 1, 3).reshape(groups * 8, row)


def pack_plan(width, total, count):
    plan = []
    for index in range(count):
        for kind, first, last, tile, begin, end in window_pieces(index, width, total):
            tiles = KINDS[kind][1]
            if kind == "rest":
                plan.append((index, 6, first, last - first, tile))
                continue
            size = (PIX if kind == "embed" else D) // 8
            while first < last:
                source = first // size
                stop = min(last, (source + 1) * size)
                number = source + (0 if kind == "embed" else 3)
                plan.append((index, number, (first - source * size) * tiles, (stop - first) * tiles, tile))
                tile += (stop - first) * tiles
                first = stop
    return plan


def pack_kernel(plan, place_ref, *refs):
    sources, (keep_ref, send_ref, sems) = refs[:7], refs[7:]
    zh, zl, x, y, c = (place_ref[i] for i in range(5))
    ends = []
    for number, (index, source, begin, size, tile) in enumerate(plan):
        core = index % 2
        place = zip((16, 8, 4, 2), (zh, zl, x, y))
        spot = tuple((index // unit + own) % 2 for unit, own in place) + (pl.ds(tile, size),)
        from_ref = sources[source].at[pl.ds(begin, size)]
        keep = pltpu.make_async_copy(from_ref, keep_ref.at[spot], sems.at[number])
        send = pltpu.make_async_copy(from_ref, send_ref.at[spot], sems.at[number])

        @pl.when(c == core)
        def _():
            keep.start()

        @pl.when(c != core)
        def _():
            send.start()

        ends.append(keep)
    for copy in ends:
        copy.wait()


def tiles_of(values):
    rows, columns = values.shape
    split = values.reshape(rows // 8, 8, columns // LANES, LANES)
    return split.transpose(0, 2, 1, 3).reshape(-1, 8, LANES)


def swap(values, axis):
    return lax.ppermute(values, axis, [(0, 1), (1, 0)])


def add_low(*values):
    return sum(v.astype(jnp.float32) for v in values).astype(NARROW)


def side(values, dim, which, turn):
    if turn is None:
        return lax.index_in_dim(values, which, dim, keepdims=True)
    return lax.dynamic_slice_in_dim(values, (which + turn) % 2, 1, dim)


def chip_parts(kept, ways, cuts, cut_dim):
    return [
        ([lax.slice_in_dim(v, cuts[i], cuts[i + 1], axis=cut_dim) for v in kept], ways[i:] + ways[:i])
        for i in range(3)
    ]


def chip_stage(parts, stage):
    result = []
    for values, order in parts:
        dim, axis, turn = order[stage]
        got = swap(add_low(*(side(v, dim, 1, turn) for v in values)), axis)
        result.append(([add_low(got, *(side(v, dim, 0, turn) for v in values))], order))
    return result


def chip_join(parts, cut_dim):
    return jnp.concatenate([values[0] for values, order in parts], axis=cut_dim)


def held_back(parts, *others):
    flat = [values[0] for values, order in parts]
    flat, others = lax.optimization_barrier((flat, others))
    return [([v], order) for v, (unused, order) in zip(flat, parts)], *others


def plane_sum(values):
    rows = values.shape[0]
    core = lax.axis_index("c")
    halves = values.reshape(2, rows // 2, values.shape[1])
    kept = lax.dynamic_index_in_dim(halves, core, 0, keepdims=False)
    sent = lax.dynamic_index_in_dim(halves, 1 - core, 0, keepdims=False).astype(NARROW)
    kept = kept + swap(sent, "c").astype(jnp.float32)
    quarter = rows // 4
    parts = []
    for start, order in ((0, ("x", "y")), (quarter, ("y", "x"))):
        value = kept[start : start + quarter]
        for axis in order:
            low = value.astype(NARROW)
            value = low.astype(jnp.float32) + swap(low, axis).astype(jnp.float32)
        parts.append(value)
    mine = jnp.concatenate(parts, axis=0).astype(NARROW)
    other = swap(mine, "c")
    first = jnp.where(core == 0, mine, other)
    second = jnp.where(core == 0, other, mine)
    return jnp.concatenate([first, second], axis=0).astype(jnp.float32)


def line_gather(own):
    plane = lax.axis_index(Z_AXES)
    below, above = [], []
    value = own
    for step in (1, 2, 3):
        value = lax.ppermute(value, Z_AXES, [(i, i + 1) for i in range(step - 1, 3)])
        below.append(value)
    value = own
    for step in (1, 2, 3):
        value = lax.ppermute(value, Z_AXES, [(i, i - 1) for i in range(1, 5 - step)])
        above.append(value)
    stack = jnp.stack(below[::-1] + [own] + above)
    return lax.dynamic_slice_in_dim(stack, 3 - plane, 4, 0)


def unpack_rest(rest):
    found = []
    offset = 0
    for dims in ((D,), (PIX,), (L, 2, 2, D), (L, 4, D), (L, FF + D)):
        amount = math.prod(dims)
        found.append(rest[offset : offset + amount].reshape(dims))
        offset += amount
    return found


def fast_body(pixels, targets, mask, lat_rows, adam_params, adam_m, adam_v, mlp_weights, mlp_momentum):
    lat_index, lon_index = lax.axis_index(LAT_AXES), lax.axis_index(LON_AXES)
    device = lax.axis_index(SUB_AXES)
    devices = lax.axis_size(SUB_AXES)
    width = adam_params.shape[0]
    total = width * devices
    low_side = lax.axis_index("zl") == 0
    x, y, c = lax.axis_index("x"), lax.axis_index("y"), lax.axis_index("c")
    block = lax.axis_index(("x", "y", "c"))
    shifts = jnp.asarray(shift_tables(), NARROW)
    row_fwd = jnp.asarray(two_terms(row_table()))
    row_back = jnp.asarray(two_terms(row_table().T))
    col_fwd = jnp.asarray(two_terms(column_tables()))
    col_back = jnp.asarray(two_terms(column_tables().transpose(0, 2, 1)))
    col_fwd = jnp.where(low_side, col_fwd, col_fwd[:, 1:2])
    col_back = jnp.where(low_side, col_back, col_back[:, 1:2])
    spread = jnp.asarray(spread_table(), NARROW)

    def to_items(values):
        rest = values.shape[4:]
        lead, items, rows, cols = values.shape[:4]
        split = values.reshape((lead, items, rows, 4, OWN) + rest)
        order = (1, 3, 0, 2, 4) + tuple(range(5, 5 + len(rest)))
        packed = split.transpose(order).reshape((items * 4, lead * rows * OWN) + rest)
        got = lax.all_to_all(packed, LAT_AXES, split_axis=0, concat_axis=0, tiled=True)
        got = got.reshape((items * 4, lead, rows * OWN) + rest)
        return jnp.moveaxis(got, 1, 0).reshape((lead, TOK) + rest)

    source = to_items(pixels[None])[0]
    zh, zl = lax.axis_index("zh"), lax.axis_index("zl")
    place = jnp.stack([zh, zl, x, y, c])
    own = own_window(adam_params, device, width, total, devices).astype(NARROW)
    quarters = [own_quarters(mlp_weights, depth, x[None]) for depth in range(L)]
    windows, source, *quarters = gather_windows(own, source, *quarters)
    own_mask = own_window(jnp.ones((width,), jnp.float32), device, width, total, devices)
    mlp_low = []
    for depth, own in enumerate(quarters):
        if depth % 2 == 0:
            first = swap(lax.dynamic_index_in_dim(own[:, 0], zl, 1, keepdims=False), "y")
            both = jnp.stack([first, swap(first, "x")], axis=1)
            others = swap(both, "zl")
            across_y = jnp.where(
                zl == 0, jnp.stack([both, others], axis=2), jnp.stack([others, both], axis=2)
            )
        else:
            first = swap(own[:, 0], "y")
            across_y = jnp.stack([first, swap(first, "x")], axis=1)
        four = (own, across_y, swap(own, "c"), swap(across_y, "c"))
        mlp_low.append([chunk.reshape(2, D, D) for chunk in four])
    wanted = to_items(targets)
    row_weight = jnp.sin(math.pi * (lat_rows.astype(jnp.float32) + 0.5) / ROWS)
    weight_local = row_weight[None, :, None] * mask.astype(jnp.float32)
    weights = to_items(weight_local[None])[0]
    weight_sum = total_over(jnp.sum(weight_local)[None], SUB_AXES)[0]
    loss_scale = 2.0 / (STEPS * PIX * weight_sum)
    weight_pair = jnp.stack([weights, weights * loss_scale], axis=1)

    embed_w = join_windows(windows, place, "embed", width, total, devices)
    head_w = join_windows(windows, place, "head", width, total, devices)
    rest = join_windows(windows, place, "rest", width, total, devices)
    spec_rows = L * 4 * NB * BS * BS // LANES
    spec_w = rest[:spec_rows].reshape(L, 2, 2, NB, BS, BS)
    embed_b, head_b, spec_b, norm_params, mlp_b = unpack_rest(rest[spec_rows:].reshape(-1))
    embed_b, head_b = embed_b.astype(jnp.float32)[None], head_b.astype(jnp.float32)[None]
    norms = norm_params.astype(jnp.float32)
    mlp_b = mlp_b.astype(jnp.float32)

    def by_place(values):
        for dim, side in ((1, y), (2, c), (3, x)):
            values = jnp.where(side == 0, values, jnp.flip(values, dim))
        return values

    up_b = by_place(mlp_b[:, :FF].reshape(L, 2, 2, 2, -1)).transpose(0, 2, 1, 3, 4)
    up_b = up_b.reshape(L, 1, FF)
    down_b = mlp_b[:, None, FF:]
    gap = LANES - BS
    own_w = lax.dynamic_index_in_dim(spec_w, block, 3, keepdims=False)
    own_w = jnp.pad(own_w, ((0, 0),) * 3 + ((0, gap), (0, gap)))
    real, imag = own_w[:, :, 0], own_w[:, :, 1]
    pair_w = jnp.concatenate(
        [jnp.concatenate([real, imag], axis=-1), jnp.concatenate([-imag, real], axis=-1)], axis=-2
    )
    own_b = lax.dynamic_slice_in_dim(spec_b, block * BS, BS, 3).astype(jnp.float32)
    pair_b = jnp.pad(own_b, ((0, 0),) * 3 + ((0, gap),)).reshape(L, 2, 2 * LANES)

    f32 = jnp.float32
    payload = ((GROUP, HALF_TOK, LANES), NARROW)
    state_f32 = ((TOK, D), f32)
    wide = pltpu.VMEM((GROUP, HALF_TOK + 8, LANES), f32)
    sem = pltpu.SemaphoreType.DMA
    held_mlp = (pltpu.VMEM((4, 2, D, D), NARROW), sem((4,)))

    current = source
    saved = []
    loss_sums = []
    for roll_idx in range(STEPS):
        state, sent = launch(
            embed_kernel, "embed", [state_f32, payload],
            [current, shifts, embed_b, norms[0], spread, row_fwd, embed_w], going=(0,),
        )
        layers = []
        for depth in range(L):
            got = exchange(sent)
            out, mixed_in = launch(
                spec_kernel, "spec", [payload, ((FREQ, 2 * LANES), NARROW)],
                [got, col_fwd, col_back, pair_w[depth], pair_b[depth]], scratch=(wide, wide),
                going=(1,),
            )
            got = exchange(out)
            has_next = depth + 1 < L
            outs = [state_f32, ((TOK, D), NARROW), ((TOK, FF), f32), ((TOK, FF), NARROW), state_f32]
            results = launch(
                functools.partial(mlp_kernel, has_next), "mlp", outs + [payload] * has_next,
                [got, state, norms[depth], norms[min(depth + 1, L - 1)], up_b[depth], down_b[depth],
                 spread, row_fwd, row_back, *mlp_low[depth]], far=(9, 10, 11, 12), scratch=held_mlp, limit=MLP_LIMIT,
                coming=(1,), going=(0, 1, 2, 3, 4),
            )
            layers.append((state, mixed_in) + tuple(results[:4]))
            state = results[4]
            if has_next:
                sent = results[5]
        low, predicted, loss_grad, loss_part = launch(
            head_kernel, "head",
            [((TOK, D), NARROW), ((TOK, PIX), NARROW), ((TOK, PIX), f32), ((1, PIX), f32)],
            [state, shifts, head_b, wanted[roll_idx], weight_pair, head_w], coming=(0, 3), going=(0, 2),
        )
        loss_sums.append(loss_part)
        saved.append((current, layers, low, loss_grad))
        current = predicted

    rows_own = mlp_momentum.shape[2] // 2
    half_ff = FF // 2

    def joined(terms, member):
        return jnp.concatenate([now[member] for now in terms], axis=0)

    mlp_ways = [(3, "x", None), (2, "y", None), (1, "zl", zl)]

    def mlp_sends(depth):
        g_before, hidden_in, hidden, grad_out = (joined(mlp_terms[depth], m) for m in range(4))
        pairs = ((g_before, hidden_in), (hidden, grad_out))
        return pairs, [swap(dot_tn(a[:, half_ff:], b).astype(NARROW), "c") for a, b in pairs]

    def mlp_kept(pairs, got):
        kept = [
            (dot_tn(a[:, :half_ff], b) + sent.astype(f32)).astype(NARROW)
            for (a, b), sent in zip(pairs, got)
        ]
        return jnp.stack(kept).reshape(2, 2, 2, rows_own, D)

    head_terms, embed_terms = [], []
    mlp_terms = [[] for unused in range(L)]
    spec_terms = [[] for unused in range(L)]
    sum_terms = [[] for unused in range(L)]
    head_sums, embed_sums = [], []
    upstream = None
    for roll_idx in reversed(range(STEPS)):
        current, layers, low, loss_grad = saved[roll_idx]
        upstream = loss_grad if upstream is None else upstream
        upstream_low, head_sum, grad_state = launch(
            head_back_kernel, "head_back",
            [((TOK, PIX), NARROW), ((1, PIX), f32), state_f32], [upstream, shifts, head_w],
            coming=(0,), going=(0,),
        )
        head_terms.append((low, upstream_low))
        head_sums.append(head_sum)
        for depth in reversed(range(L)):
            state, mixed_in, mixed, hidden_in, before, hidden = layers[depth]
            grad_out, g_before, g_mixed, g_up_b, sums_two, sent = launch(
                mlp_back_kernel, "mlp_back",
                [((TOK, D), NARROW), ((TOK, FF), NARROW), state_f32, ((1, FF), f32), ((3, D), f32),
                 payload],
                [grad_state, before, mixed, norms[depth], spread, row_fwd, *mlp_low[depth]],
                far=(6, 7, 8, 9), scratch=held_mlp, limit=MLP_LIMIT,
                coming=(1, 2), going=(0, 1, 2),
            )
            mlp_terms[depth].append((g_before, hidden_in, hidden, grad_out))
            got = exchange(sent)
            if roll_idx == 0 and depth == L - 1:
                last_sends = mlp_sends(depth)
                last_kept, got = lax.optimization_barrier((mlp_kept(*last_sends), got))
            if roll_idx == 0 and depth == 0:
                first_kept, got = lax.optimization_barrier((mlp_kept(*mlp_sends(0)), got))
            out, g_pair, g_pair_b = launch(
                spec_back_kernel, "spec_back",
                [payload, ((2, 2 * LANES, 2 * LANES), f32), ((2, 2 * LANES), f32)],
                [got, col_fwd, col_back, pair_w[depth], pair_b[depth], mixed_in],
                scratch=(wide, wide), coming=(5,),
            )
            got = exchange(out)
            if roll_idx == 0 and depth == 0:
                last_kept, first_kept, got = lax.optimization_barrier((last_kept, first_kept, got))
            grad_state, state_low, sums_one = launch(
                norm_back_kernel, "norm_back", [state_f32, ((TOK, D), NARROW), ((3, D), f32)],
                [got, g_mixed, state, norms[depth], spread, row_back], coming=(1, 2),
            )
            spec_terms[depth].append((g_pair, g_pair_b))
            sum_terms[depth].append((sums_one, sums_two, g_up_b))
        embed_terms.append((current, state_low))
        embed_sums.append(sums_one[2])
        if roll_idx:
            (upstream,) = launch(
                embed_back_kernel, "embed_back", [((TOK, PIX), f32)],
                [state_low, shifts, saved[roll_idx - 1][3], embed_w], coming=(2,), going=(0,),
            )

    mlp_kept_all = jnp.stack([first_kept, last_kept])
    mlp_parts = chip_stage(chip_parts([mlp_kept_all], mlp_ways, MLP_CUTS, 4), 0)

    def moved_pair(values, amount):
        return jnp.concatenate([jnp.roll(now, amount, axis=0) for now in values], axis=0)

    embed_src = joined(embed_terms, 0)
    head_up = joined(head_terms, 1)
    g_embed = [
        dot_tn(embed_src, moved_pair([now[1] for now in embed_terms], OWN * (o - 1))).astype(NARROW)
        for o in range(3)
    ]
    g_head = [
        dot_tn(moved_pair([now[0] for now in head_terms], -OWN * (o - 1)), head_up).astype(NARROW)
        for o in range(3)
    ]
    g_spec, g_spec_b, g_norm, g_mlp_b = [], [], [], []
    for depth in range(L):
        pair_sum = sum(now[0] for now in spec_terms[depth]).reshape(2, 2, LANES, 2, LANES)
        pair_sum = pair_sum[:, :, :BS, :, :BS]
        g_real = pair_sum[:, 0, :, 0] + pair_sum[:, 1, :, 1]
        g_imag = pair_sum[:, 0, :, 1] - pair_sum[:, 1, :, 0]
        g_spec.append(jnp.stack([g_real, g_imag], axis=1))
        g_spec_b.append(sum(now[1] for now in spec_terms[depth]).reshape(2, 2, LANES)[:, :, :BS])
        one = sum(now[0] for now in sum_terms[depth])
        two = sum(now[1] for now in sum_terms[depth])
        g_norm.append(jnp.stack([one[0], one[1], two[1], two[2]]))
        up_sum = sum(now[2] for now in sum_terms[depth]).reshape(1, 2, 2, 2, -1)
        up_sum = by_place(up_sum.transpose(0, 2, 1, 3, 4)).reshape(-1)
        g_mlp_b.append(jnp.concatenate([up_sum, two[0]]))
    full_spec = jnp.zeros((L, 2, 2, NB, BS, BS), NARROW)
    full_spec = lax.dynamic_update_slice_in_dim(
        full_spec, jnp.stack(g_spec).astype(NARROW)[:, :, :, None], block, 3
    )
    full_spec_b = lax.dynamic_update_slice_in_dim(
        jnp.zeros((L, 2, 2, D), f32), jnp.stack(g_spec_b), block * BS, 3
    )
    small = jnp.concatenate(
        [sum(embed_sums), sum(head_sums)[0], full_spec_b.reshape(-1),
         jnp.stack(g_norm).reshape(-1), jnp.stack(g_mlp_b).reshape(-1)]
    ).astype(NARROW)
    rest_grad = jnp.concatenate([full_spec.reshape(-1), small])
    rest_grad = jnp.pad(rest_grad, (0, -rest_grad.shape[0] % (8 * LANES))).reshape(-1, 8, LANES)
    plan = pack_plan(width, total, devices)
    window_set = ((2, 2, 2, 2, WINDOW, 8, LANES), NARROW)
    kept, sent = launch(
        functools.partial(pack_kernel, plan), "pack", [window_set, window_set],
        [place] + [tiles_of(g) for g in g_embed + g_head] + [rest_grad],
        near=(0,), far_out=True, scratch=(sem((len(plan),)),), limit=8,
    )
    ways = [(2, "x", None), (3, "y", None), (1, "zl", None)]
    got = swap(sent, "c")
    mlp_parts, got = held_back(mlp_parts, got)
    parts = chip_parts([kept, got], ways, WINDOW_CUTS, 4)
    for stage in range(3):
        parts = chip_stage(parts, stage)
        if stage:
            mlp_parts = chip_stage(mlp_parts, stage)
    mlp_pair = chip_join(mlp_parts, 4).reshape(2, rows_own, D)
    mlp_send = jnp.where(zh == 0, mlp_pair[1], mlp_pair[0])
    mlp_keep = jnp.where(zh == 0, mlp_pair[0], mlp_pair[1])
    mlp_mine = mlp_keep.astype(f32) + swap(mlp_send, "zh").astype(f32)
    flat_pair = chip_join(parts, 4).reshape(2, WINDOW, 8, LANES)
    flat_window = flat_pair[0].astype(f32) + swap(flat_pair[1], "zh").astype(f32)
    flat_piece = own_range(flat_window, device, width, total, devices)
    local = jnp.stack(
        [jnp.sum(jnp.where(own_mask > 0, flat_window * flat_window, 0.0)) + jnp.sum(mlp_mine * mlp_mine),
         sum(jnp.sum(now) for now in loss_sums)]
    )
    square_sum, loss_total = total_over(local, SUB_AXES)
    loss_total = loss_total / (STEPS * PIX * weight_sum)
    grad_norm = jnp.sqrt(square_sum)
    factor = jnp.minimum(1.0, CLIP_LEVEL / (grad_norm + 1e-06))

    mlp_grad = lax.all_gather(mlp_mine.astype(NARROW), LAT_AXES, axis=0, tiled=True)

    held = mlp_momentum.reshape(2 * L * 2, rows_own, D)
    held = lax.dynamic_index_in_dim(held, lat_index, 0, keepdims=False)
    mine_new = MOMENT_KEEP * held + mlp_mine * factor
    high = lax.Precision.HIGH
    gram = plane_sum(lax.dot_general(mine_new, mine_new, (((0,), (0,)), ((), ())), precision=high))
    inverse = 1.0 / (jnp.sqrt(jnp.trace(gram)) + 1e-07)
    lead, mid, last = POLY_COEF
    square = gram * (inverse * inverse)
    mul = functools.partial(jnp.dot, precision=high)
    poly_one = mid * square + last * mul(square, square)
    turned = mul(square, poly_one)
    square_two = lead * lead * square + 2.0 * lead * turned + mul(turned, poly_one)
    poly_two = mid * square_two + last * mul(square_two, square_two)
    mine_one, mine_two = (
        lax.dynamic_slice_in_dim(now, c * (D // 2), D // 2, 0) for now in (poly_one, poly_two)
    )
    change = (lead * (mine_one + mine_two) + mul(mine_one, poly_two)) * inverse
    level_high = inverse.astype(NARROW)
    level_mid = (inverse - level_high.astype(f32)).astype(NARROW)
    level_low = (inverse - level_high.astype(f32) - level_mid.astype(f32)).astype(NARROW)
    column = jnp.arange(D)[None]
    extra = jnp.where(column == 0, level_high, jnp.where(column == 1, level_mid, level_low))
    extra = jnp.broadcast_to(extra, (8, D))
    change = change.astype(NARROW)
    packed = jnp.concatenate([change, extra], axis=0)
    packed, mlp_grad = lax.optimization_barrier((packed, mlp_grad))
    gathered = line_gather(packed)
    mlp_grad = mlp_grad.reshape(mlp_momentum.shape).astype(f32)
    momentum_new = MOMENT_KEEP * mlp_momentum + mlp_grad * factor
    clipped = flat_piece * factor
    first_new = BETA_FIRST * adam_m + (1.0 - BETA_FIRST) * clipped
    second_new = BETA_SECOND * adam_v + (1.0 - BETA_SECOND) * clipped * clipped
    count_value = float(STEP_NUM)
    first_hat = first_new / (1.0 - BETA_FIRST**count_value)
    second_hat = second_new / (1.0 - BETA_SECOND**count_value)
    adam_new = adam_params - ADAM_RATE * (
        first_hat / (jnp.sqrt(second_hat) + 1e-08) + DECAY_RATE * adam_params
    )
    gathered, momentum_new, adam_new, first_new, second_new = lax.optimization_barrier(
        (gathered, momentum_new, adam_new, first_new, second_new)
    )
    levels = jnp.sum(gathered[:, D // 2, :3].astype(f32), axis=-1)
    gathered = gathered[:, : D // 2]
    other = swap(gathered, "c")
    changes = jnp.concatenate(
        [jnp.where(c == 0, gathered, other), jnp.where(c == 0, other, gathered)], axis=1
    )
    (mlp_new,) = pl.pallas_call(
        muon_kernel,
        name="muon",
        grid=(2 * L, 2),
        out_shape=[jax.ShapeDtypeStruct((2 * L, D, D), f32)],
        in_specs=[pl.BlockSpec(memory_space=pltpu.SMEM)]
        + [pl.BlockSpec((None, rows_own, D), lambda m, h: (m, h, 0))] * 2
        + [pl.BlockSpec((None, D, D), lambda m, h: (m, 0, 0))],
        out_specs=[pl.BlockSpec((None, rows_own, D), lambda m, h: (m, h, 0))],
        compiler_params=pltpu.CompilerParams(vmem_limit_bytes=28 * 1024 * 1024),
    )(levels, momentum_new.reshape(2 * L, D, D), mlp_weights.reshape(2 * L, D, D), changes)
    mlp_new = mlp_new.reshape(mlp_weights.shape)

    return (adam_new, first_new, second_new, mlp_new, momentum_new, loss_total, grad_norm)


def solution(mesh):
    if tuple(mesh.shape.items()) == (("lat", 8), ("lon", 4)):
        fine = Mesh(mesh.devices.reshape(2, 2, 2, 2, 2), SUB_AXES)
        return placed(fast_body, fine, LAT_AXES, LON_AXES)
    return placed(body, mesh, ("lat",), ("lon",))


def placed(step, mesh, lat, lon):
    flat = P(lat + lon)
    halves = P(None, None, lon, None)
    return jax.shard_map(
        step,
        mesh=mesh,
        in_specs=(
            P(None, lat, lon, None),
            P(None, None, lat, lon, None),
            P(None, lat, lon),
            P(lat),
            flat,
            flat,
            flat,
            halves,
            halves,
        ),
        out_specs=(flat, flat, flat, halves, halves, P(), P()),
        check_vma=False,
    )
```

```python
import functools
import math

import jax
import ml_dtypes
import numpy as np
import jax.numpy as jnp
from jax import lax
from jax.experimental import pallas as pl
from jax.experimental.pallas import tpu as pltpu
from jax.sharding import Mesh
from jax.sharding import PartitionSpec as P

D = 768
FF = 3072
NB = 8
PIX = 1280
BS = 96
L = 2
STEPS = 2
NS_STEPS = 2
STEP_NUM = 5


HIGH_PREC = lax.Precision.HIGHEST
NORM_EPS = 1e-05
CLIP_LEVEL = 0.001
BETA_FIRST = 0.9
BETA_SECOND = 0.95
ADAM_RATE = 0.01
MUON_RATE = 0.8
DECAY_RATE = 0.05
MOMENT_KEEP = 0.95
POLY_COEF = (3.4445, -4.775, 2.0315)


def for_sending(value):

    def short(part):
        return part.astype(jnp.bfloat16) if part.dtype == jnp.float32 else part

    return jax.tree.map(short, value)


def with_halo(block, sides, width):
    for axis, dim in sides:
        count = lax.axis_size(axis)
        forward = [(i, i + 1) for i in range(count - 1)]
        forward.append((count - 1, 0))
        backward = [(target, source) for source, target in forward]
        low = lax.ppermute(
            lax.slice_in_dim(block, block.shape[dim] - width, None, axis=dim), axis, forward
        )
        high = lax.ppermute(lax.slice_in_dim(block, 0, width, axis=dim), axis, backward)
        block = jnp.concatenate([low, block, high], axis=dim)
    return block


def unpack(flat_params):
    layout = [
        (3, PIX, D),
        (3, D, PIX),
        (L, 2, 2, NB, BS, BS),
        (D,),
        (PIX,),
        (L, 2, 2, D),
        (L, 4, D),
        (L, FF + D),
    ]
    pieces_out = []
    offset = 0
    for dims_now in layout:
        amount = math.prod(dims_now)
        pieces_out.append(flat_params[offset : offset + amount].reshape(dims_now))
        offset = offset + amount
    return pieces_out


def along(matrix, values, axis_dim):
    if axis_dim == 1:
        return jnp.einsum("kn,bncd->bkcd", matrix, values, precision=HIGH_PREC)
    return jnp.einsum("kn,brnd->brkd", matrix, values, precision=HIGH_PREC)


def phase_table(out_count, in_count, length_all):
    out_index = jnp.arange(out_count, dtype=jnp.int32)
    in_index = jnp.arange(in_count, dtype=jnp.int32)
    phase = out_index[:, None] * in_index[None, :] % length_all
    angle = phase.astype(jnp.float32) * (2.0 * math.pi / length_all)
    scale_value = 1.0 / math.sqrt(length_all)
    return (jnp.cos(angle) * scale_value, jnp.sin(angle) * scale_value)


def combine(pieces, axis_dim, sign_value, tables, real_only):
    cosine, sine_table = tables
    values = [piece_now.astype(jnp.float32) for piece_now in pieces]
    real_out = along(cosine, values[0], axis_dim)
    if len(values) > 1:
        real_out = real_out - sign_value * along(sine_table, values[1], axis_dim)
    if real_only:
        return (real_out,)
    imag_out = sign_value * along(sine_table, values[0], axis_dim)
    if len(values) > 1:
        imag_out = imag_out + along(cosine, values[1], axis_dim)
    return (real_out, imag_out)


def turn_transform(pieces, axis_dim, sign_value, real_only):
    if axis_dim == 1:
        wide = jax.tree.map(
            lambda part, own: part.astype(own.dtype),
            lax.all_to_all(for_sending(pieces), "lat", split_axis=3, concat_axis=1, tiled=True),
            pieces,
        )
        length_all = wide[0].shape[1]
        result = combine(
            wide, 1, sign_value, phase_table(length_all, length_all, length_all), real_only
        )
        narrow = tuple((piece_now.astype(jnp.bfloat16) for piece_now in result))
        returned = jax.tree.map(
            lambda part, own: part.astype(own.dtype),
            lax.all_to_all(for_sending(narrow), "lat", split_axis=1, concat_axis=3, tiled=True),
            narrow,
        )
        return tuple((piece_now.astype(jnp.float32) for piece_now in returned))
    wide = jax.tree.map(
        lambda part, own: part.astype(own.dtype),
        lax.all_to_all(for_sending(pieces), "lon", split_axis=3, concat_axis=2, tiled=True),
        pieces,
    )
    length_all = wide[0].shape[2]
    result = combine(
        wide, 2, sign_value, phase_table(length_all, length_all, length_all), real_only
    )
    return jax.tree.map(
        lambda part, own: part.astype(own.dtype),
        lax.all_to_all(for_sending(result), "lon", split_axis=2, concat_axis=3, tiled=True),
        result,
    )


def transform(pieces, axis_dim, sign_value, real_only):
    return turn_transform(pieces, axis_dim, sign_value, real_only)


def to_low(pieces):
    return tuple((piece_now.astype(jnp.bfloat16) for piece_now in pieces))


def exact_gelu(values):
    return jax.nn.gelu(values, approximate=False)


def gelu_back(values, upstream):
    return jax.vjp(exact_gelu, values)[1](upstream)[0]


def norm_forward(inputs, gain, shift):
    center = inputs - jnp.mean(inputs, axis=-1, keepdims=True)
    inverse = lax.rsqrt(jnp.mean(center * center, axis=-1, keepdims=True) + NORM_EPS)
    scaled = center * inverse
    return (scaled * gain + shift, (scaled, inverse))


def norm_backward(upstream, saved, gain):
    scaled, inverse = saved
    g_gain = jnp.sum(upstream * scaled, axis=(0, 1, 2))
    g_shift = jnp.sum(upstream, axis=(0, 1, 2))
    g_scaled = upstream * gain
    g_input = inverse * (
        g_scaled
        - jnp.mean(g_scaled, axis=-1, keepdims=True)
        - scaled * jnp.mean(g_scaled * scaled, axis=-1, keepdims=True)
    )
    return (g_input, g_gain, g_shift)


def block_mix(pieces, weights, bias):
    shaped = [piece_now.reshape(piece_now.shape[:-1] + (NB, BS)) for piece_now in pieces]

    def multiply(left_side, right_side):
        return jnp.einsum(
            "brcni,nio->brcno", left_side, right_side, preferred_element_type=jnp.float32
        )

    real_out = multiply(shaped[0], weights[0]) - multiply(shaped[1], weights[1])
    imag_out = multiply(shaped[0], weights[1]) + multiply(shaped[1], weights[0])
    full_dims = pieces[0].shape
    return (
        real_out.reshape(full_dims) + bias[0].astype(jnp.float32),
        imag_out.reshape(full_dims) + bias[1].astype(jnp.float32),
    )


def block_back(grads_low, pieces, weights):
    shaped = [piece_now.reshape(piece_now.shape[:-1] + (NB, BS)) for piece_now in pieces]
    g_shaped = [grad_now.reshape(grad_now.shape[:-1] + (NB, BS)) for grad_now in grads_low]

    def back_multiply(grad_side, weight_side):
        return jnp.einsum(
            "brcno,nio->brcni", grad_side, weight_side, preferred_element_type=jnp.float32
        )

    def weight_multiply(input_side, grad_side):
        return jnp.einsum(
            "brcni,brcno->nio", input_side, grad_side, preferred_element_type=jnp.float32
        )

    g_real = back_multiply(g_shaped[0], weights[0]) + back_multiply(g_shaped[1], weights[1])
    g_imag = back_multiply(g_shaped[1], weights[0]) - back_multiply(g_shaped[0], weights[1])
    g_w_real = weight_multiply(shaped[0], g_shaped[0]) + weight_multiply(shaped[1], g_shaped[1])
    g_w_imag = weight_multiply(shaped[0], g_shaped[1]) - weight_multiply(shaped[1], g_shaped[0])
    g_bias = jnp.stack(
        [jnp.sum(grad_now.astype(jnp.float32), axis=(0, 1, 2)) for grad_now in grads_low]
    )
    full_dims = pieces[0].shape
    return (
        (g_real.reshape(full_dims), g_imag.reshape(full_dims)),
        jnp.stack([g_w_real, g_w_imag]),
        g_bias,
    )


def halo_rows(values):
    return with_halo(values, (("lat", 1),), 1)


def rows_conv(source_low, weight3, bias):
    padded = halo_rows(source_low)
    row_count = source_low.shape[1]
    window = jnp.concatenate(
        [padded[:, offset : offset + row_count] for offset in range(3)], axis=-1
    )
    flat_weight = weight3.reshape(-1, weight3.shape[-1])
    result = jnp.einsum("brci,io->brco", window, flat_weight, preferred_element_type=jnp.float32)
    return (result + bias.astype(jnp.float32), window)


def rows_back(grad_low, weight3, need_source):
    g_bias = jnp.sum(grad_low.astype(jnp.float32), axis=(0, 1, 2))
    if not need_source:
        return (g_bias, None)
    padded = halo_rows(grad_low)
    row_count = grad_low.shape[1]
    window_back = jnp.concatenate(
        [padded[:, 2 - offset : 2 - offset + row_count] for offset in range(3)], axis=-1
    )
    flipped = jnp.transpose(weight3, (0, 2, 1)).reshape(-1, weight3.shape[1])
    g_source = jnp.einsum("brco,oi->brci", window_back, flipped, preferred_element_type=jnp.float32)
    return (g_bias, g_source)


def conv_weight_grad(terms_list, weight3):
    window = jnp.concatenate([terms_now[0] for terms_now in terms_list], axis=0)
    grads_low = jnp.concatenate([terms_now[1] for terms_now in terms_list], axis=0)
    return jnp.einsum(
        "brci,brco->io", window, grads_low, preferred_element_type=jnp.float32
    ).reshape(weight3.shape)


def layer_forward(state, params_now):
    spec_w, spec_b, norm_vals, mlp_pair, mlp_bias = params_now
    normed, first_saved = norm_forward(state, norm_vals[0], norm_vals[1])
    spectrum = transform((normed.astype(jnp.bfloat16),), 2, -1.0, False)
    spectrum = transform(to_low(spectrum), 1, -1.0, False)
    mixed_in = to_low(spectrum)
    inner = block_mix(mixed_in, spec_w[0], spec_b[0])
    activated = to_low(tuple((exact_gelu(piece_now) for piece_now in inner)))
    outer = block_mix(activated, spec_w[1], spec_b[1])
    spectrum = transform(to_low(outer), 1, 1.0, False)
    spatial = transform(to_low(spectrum), 2, 1.0, True)[0]
    mixed = state + spatial + normed
    second, second_saved = norm_forward(mixed, norm_vals[2], norm_vals[3])
    hidden_in = second.astype(jnp.bfloat16)
    before = (
        jnp.einsum("brcd,fd->brcf", hidden_in, mlp_pair[0], preferred_element_type=jnp.float32)
        + mlp_bias[:FF]
    )
    hidden = exact_gelu(before).astype(jnp.bfloat16)
    result = (
        jnp.einsum("brcf,fd->brcd", hidden, mlp_pair[1], preferred_element_type=jnp.float32)
        + mlp_bias[FF:]
    )
    return (
        mixed + result,
        (first_saved, mixed_in, inner, activated, second_saved, hidden_in, before, hidden),
    )


def layer_backward(upstream, cache, params_now):
    spec_w, spec_b, norm_vals, mlp_pair, mlp_bias = params_now
    first_saved, mixed_in, inner, activated, second_saved, hidden_in, before, hidden = cache
    grad_out = upstream.astype(jnp.bfloat16)
    g_down_bias = jnp.sum(grad_out.astype(jnp.float32), axis=(0, 1, 2))
    g_hidden = jnp.einsum(
        "brcd,fd->brcf", grad_out, mlp_pair[1], preferred_element_type=jnp.float32
    )
    g_before = gelu_back(before, g_hidden).astype(jnp.bfloat16)
    g_up_bias = jnp.sum(g_before.astype(jnp.float32), axis=(0, 1, 2))
    g_second = jnp.einsum(
        "brcf,fd->brcd", g_before, mlp_pair[0], preferred_element_type=jnp.float32
    )
    g_norm_in, g_gain_two, g_shift_two = norm_backward(g_second, second_saved, norm_vals[2])
    g_mixed = upstream + g_norm_in
    g_spectrum = transform((g_mixed.astype(jnp.bfloat16),), 2, -1.0, False)
    g_outer = to_low(transform(to_low(g_spectrum), 1, -1.0, False))
    g_activated, g_w_outer, g_b_outer = block_back(g_outer, activated, spec_w[1])
    g_inner = to_low(
        tuple((gelu_back(piece_now, grad_now) for piece_now, grad_now in zip(inner, g_activated)))
    )
    g_mixed_in, g_w_inner, g_b_inner = block_back(g_inner, mixed_in, spec_w[0])
    g_spectrum = transform(to_low(g_mixed_in), 1, 1.0, False)
    g_normed = transform(to_low(g_spectrum), 2, 1.0, True)[0] + g_mixed
    g_state_norm, g_gain_one, g_shift_one = norm_backward(g_normed, first_saved, norm_vals[0])
    layer_grads = (
        jnp.stack([g_w_inner, g_w_outer]),
        jnp.stack([g_b_inner, g_b_outer]),
        jnp.stack([g_gain_one, g_shift_one, g_gain_two, g_shift_two]),
        jnp.concatenate([g_up_bias, g_down_bias]),
    )
    return (g_mixed + g_state_norm, layer_grads, (hidden, grad_out, g_before, hidden_in))


def body(pixels, targets, mask, lat_rows, adam_params, adam_m, adam_v, mlp_weights, mlp_momentum):
    flat_low = lax.all_gather(adam_params.astype(jnp.bfloat16), ("lat", "lon"), axis=0, tiled=True)
    mlp_low = lax.all_gather(mlp_weights.astype(jnp.bfloat16), "lon", axis=2, tiled=True)
    embed_w, head_w, spec_w, embed_b, head_b, spec_b, norm_params, mlp_b = unpack(flat_low)
    row_count = pixels.shape[1]
    lat_total = lax.axis_size("lat") * row_count
    row_weight = jnp.sin(math.pi * (lat_rows.astype(jnp.float32) + 0.5) / lat_total)
    weight_map = row_weight[None, :, None] * mask.astype(jnp.float32)
    weight_sum = lax.psum(jnp.sum(weight_map), ("lat", "lon"))
    loss_scale = 2.0 / (STEPS * PIX * weight_sum)

    def params_at(depth_idx):
        return (
            spec_w[depth_idx],
            spec_b[depth_idx],
            norm_params[depth_idx].astype(jnp.float32),
            mlp_low[depth_idx],
            mlp_b[depth_idx].astype(jnp.float32),
        )

    current = pixels
    saved_steps = []
    loss_local = jnp.zeros((), jnp.float32)
    for roll_idx in range(STEPS):
        state, embed_window = rows_conv(current.astype(jnp.bfloat16), embed_w, embed_b)
        caches = []
        for depth_idx in range(L):
            state, cache_now = layer_forward(state, params_at(depth_idx))
            caches.append(cache_now)
        predicted, head_window = rows_conv(state.astype(jnp.bfloat16), head_w, head_b)
        differ = predicted - targets[roll_idx].astype(jnp.float32)
        loss_local = loss_local + jnp.sum(weight_map[..., None] * differ * differ)
        saved_steps.append(
            (embed_window, caches, head_window, weight_map[..., None] * differ * loss_scale)
        )
        current = predicted
    g_embed_b = jnp.zeros(embed_b.shape, jnp.float32)
    g_head_b = jnp.zeros(head_b.shape, jnp.float32)
    head_terms = []
    embed_terms = []
    mlp_terms = [[] for unused in range(L)]
    g_layers = [None] * L
    carried = None
    for roll_idx in reversed(range(STEPS)):
        embed_window, caches, head_window, loss_grad = saved_steps[roll_idx]
        upstream = loss_grad if carried is None else loss_grad + carried
        upstream_low = upstream.astype(jnp.bfloat16)
        head_terms.append((head_window, upstream_low))
        grad_b, grad_state = rows_back(upstream_low, head_w, True)
        g_head_b = g_head_b + grad_b
        for depth_idx in reversed(range(L)):
            grad_state, layer_grads, mlp_now = layer_backward(
                grad_state, caches[depth_idx], params_at(depth_idx)
            )
            mlp_terms[depth_idx].append(mlp_now)
            if g_layers[depth_idx] is None:
                g_layers[depth_idx] = layer_grads
            else:
                g_layers[depth_idx] = jax.tree.map(jnp.add, g_layers[depth_idx], layer_grads)
        state_low = grad_state.astype(jnp.bfloat16)
        embed_terms.append((embed_window, state_low))
        grad_b, carried = rows_back(state_low, embed_w, roll_idx > 0)
        g_embed_b = g_embed_b + grad_b
    g_embed_w = conv_weight_grad(embed_terms, embed_w)
    g_head_w = conv_weight_grad(head_terms, head_w)
    mlp_grads = []
    for depth_idx in range(L):
        joined = [
            jnp.concatenate([terms_now[member] for terms_now in mlp_terms[depth_idx]], axis=0)
            for member in range(4)
        ]
        g_up = jnp.einsum("brcf,brcd->fd", joined[2], joined[3], preferred_element_type=jnp.float32)
        g_down = jnp.einsum(
            "brcf,brcd->fd", joined[0], joined[1], preferred_element_type=jnp.float32
        )
        mlp_grads.append(jnp.stack([g_up, g_down]))
    full_mlp = jnp.stack(mlp_grads)
    stacked = [
        jnp.stack([g_layers[depth_idx][member] for depth_idx in range(L)]) for member in range(4)
    ]
    flat_grad = jnp.concatenate(
        [
            g_embed_w.reshape(-1),
            g_head_w.reshape(-1),
            stacked[0].reshape(-1),
            g_embed_b,
            g_head_b,
            stacked[1].reshape(-1),
            stacked[2].reshape(-1),
            stacked[3].reshape(-1),
        ]
    )
    lon_count = lax.axis_size("lon")
    lat_count = lax.axis_size("lat")
    dev_count = lon_count * lat_count
    per_block = full_mlp.shape[2] // dev_count
    mlp_rows = (
        full_mlp.reshape(L, 2, lon_count, lat_count, per_block, D)
        .transpose(3, 2, 0, 1, 4, 5)
        .reshape(dev_count, -1)
    )
    flat_rows = flat_grad.reshape(dev_count, -1)
    flat_width = flat_rows.shape[1]
    summed = lax.psum_scatter(
        jnp.concatenate([flat_rows, mlp_rows], axis=1),
        ("lat", "lon"),
        scatter_dimension=0,
        tiled=True,
    )[0]
    flat_piece = summed[:flat_width]
    mlp_piece = summed[flat_width:].reshape(L, 2, per_block, D)
    local_square = jnp.sum(flat_piece * flat_piece) + jnp.sum(mlp_piece * mlp_piece)
    loss_total, square_sum = lax.psum(
        (loss_local / (STEPS * PIX * weight_sum), local_square), ("lat", "lon")
    )
    mlp_grad = lax.all_gather(mlp_piece.astype(jnp.bfloat16), "lat", axis=2, tiled=True).astype(
        mlp_piece.dtype
    )
    grad_norm = jnp.sqrt(square_sum)
    factor = jnp.minimum(1.0, CLIP_LEVEL / (grad_norm + 1e-06))
    clipped = flat_piece * factor
    first_new = BETA_FIRST * adam_m + (1.0 - BETA_FIRST) * clipped
    second_new = BETA_SECOND * adam_v + (1.0 - BETA_SECOND) * clipped * clipped
    count_value = float(STEP_NUM)
    first_hat = first_new / (1.0 - BETA_FIRST**count_value)
    second_hat = second_new / (1.0 - BETA_SECOND**count_value)
    adam_new = adam_params - ADAM_RATE * (
        first_hat / (jnp.sqrt(second_hat) + 1e-08) + DECAY_RATE * adam_params
    )
    momentum_new = MOMENT_KEEP * mlp_momentum + mlp_grad * factor
    ortho = momentum_new
    for ns_idx in range(NS_STEPS):
        partial_gram = jnp.einsum("lkfd,lkfe->lkde", ortho, ortho, precision=HIGH_PREC)
        square = lax.psum(partial_gram.astype(jnp.bfloat16), "lon").astype(jnp.float32)
        if ns_idx == 0:
            trace_val = jnp.trace(square, axis1=2, axis2=3)
            inverse = 1.0 / (jnp.sqrt(trace_val) + 1e-07)
            ortho = ortho * inverse[:, :, None, None]
            square = square * (inverse * inverse)[:, :, None, None]
        poly = POLY_COEF[1] * square + POLY_COEF[2] * jnp.einsum(
            "lkde,lkef->lkdf", square, square, precision=HIGH_PREC
        )
        ortho = POLY_COEF[0] * ortho + jnp.einsum(
            "lkfd,lkde->lkfe", ortho, poly, precision=HIGH_PREC
        )
    mlp_new = mlp_weights * (1.0 - MUON_RATE * DECAY_RATE) - MUON_RATE * (FF / D) ** 0.5 * ortho
    return (adam_new, first_new, second_new, mlp_new, momentum_new, loss_total, grad_norm)


ROWS = 48
COLS = 48
GROUP = 16
OWN = 3
TOK = ROWS * OWN
HALF_TOK = TOK // 2
PAIRS = 12
LANES = 128
WIDE = NB * LANES
FREQ = PAIRS * 96
NARROW = jnp.bfloat16
WINDOW = 212
MLP_LIMIT = 26
WINDOW_CUTS = (0, 72, 142, WINDOW)
MLP_CUTS = (0, 128, 256, 384)
EMBED_AT = 2
Z_AXES = ("zh", "zl")
EMBED_SIZE = 3 * PIX * D
SUB_AXES = ("zh", "zl", "x", "y", "c")
LAT_AXES = ("zh", "zl", "x")
LON_AXES = ("y", "c")
ITEM_AXES = ("zl", "x", "y", "c")


def shift_tables():
    table = np.zeros((3, TOK, TOK), np.float32)
    spots = np.arange(TOK)
    for offset in range(3):
        table[offset, spots, (spots + OWN * (offset - 1)) % TOK] = 1.0
    return table


def row_table():
    table = np.zeros((TOK, TOK), np.float64)
    rows = np.arange(ROWS)
    for pair in range(2 * PAIRS):
        if pair == 0:
            waves = (np.ones(ROWS), np.cos(np.pi * rows))
        else:
            angle = 2.0 * np.pi * (pair * rows % ROWS) / ROWS
            waves = (np.cos(angle), np.sin(angle))
        for part in range(2):
            for own in range(OWN):
                table[pair * 6 + part * OWN + own, rows * OWN + own] = waves[part]
    return table / math.sqrt(ROWS)


def column_tables():
    freq = np.arange(COLS)[:, None]
    table = np.zeros((2, 192, 128), np.float64)
    for source in range(GROUP):
        quad, lon = source // 4, source % 4
        for own in range(OWN):
            column = lon * 12 + quad * OWN + own
            angle = 2.0 * np.pi * (freq[:, 0] * column % COLS) / COLS
            cosine, sine = np.cos(angle), np.sin(angle)
            first, second = source * 8 + own, source * 8 + OWN + own
            table[0, 0:48, first] = cosine
            table[0, 96:144, first] = -sine
            table[0, 48:96, second] = cosine
            table[0, 144:192, second] = -sine
            table[1, 0:48, first] = cosine
            table[1, 48:96, first] = cosine
            table[1, 96:144, first] = -sine
            table[1, 144:192, first] = -sine
            table[1, 0:48, second] = -sine
            table[1, 48:96, second] = sine
            table[1, 96:144, second] = -cosine
            table[1, 144:192, second] = cosine
    return table / math.sqrt(COLS)


def spread_table():
    table = np.zeros((384, 512), np.float32)
    spots = np.arange(384)
    table[spots, spots // BS * LANES + spots % BS] = 1.0
    return table


def two_terms(table):
    high = table.astype(ml_dtypes.bfloat16)
    low = (table - high.astype(np.float64)).astype(ml_dtypes.bfloat16)
    return np.stack([high, low])


def dot(left, right):
    return lax.dot_general(left, right, (((1,), (0,)), ((), ())), preferred_element_type=jnp.float32)


def dot_nt(left, right):
    return lax.dot_general(left, right, (((1,), (1,)), ((), ())), preferred_element_type=jnp.float32)


def dot_tn(left, right):
    return lax.dot_general(left, right, (((0,), (0,)), ((), ())), preferred_element_type=jnp.float32)


def normalize(values):
    center = values - jnp.mean(values, axis=-1, keepdims=True)
    inverse = lax.rsqrt(jnp.mean(center * center, axis=-1, keepdims=True) + NORM_EPS)
    return center * inverse, inverse


def normalize_back(upstream, scaled, inverse, gain):
    inner = upstream * gain
    return inverse * (
        inner
        - jnp.mean(inner, axis=-1, keepdims=True)
        - scaled * jnp.mean(inner * scaled, axis=-1, keepdims=True)
    )


def column_sum(values):
    return jnp.sum(values, axis=0, keepdims=True)


def bell(values):
    return 0.5 * (1.0 + lax.erf(values * math.sqrt(0.5)))


def bell_slope(values, area):
    return area + values * jnp.exp(-0.5 * values * values) * (1.0 / math.sqrt(2.0 * math.pi))


def send_rows(low, spread_ref, row_ref, out_ref):
    wide = jnp.concatenate(
        [dot(low[:, :384], spread_ref[...]), dot(low[:, 384:], spread_ref[...])], axis=1
    ).astype(NARROW)
    turned = dot(row_ref[0], wide) + dot(row_ref[1], wide)
    for side in range(2):
        for block in range(NB):
            out_ref[side * NB + block] = turned[
                side * HALF_TOK : (side + 1) * HALF_TOK, block * LANES : (block + 1) * LANES
            ].astype(NARROW)


def take_rows(in_ref, spread_ref, row_back_ref):
    sides = []
    for side in range(2):
        sides.append(
            jnp.concatenate(
                [in_ref[side * NB + block].astype(jnp.float32) for block in range(NB)], axis=1
            )
        )
    wide = jnp.concatenate(sides, axis=0).astype(NARROW)
    low = jnp.concatenate(
        [dot_nt(wide[:, :512], spread_ref[...]), dot_nt(wide[:, 512:], spread_ref[...])], axis=1
    ).astype(NARROW)
    return dot(row_back_ref[0], low) + dot(row_back_ref[1], low)


def fetch(sources, held_ref, sems):
    copies = [pltpu.make_async_copy(src, held_ref.at[i], sems.at[i]) for i, src in enumerate(sources)]
    for copy in copies:
        copy.start()
    return copies


def thirds(w_ref, size):
    return [w_ref[i * size : (i + 1) * size] for i in range(3)]


def embed_kernel(src_ref, shift_ref, bias_ref, norm_ref, spread_ref, row_ref, w_ref,
                 state_ref, send_ref):
    src = src_ref[...]
    state = bias_ref[...]
    for offset, weight in enumerate(thirds(w_ref, PIX)):
        moved = src if offset == 1 else dot(shift_ref[offset], src).astype(NARROW)
        state = state + dot(moved, weight)
    state_ref.put(state)
    scaled, _unused = normalize(state)
    normed = scaled * norm_ref[0:1] + norm_ref[1:2]
    send_rows(normed.astype(NARROW), spread_ref, row_ref, send_ref)


def turn_columns(wide_ref, col_ref, pair):
    kind = 0 if pair == 0 else 1
    low = wide_ref[:, 6 * pair : 6 * pair + 8, :].reshape(128, 128).astype(NARROW)
    both = dot(col_ref[0, kind], low) + dot(col_ref[1, kind], low)
    return jnp.concatenate([both[:96], both[96:]], axis=1).astype(NARROW)


def back_columns(wide_ref, col_back_ref, pair, low):
    kind = 0 if pair == 0 else 1
    both = jnp.concatenate([low[:, :128], low[:, 128:]], axis=0)
    back = dot(col_back_ref[0, kind], both) + dot(col_back_ref[1, kind], both)
    wide_ref[:, 6 * pair : 6 * pair + 8, :] = back.reshape(16, 8, 128)


def spec_kernel(
    in_ref, col_ref, col_back_ref, w_ref, b_ref, out_ref, mixed_ref, wide_ref, wide_out_ref
):
    wide_ref[:, :HALF_TOK, :] = in_ref[...].astype(jnp.float32)
    wide_ref[:, HALF_TOK:, :] = jnp.zeros((16, 8, 128), jnp.float32)
    for chunk in range(4):
        pairs = range(chunk * 3, chunk * 3 + 3)
        mixed = jnp.concatenate([turn_columns(wide_ref, col_ref, pair) for pair in pairs], axis=0)
        mixed_ref.put(mixed, slice(chunk * 288, (chunk + 1) * 288), slice(None))
        inner = dot(mixed, w_ref[0]) + b_ref[0:1]
        act = (inner * bell(inner)).astype(NARROW)
        outer = (dot(act, w_ref[1]) + b_ref[1:2]).astype(NARROW)
        for place, pair in enumerate(pairs):
            back_columns(wide_out_ref, col_back_ref, pair, outer[place * 96 : place * 96 + 96])
    out_ref[...] = wide_out_ref[:, :HALF_TOK, :].astype(NARROW)


def spec_back_kernel(
    in_ref, col_ref, col_back_ref, w_ref, b_ref, mixed_ref,
    out_ref, gw_ref, gb_ref, wide_ref, wide_out_ref,
):
    wide_ref[:, :HALF_TOK, :] = in_ref[...].astype(jnp.float32)
    wide_ref[:, HALF_TOK:, :] = jnp.zeros((16, 8, 128), jnp.float32)
    for chunk in range(4):
        pairs = range(chunk * 3, chunk * 3 + 3)
        g_outer = jnp.concatenate([turn_columns(wide_ref, col_ref, pair) for pair in pairs], axis=0)
        mixed = mixed_ref()[chunk * 288 : (chunk + 1) * 288, :]
        inner = dot(mixed, w_ref[0]) + b_ref[0:1]
        area = bell(inner)
        act = (inner * area).astype(NARROW)
        g_inner = (bell_slope(inner, area) * dot_nt(g_outer, w_ref[1])).astype(NARROW)
        g_mixed = dot_nt(g_inner, w_ref[0]).astype(NARROW)
        first, second = dot_tn(mixed, g_inner), dot_tn(act, g_outer)
        sums = jnp.concatenate(
            [column_sum(g_inner.astype(jnp.float32)), column_sum(g_outer.astype(jnp.float32))], axis=0
        )
        if chunk == 0:
            gw_ref[0], gw_ref[1], gb_ref[...] = first, second, sums
        else:
            gw_ref[0] += first
            gw_ref[1] += second
            gb_ref[...] += sums
        for place, pair in enumerate(pairs):
            back_columns(wide_out_ref, col_back_ref, pair, g_mixed[place * 96 : place * 96 + 96])
    out_ref[...] = wide_out_ref[:, :HALF_TOK, :].astype(NARROW)


def mlp_kernel(has_next, in_ref, state_ref, norm_ref, next_norm_ref, up_b_ref, down_b_ref,
               spread_ref, row_ref, row_back_ref, w0_ref, w1_ref, w2_ref, w3_ref, *rest):
    held_ref, sems = rest[-2:]
    mixed_ref, hidden_in_ref, before_ref, hidden_ref, out_ref = rest[:5]
    copies = fetch((w0_ref, w1_ref, w2_ref, w3_ref), held_ref, sems)
    spatial = take_rows(in_ref, spread_ref, row_back_ref)
    state = state_ref()[...]
    scaled, _unused = normalize(state)
    mixed = state + spatial + (scaled * norm_ref[0:1] + norm_ref[1:2])
    mixed_ref.put(mixed)
    again, _unused = normalize(mixed)
    hidden_in = (again * norm_ref[2:3] + norm_ref[3:4]).astype(NARROW)
    hidden_in_ref.put(hidden_in)
    out = mixed + down_b_ref[...]
    for part in range(4):
        spot = slice(part * D, (part + 1) * D)
        copies[part].wait()
        before = dot_nt(hidden_in, held_ref[part, 0]) + up_b_ref[:, spot]
        before_ref.put(before, slice(None), spot)
        hidden = (before * bell(before)).astype(NARROW)
        hidden_ref.put(hidden, slice(None), spot)
        out = out + dot(hidden, held_ref[part, 1])
    out_ref.put(out)
    if has_next:
        scaled, _unused = normalize(out)
        normed = scaled * next_norm_ref[0:1] + next_norm_ref[1:2]
        send_rows(normed.astype(NARROW), spread_ref, row_ref, rest[5])


def head_kernel(state_ref, shift_ref, bias_ref, target_ref, weight_ref, w_ref,
                low_ref, pred_ref, grad_ref, loss_ref):
    low = state_ref()[...].astype(NARROW)
    low_ref.put(low)
    predicted = bias_ref[...]
    for offset, weight in enumerate(thirds(w_ref, D)):
        moved = low if offset == 1 else dot(shift_ref[offset], low).astype(NARROW)
        predicted = predicted + dot(moved, weight)
    pred_ref[...] = predicted.astype(NARROW)
    differ = predicted - target_ref()[...].astype(jnp.float32)
    grad_ref.put(weight_ref[:, 1:2] * differ)
    loss_ref[...] = column_sum(weight_ref[:, 0:1] * differ * differ)


def head_back_kernel(grad_ref, shift_ref, w_ref, low_ref, sum_ref, out_ref):
    low = grad_ref()[...].astype(NARROW)
    low_ref.put(low)
    sum_ref[...] = column_sum(low.astype(jnp.float32))
    total = None
    for offset, weight in enumerate(thirds(w_ref, D)):
        moved = low if offset == 1 else dot(shift_ref[2 - offset], low).astype(NARROW)
        part = dot_nt(moved, weight)
        total = part if total is None else total + part
    out_ref[...] = total


def embed_back_kernel(low_ref, shift_ref, add_ref, w_ref, out_ref):
    low = low_ref[...]
    total = None
    for offset, weight in enumerate(thirds(w_ref, PIX)):
        moved = low if offset == 1 else dot(shift_ref[2 - offset], low).astype(NARROW)
        part = dot_nt(moved, weight)
        total = part if total is None else total + part
    out_ref.put(add_ref()[...] + total)


def mlp_back_kernel(up_ref, before_ref, mixed_ref, norm_ref, spread_ref, row_ref,
                    w0_ref, w1_ref, w2_ref, w3_ref,
                    grad_out_ref, g_before_ref, g_mixed_ref, g_up_b_ref, sums_ref, send_ref,
                    held_ref, sems):
    copies = fetch((w0_ref, w1_ref, w2_ref, w3_ref), held_ref, sems)
    upstream = up_ref[...]
    grad_out = upstream.astype(NARROW)
    grad_out_ref.put(grad_out)
    sums_ref[0:1] = column_sum(grad_out.astype(jnp.float32))
    g_second = None
    for part in range(4):
        spot = slice(part * D, (part + 1) * D)
        before = before_ref()[:, spot]
        slope = bell_slope(before, bell(before))
        copies[part].wait()
        g_before = (slope * dot_nt(grad_out, held_ref[part, 1])).astype(NARROW)
        g_before_ref.put(g_before, slice(None), spot)
        g_up_b_ref[:, spot] = column_sum(g_before.astype(jnp.float32))
        now = dot(g_before, held_ref[part, 0])
        g_second = now if g_second is None else g_second + now
    scaled, inverse = normalize(mixed_ref()[...])
    sums_ref[1:2] = column_sum(g_second * scaled)
    sums_ref[2:3] = column_sum(g_second)
    g_mixed = upstream + normalize_back(g_second, scaled, inverse, norm_ref[2:3])
    g_mixed_ref.put(g_mixed)
    send_rows(g_mixed.astype(NARROW), spread_ref, row_ref, send_ref)


def norm_back_kernel(in_ref, g_mixed_ref, state_ref, norm_ref, spread_ref, row_back_ref,
                     out_ref, low_ref, sums_ref):
    g_normed = take_rows(in_ref, spread_ref, row_back_ref)
    g_mixed = g_mixed_ref()[...]
    g_normed = g_normed + g_mixed
    scaled, inverse = normalize(state_ref()[...])
    out = g_mixed + normalize_back(g_normed, scaled, inverse, norm_ref[0:1])
    out_ref[...] = out
    low = out.astype(NARROW)
    low_ref[...] = low
    sums_ref[0:1] = column_sum(g_normed * scaled)
    sums_ref[1:2] = column_sum(g_normed)
    sums_ref[2:3] = column_sum(low.astype(jnp.float32))


def narrow_kernel(place_ref, in_ref, out_ref):
    out_ref[...] = in_ref[...].astype(NARROW)


def own_quarters(weights, depth, place):
    size = weights.shape[2] // 4

    def from_spot(m, q, place_ref):
        return (depth, m, (q // 2 + place_ref[0]) % 2 * 2 + q % 2, 0)

    return pl.pallas_call(
        narrow_kernel,
        name="narrow",
        out_shape=jax.ShapeDtypeStruct((2, 2, 2, size, D), NARROW),
        grid_spec=pltpu.PrefetchScalarGridSpec(
            num_scalar_prefetch=1,
            grid=(2, 4),
            in_specs=[pl.BlockSpec((None, None, size, D), from_spot)],
            out_specs=pl.BlockSpec(
                (None, None, None, size, D), lambda m, q, place_ref: (m, q // 2, q % 2, 0, 0)
            ),
        ),
    )(place, weights)


def muon_kernel(level_ref, momentum_ref, weight_ref, change_ref, out_ref):
    momentum = momentum_ref[...]
    ortho = POLY_COEF[0] * POLY_COEF[0] * level_ref[pl.program_id(0)] * momentum
    ortho = ortho + dot(momentum.astype(NARROW), change_ref[...])
    out_ref[...] = weight_ref[...] * (1.0 - MUON_RATE * DECAY_RATE) - MUON_RATE * (FF / D) ** 0.5 * ortho


class Coming:
    def __init__(self, far_ref, held_ref, sem):
        self.held, self.copy = held_ref, pltpu.make_async_copy(far_ref, held_ref, sem)
        self.copy.start()

    def __call__(self):
        if self.copy is not None:
            self.copy.wait()
        self.copy = None
        return self.held


class Going:
    def __init__(self, far_ref, held_ref, sems):
        self.far, self.held, self.sems, self.copies = far_ref, held_ref, sems, []

    def put(self, value, *spot):
        if spot:
            self.held[spot] = value
            source, target = self.held.at[spot], self.far.at[spot]
        else:
            self.held[...] = value
            source, target = self.held, self.far
        copy = pltpu.make_async_copy(source, target, self.sems.at[len(self.copies)])
        copy.start()
        self.copies.append(copy)


PIECES = 4


def launch(kernel, name, out_dims, operands, far=(), far_out=False, near=(), scratch=(), limit=16,
           coming=(), going=()):
    anywhere = pl.BlockSpec(memory_space=pltpu.HBM)
    local = pl.BlockSpec(memory_space=pltpu.VMEM)
    in_specs = []
    for i in range(len(operands)):
        if i in near:
            in_specs.append(pl.BlockSpec(memory_space=pltpu.SMEM))
        else:
            in_specs.append(anywhere if i in far or i in coming else local)
    sem = pltpu.SemaphoreType.DMA
    staged = [pltpu.VMEM(operands[i].shape, operands[i].dtype) for i in coming]
    staged += [pltpu.VMEM(*out_dims[i]) for i in going]
    staged += [sem((len(coming),))] * bool(coming) + [sem((PIECES,))] * len(going)
    ins, outs = len(operands), len(out_dims)

    def body(*refs):
        refs, rest = list(refs[: ins + outs]), refs[ins + outs :]
        held, rest = rest[: len(staged)], rest[len(staged) :]
        tail = len(coming) + len(going)
        for number, i in enumerate(coming):
            refs[i] = Coming(refs[i], held[number], held[tail].at[number])
        sent = []
        for number, i in enumerate(going):
            sems = held[tail + bool(coming) + number]
            refs[ins + i] = Going(refs[ins + i], held[len(coming) + number], sems)
            sent.append(refs[ins + i])
        kernel(*refs, *rest)
        for way in sent:
            for copy in way.copies:
                copy.wait()

    operands = [
        pltpu.with_memory_space_constraint(a, pltpu.HBM) if i in far or i in coming else a
        for i, a in enumerate(operands)
    ]
    out_shape = [
        pltpu.HBM(*dims) if far_out or i in going else jax.ShapeDtypeStruct(*dims)
        for i, dims in enumerate(out_dims)
    ]
    return pl.pallas_call(
        body,
        name=name,
        out_shape=out_shape,
        in_specs=in_specs,
        out_specs=[anywhere if far_out or i in going else local for i in range(outs)],
        scratch_shapes=staged + list(scratch),
        compiler_params=pltpu.CompilerParams(vmem_limit_bytes=limit * 1024 * 1024),
    )(*operands)


def exchange(values):
    return lax.all_to_all(values, ITEM_AXES, split_axis=0, concat_axis=0, tiled=True)


def total_over(values, axes):
    count = lax.axis_size(axes)
    spread = jnp.broadcast_to(jnp.pad(values, (0, LANES - values.shape[0])), (count, 1, LANES))
    got = lax.all_to_all(spread, axes, split_axis=0, concat_axis=0, tiled=True)
    return jnp.sum(got, axis=(0, 1))[: values.shape[0]]


KINDS = {"embed": (D, 6), "head": (PIX, 10), "rest": (LANES, 1)}


def kind_ranges(total):
    edges = (0, EMBED_SIZE, 2 * EMBED_SIZE, total)
    return dict(zip(KINDS, zip(edges[:-1], edges[1:])))


def window_pieces(index, width, total):
    found = []
    for kind, (low, high) in kind_ranges(total).items():
        begin, end = max(index * width, low), min((index + 1) * width, high)
        if begin >= end:
            continue
        row, tiles = KINDS[kind]
        first = (begin - low) // (8 * row)
        last = -(-(end - low) // (8 * row))
        found.append([kind, first, last, 0, begin, end])
    spot = {"embed": EMBED_AT, "head": 0, "rest": 0}
    kinds = [piece[0] for piece in found]
    for piece in found:
        piece[3] = spot[piece[0]]
    if kinds == ["embed", "head"]:
        used = (found[1][2] - found[1][1]) * 10
        found[0][3] = EMBED_AT + -(-(used - EMBED_AT) // 6) * 6
    if kinds == ["head", "rest"]:
        found[1][3] = (found[0][2] - found[0][1]) * 10
    for piece in found:
        assert piece[3] + (piece[2] - piece[1]) * KINDS[piece[0]][1] <= WINDOW
    return found


def form_range(kind, device, width, total, count):
    row, tiles = KINDS[kind]
    base, edge = kind_ranges(total)[kind]
    origin = device * width
    low = jnp.clip(base - origin, 0, width)
    high = jnp.clip(edge - origin, 0, width)
    inside = jnp.maximum(origin - base, 0)
    start = inside % (8 * row) - low
    first = EMBED_AT if kind == "embed" else 0
    for index in range(count):
        for piece in window_pieces(index, width, total):
            if piece[0] == kind and piece[3] != first:
                start = start + jnp.where(device == index, (piece[3] - first) * 8 * LANES, 0)
    return start, low, high


def form_tiles(kind):
    if kind == "embed":
        return EMBED_AT, (WINDOW - EMBED_AT) // 6
    return (0, WINDOW // 10) if kind == "head" else (0, WINDOW)


def own_window(own, device, width, total, count):
    spot = jnp.arange(width, dtype=jnp.int32)
    window = jnp.zeros((WINDOW, 8, LANES), jnp.float32)
    for kind, (row, tiles) in KINDS.items():
        start, low, high = form_range(kind, device, width, total, count)
        first, groups = form_tiles(kind)
        length = groups * tiles * 8 * LANES
        held = jnp.where((spot >= low) & (spot < high), own, 0.0)
        held = jnp.pad(held, (length, length))
        form = lax.dynamic_slice(held, (length - start,), (length,))
        form = form.reshape(groups, 8, tiles, LANES).transpose(0, 2, 1, 3).reshape(-1, 8, LANES)
        window = window + jnp.pad(form, ((first, WINDOW - first - groups * tiles), (0, 0), (0, 0)))
    return window


def own_range(window, device, width, total, count):
    spot = jnp.arange(width, dtype=jnp.int32)
    result = jnp.zeros((width,), jnp.float32)
    for kind, (row, tiles) in KINDS.items():
        start, low, high = form_range(kind, device, width, total, count)
        first, groups = form_tiles(kind)
        form = window[first : first + groups * tiles].reshape(groups, tiles, 8, LANES)
        form = jnp.pad(form.transpose(0, 2, 1, 3).reshape(-1), (width, width))
        held = lax.dynamic_slice(form, (width + start,), (width,))
        result = jnp.where((spot >= low) & (spot < high), held, result)
    return result


def gather_windows(own, *early):
    value, *early = lax.optimization_barrier((jnp.stack([own, swap(own, "zh")]), *early))
    thirds = []
    ways = ["x", "y", "zl"]
    for i in range(3):
        part = value[:, WINDOW_CUTS[i] : WINDOW_CUTS[i + 1]]
        for axis in ways[i:] + ways[:i]:
            part = jnp.stack([part, swap(part, axis)])
        thirds.append((part, swap(part, "c")))
    return thirds, *early


def join_plan(kind, width, total, count):
    tiles = KINDS[kind][1]
    pieces = []
    for index in range(count):
        for piece in window_pieces(index, width, total):
            if piece[0] == kind:
                pieces.append((index, piece[1] * tiles, piece[2] * tiles, piece[3]))
    single, double = [], []
    for spot, (index, first, last, tile) in enumerate(pieces):
        begin, end = first, last
        if spot and pieces[spot - 1][2] > first:
            before, before_first, begin, before_tile = pieces[spot - 1]
            double.append((first, begin - first, before, before_tile + first - before_first, index, tile))
        if spot + 1 < len(pieces):
            end = min(last, pieces[spot + 1][1])
        if begin < end:
            single.append((begin, end - begin, index, tile + begin - first))
    return single, double


def by_thirds(size, tile):
    found = []
    for third in range(3):
        begin, end = max(tile, WINDOW_CUTS[third]), min(tile + size, WINDOW_CUTS[third + 1])
        if begin < end:
            found.append((third, begin - WINDOW_CUTS[third], end - begin, begin - tile))
    return found


def join_kernel(single, double, place_ref, *refs):
    sources, (out_ref, left_ref, right_ref, sems) = refs[:6], refs[6:]
    own = [place_ref[i] for i in range(5)]
    count = 0

    def start(index, size, tile, target_ref, at):
        nonlocal count
        rel = {
            axis: (index // unit + spot) % 2
            for axis, unit, spot in zip(SUB_AXES, (16, 8, 4, 2, 1), own)
        }
        ways = ["x", "y", "zl"]
        ends = []
        for third, begin, amount, offset in by_thirds(size, tile):
            spots = [rel[axis] for axis in (ways[third:] + ways[:third])[::-1]] + [rel["zh"]]
            sources_now = sources[2 * third : 2 * third + 2]
            copies = [
                pltpu.make_async_copy(
                    ref.at[(*spots, pl.ds(begin, amount))],
                    target_ref.at[pl.ds(at + offset, amount)],
                    sems.at[count],
                )
                for ref in sources_now
            ]
            count += 1

            @pl.when(rel["c"] == 0)
            def _():
                copies[0].start()

            @pl.when(rel["c"] == 1)
            def _():
                copies[1].start()

            ends.append(copies[0])
        return ends

    edges = []
    for spot, (begin, size, before, before_tile, index, tile) in enumerate(double):
        edges += start(before, size, before_tile, left_ref.at[spot], 0)
        edges += start(index, size, tile, right_ref.at[spot], 0)
    ends = []
    for begin, size, index, tile in single:
        ends += start(index, size, tile, out_ref, begin)
    for copy in edges:
        copy.wait()
    for spot, (begin, size, *unused) in enumerate(double):
        both = left_ref[spot, :size].astype(jnp.float32) + right_ref[spot, :size].astype(jnp.float32)
        out_ref[begin : begin + size] = both.astype(NARROW)
    for copy in ends:
        copy.wait()


def join_windows(thirds, place, kind, width, total, count):
    row, tiles = KINDS[kind]
    low, high = kind_ranges(total)[kind]
    single, double = join_plan(kind, width, total, count)
    groups = -(-(high - low) // (8 * row))
    amount = sum(len(by_thirds(size, tile)) for begin, size, index, tile in single)
    for begin, size, before, before_tile, index, tile in double:
        amount += len(by_thirds(size, before_tile)) + len(by_thirds(size, tile))
    held = pltpu.VMEM((max(len(double), 1), max([d[1] for d in double] + [1]), 8, LANES), NARROW)
    (out,) = launch(
        functools.partial(join_kernel, single, double), "join_" + kind,
        [((groups * tiles, 8, LANES), NARROW)], [place] + [ref for pair in thirds for ref in pair],
        near=(0,), far=tuple(range(1, 7)), scratch=(held, held, pltpu.SemaphoreType.DMA((amount,))),
    )
    return out.reshape(groups, tiles, 8, LANES).transpose(0, 2, 1, 3).reshape(groups * 8, row)


def pack_plan(width, total, count):
    plan = []
    for index in range(count):
        for kind, first, last, tile, begin, end in window_pieces(index, width, total):
            tiles = KINDS[kind][1]
            if kind == "rest":
                plan.append((index, 6, first, last - first, tile))
                continue
            size = (PIX if kind == "embed" else D) // 8
            while first < last:
                source = first // size
                stop = min(last, (source + 1) * size)
                number = source + (0 if kind == "embed" else 3)
                plan.append((index, number, (first - source * size) * tiles, (stop - first) * tiles, tile))
                tile += (stop - first) * tiles
                first = stop
    return plan


def pack_kernel(plan, place_ref, *refs):
    sources, (keep_ref, send_ref, sems) = refs[:7], refs[7:]
    zh, zl, x, y, c = (place_ref[i] for i in range(5))
    ends = []
    for number, (index, source, begin, size, tile) in enumerate(plan):
        core = index % 2
        place = zip((16, 8, 4, 2), (zh, zl, x, y))
        spot = tuple((index // unit + own) % 2 for unit, own in place) + (pl.ds(tile, size),)
        from_ref = sources[source].at[pl.ds(begin, size)]
        keep = pltpu.make_async_copy(from_ref, keep_ref.at[spot], sems.at[number])
        send = pltpu.make_async_copy(from_ref, send_ref.at[spot], sems.at[number])

        @pl.when(c == core)
        def _():
            keep.start()

        @pl.when(c != core)
        def _():
            send.start()

        ends.append(keep)
    for copy in ends:
        copy.wait()


def tiles_of(values):
    rows, columns = values.shape
    split = values.reshape(rows // 8, 8, columns // LANES, LANES)
    return split.transpose(0, 2, 1, 3).reshape(-1, 8, LANES)


def swap(values, axis):
    return lax.ppermute(values, axis, [(0, 1), (1, 0)])


def add_low(*values):
    return sum(v.astype(jnp.float32) for v in values).astype(NARROW)


def side(values, dim, which, turn):
    if turn is None:
        return lax.index_in_dim(values, which, dim, keepdims=True)
    return lax.dynamic_slice_in_dim(values, (which + turn) % 2, 1, dim)


def chip_parts(kept, ways, cuts, cut_dim):
    return [
        ([lax.slice_in_dim(v, cuts[i], cuts[i + 1], axis=cut_dim) for v in kept], ways[i:] + ways[:i])
        for i in range(3)
    ]


def chip_stage(parts, stage):
    result = []
    for values, order in parts:
        dim, axis, turn = order[stage]
        got = swap(add_low(*(side(v, dim, 1, turn) for v in values)), axis)
        result.append(([add_low(got, *(side(v, dim, 0, turn) for v in values))], order))
    return result


def chip_join(parts, cut_dim):
    return jnp.concatenate([values[0] for values, order in parts], axis=cut_dim)


def held_back(parts, *others):
    flat = [values[0] for values, order in parts]
    flat, others = lax.optimization_barrier((flat, others))
    return [([v], order) for v, (unused, order) in zip(flat, parts)], *others


def plane_sum(values):
    rows = values.shape[0]
    core = lax.axis_index("c")
    halves = values.reshape(2, rows // 2, values.shape[1])
    kept = lax.dynamic_index_in_dim(halves, core, 0, keepdims=False)
    sent = lax.dynamic_index_in_dim(halves, 1 - core, 0, keepdims=False).astype(NARROW)
    kept = kept + swap(sent, "c").astype(jnp.float32)
    quarter = rows // 4
    parts = []
    for start, order in ((0, ("x", "y")), (quarter, ("y", "x"))):
        value = kept[start : start + quarter]
        for axis in order:
            low = value.astype(NARROW)
            value = low.astype(jnp.float32) + swap(low, axis).astype(jnp.float32)
        parts.append(value)
    mine = jnp.concatenate(parts, axis=0).astype(NARROW)
    other = swap(mine, "c")
    first = jnp.where(core == 0, mine, other)
    second = jnp.where(core == 0, other, mine)
    return jnp.concatenate([first, second], axis=0).astype(jnp.float32)


def line_gather(own):
    plane = lax.axis_index(Z_AXES)
    below, above = [], []
    value = own
    for step in (1, 2, 3):
        value = lax.ppermute(value, Z_AXES, [(i, i + 1) for i in range(step - 1, 3)])
        below.append(value)
    value = own
    for step in (1, 2, 3):
        value = lax.ppermute(value, Z_AXES, [(i, i - 1) for i in range(1, 5 - step)])
        above.append(value)
    stack = jnp.stack(below[::-1] + [own] + above)
    return lax.dynamic_slice_in_dim(stack, 3 - plane, 4, 0)


def unpack_rest(rest):
    found = []
    offset = 0
    for dims in ((D,), (PIX,), (L, 2, 2, D), (L, 4, D), (L, FF + D)):
        amount = math.prod(dims)
        found.append(rest[offset : offset + amount].reshape(dims))
        offset += amount
    return found


def fast_body(pixels, targets, mask, lat_rows, adam_params, adam_m, adam_v, mlp_weights, mlp_momentum):
    lat_index, lon_index = lax.axis_index(LAT_AXES), lax.axis_index(LON_AXES)
    device = lax.axis_index(SUB_AXES)
    devices = lax.axis_size(SUB_AXES)
    width = adam_params.shape[0]
    total = width * devices
    low_side = lax.axis_index("zl") == 0
    x, y, c = lax.axis_index("x"), lax.axis_index("y"), lax.axis_index("c")
    block = lax.axis_index(("x", "y", "c"))
    shifts = jnp.asarray(shift_tables(), NARROW)
    row_fwd = jnp.asarray(two_terms(row_table()))
    row_back = jnp.asarray(two_terms(row_table().T))
    col_fwd = jnp.asarray(two_terms(column_tables()))
    col_back = jnp.asarray(two_terms(column_tables().transpose(0, 2, 1)))
    col_fwd = jnp.where(low_side, col_fwd, col_fwd[:, 1:2])
    col_back = jnp.where(low_side, col_back, col_back[:, 1:2])
    spread = jnp.asarray(spread_table(), NARROW)

    def to_items(values):
        rest = values.shape[4:]
        lead, items, rows, cols = values.shape[:4]
        split = values.reshape((lead, items, rows, 4, OWN) + rest)
        order = (1, 3, 0, 2, 4) + tuple(range(5, 5 + len(rest)))
        packed = split.transpose(order).reshape((items * 4, lead * rows * OWN) + rest)
        got = lax.all_to_all(packed, LAT_AXES, split_axis=0, concat_axis=0, tiled=True)
        got = got.reshape((items * 4, lead, rows * OWN) + rest)
        return jnp.moveaxis(got, 1, 0).reshape((lead, TOK) + rest)

    source = to_items(pixels[None])[0]
    zh, zl = lax.axis_index("zh"), lax.axis_index("zl")
    place = jnp.stack([zh, zl, x, y, c])
    own = own_window(adam_params, device, width, total, devices).astype(NARROW)
    quarters = [own_quarters(mlp_weights, depth, x[None]) for depth in range(L)]
    windows, source, *quarters = gather_windows(own, source, *quarters)
    own_mask = own_window(jnp.ones((width,), jnp.float32), device, width, total, devices)
    first = swap(lax.dynamic_index_in_dim(quarters[0][:, 0], zl, 1, keepdims=False), "y")
    second = swap(first, "x")
    others = swap(jnp.stack([first, second], axis=1), "zl")
    third = swap(quarters[1][:, 0], "y")
    coming = (first, second, others, third, swap(third, "x"))

    def feed_forward(coming):
        first, second, others, third, fourth = coming
        both = jnp.stack([first, second], axis=1)
        across = (
            jnp.where(zl == 0, jnp.stack([both, others], axis=2), jnp.stack([others, both], axis=2)),
            jnp.stack([third, fourth], axis=1),
        )
        return [
            [chunk.reshape(2, D, D) for chunk in (own, far, swap(own, "c"), swap(far, "c"))]
            for own, far in zip(quarters, across)
        ]

    wanted = to_items(targets)
    row_weight = jnp.sin(math.pi * (lat_rows.astype(jnp.float32) + 0.5) / ROWS)
    weight_local = row_weight[None, :, None] * mask.astype(jnp.float32)
    weights = to_items(weight_local[None])[0]
    weight_sum = total_over(jnp.sum(weight_local)[None], SUB_AXES)[0]
    loss_scale = 2.0 / (STEPS * PIX * weight_sum)
    weight_pair = jnp.stack([weights, weights * loss_scale], axis=1)

    embed_w = join_windows(windows, place, "embed", width, total, devices)
    head_w = join_windows(windows, place, "head", width, total, devices)
    rest = join_windows(windows, place, "rest", width, total, devices)
    spec_rows = L * 4 * NB * BS * BS // LANES
    spec_w = rest[:spec_rows].reshape(L, 2, 2, NB, BS, BS)
    embed_b, head_b, spec_b, norm_params, mlp_b = unpack_rest(rest[spec_rows:].reshape(-1))
    embed_b, head_b = embed_b.astype(jnp.float32)[None], head_b.astype(jnp.float32)[None]
    norms = norm_params.astype(jnp.float32)
    mlp_b = mlp_b.astype(jnp.float32)

    def by_place(values):
        for dim, side in ((1, y), (2, c), (3, x)):
            values = jnp.where(side == 0, values, jnp.flip(values, dim))
        return values

    up_b = by_place(mlp_b[:, :FF].reshape(L, 2, 2, 2, -1)).transpose(0, 2, 1, 3, 4)
    up_b = up_b.reshape(L, 1, FF)
    down_b = mlp_b[:, None, FF:]
    gap = LANES - BS
    own_w = lax.dynamic_index_in_dim(spec_w, block, 3, keepdims=False)
    own_w = jnp.pad(own_w, ((0, 0),) * 3 + ((0, gap), (0, gap)))
    real, imag = own_w[:, :, 0], own_w[:, :, 1]
    pair_w = jnp.concatenate(
        [jnp.concatenate([real, imag], axis=-1), jnp.concatenate([-imag, real], axis=-1)], axis=-2
    )
    own_b = lax.dynamic_slice_in_dim(spec_b, block * BS, BS, 3).astype(jnp.float32)
    pair_b = jnp.pad(own_b, ((0, 0),) * 3 + ((0, gap),)).reshape(L, 2, 2 * LANES)

    f32 = jnp.float32
    payload = ((GROUP, HALF_TOK, LANES), NARROW)
    state_f32 = ((TOK, D), f32)
    wide = pltpu.VMEM((GROUP, HALF_TOK + 8, LANES), f32)
    sem = pltpu.SemaphoreType.DMA
    held_mlp = (pltpu.VMEM((4, 2, D, D), NARROW), sem((4,)))

    current = source
    saved = []
    loss_sums = []
    for roll_idx in range(STEPS):
        state, sent = launch(
            embed_kernel, "embed", [state_f32, payload],
            [current, shifts, embed_b, norms[0], spread, row_fwd, embed_w], going=(0,),
        )
        if roll_idx == 0:
            sent, wanted = lax.optimization_barrier((sent, wanted))
        layers = []
        for depth in range(L):
            got = exchange(sent)
            out, mixed_in = launch(
                spec_kernel, "spec", [payload, ((FREQ, 2 * LANES), NARROW)],
                [got, col_fwd, col_back, pair_w[depth], pair_b[depth]], scratch=(wide, wide),
                going=(1,),
            )
            if roll_idx == 0 and depth == 0:
                unused, coming = lax.optimization_barrier((out, coming))
                mlp_low = feed_forward(coming)
            got = exchange(out)
            has_next = depth + 1 < L
            outs = [state_f32, ((TOK, D), NARROW), ((TOK, FF), f32), ((TOK, FF), NARROW), state_f32]
            results = launch(
                functools.partial(mlp_kernel, has_next), "mlp", outs + [payload] * has_next,
                [got, state, norms[depth], norms[min(depth + 1, L - 1)], up_b[depth], down_b[depth],
                 spread, row_fwd, row_back, *mlp_low[depth]], far=(9, 10, 11, 12), scratch=held_mlp, limit=MLP_LIMIT,
                coming=(1,), going=(0, 1, 2, 3, 4),
            )
            layers.append((state, mixed_in) + tuple(results[:4]))
            state = results[4]
            if has_next:
                sent = results[5]
        low, predicted, loss_grad, loss_part = launch(
            head_kernel, "head",
            [((TOK, D), NARROW), ((TOK, PIX), NARROW), ((TOK, PIX), f32), ((1, PIX), f32)],
            [state, shifts, head_b, wanted[roll_idx], weight_pair, head_w], coming=(0, 3), going=(0, 2),
        )
        loss_sums.append(loss_part)
        saved.append((current, layers, low, loss_grad))
        current = predicted

    rows_own = mlp_momentum.shape[2] // 2
    half_ff = FF // 2

    def joined(terms, member):
        return jnp.concatenate([now[member] for now in terms], axis=0)

    mlp_ways = [(3, "x", None), (2, "y", None), (1, "zl", zl)]

    def mlp_sends(depth):
        g_before, hidden_in, hidden, grad_out = (joined(mlp_terms[depth], m) for m in range(4))
        pairs = ((g_before, hidden_in), (hidden, grad_out))
        return pairs, [swap(dot_tn(a[:, half_ff:], b).astype(NARROW), "c") for a, b in pairs]

    def mlp_kept(pairs, got):
        kept = [
            (dot_tn(a[:, :half_ff], b) + sent.astype(f32)).astype(NARROW)
            for (a, b), sent in zip(pairs, got)
        ]
        return jnp.stack(kept).reshape(2, 2, 2, rows_own, D)

    head_terms, embed_terms = [], []
    mlp_terms = [[] for unused in range(L)]
    spec_terms = [[] for unused in range(L)]
    sum_terms = [[] for unused in range(L)]
    head_sums, embed_sums = [], []
    upstream = None
    for roll_idx in reversed(range(STEPS)):
        current, layers, low, loss_grad = saved[roll_idx]
        upstream = loss_grad if upstream is None else upstream
        upstream_low, head_sum, grad_state = launch(
            head_back_kernel, "head_back",
            [((TOK, PIX), NARROW), ((1, PIX), f32), state_f32], [upstream, shifts, head_w],
            coming=(0,), going=(0,),
        )
        head_terms.append((low, upstream_low))
        head_sums.append(head_sum)
        for depth in reversed(range(L)):
            state, mixed_in, mixed, hidden_in, before, hidden = layers[depth]
            grad_out, g_before, g_mixed, g_up_b, sums_two, sent = launch(
                mlp_back_kernel, "mlp_back",
                [((TOK, D), NARROW), ((TOK, FF), NARROW), state_f32, ((1, FF), f32), ((3, D), f32),
                 payload],
                [grad_state, before, mixed, norms[depth], spread, row_fwd, *mlp_low[depth]],
                far=(6, 7, 8, 9), scratch=held_mlp, limit=MLP_LIMIT,
                coming=(1, 2), going=(0, 1, 2),
            )
            mlp_terms[depth].append((g_before, hidden_in, hidden, grad_out))
            got = exchange(sent)
            if roll_idx == 0 and depth == L - 1:
                last_sends = mlp_sends(depth)
                last_kept, got = lax.optimization_barrier((mlp_kept(*last_sends), got))
            if roll_idx == 0 and depth == 0:
                first_kept, got = lax.optimization_barrier((mlp_kept(*mlp_sends(0)), got))
            out, g_pair, g_pair_b = launch(
                spec_back_kernel, "spec_back",
                [payload, ((2, 2 * LANES, 2 * LANES), f32), ((2, 2 * LANES), f32)],
                [got, col_fwd, col_back, pair_w[depth], pair_b[depth], mixed_in],
                scratch=(wide, wide), coming=(5,),
            )
            got = exchange(out)
            if roll_idx == 0 and depth == 0:
                last_kept, first_kept, got = lax.optimization_barrier((last_kept, first_kept, got))
            grad_state, state_low, sums_one = launch(
                norm_back_kernel, "norm_back", [state_f32, ((TOK, D), NARROW), ((3, D), f32)],
                [got, g_mixed, state, norms[depth], spread, row_back], coming=(1, 2),
            )
            spec_terms[depth].append((g_pair, g_pair_b))
            sum_terms[depth].append((sums_one, sums_two, g_up_b))
        embed_terms.append((current, state_low))
        embed_sums.append(sums_one[2])
        if roll_idx:
            (upstream,) = launch(
                embed_back_kernel, "embed_back", [((TOK, PIX), f32)],
                [state_low, shifts, saved[roll_idx - 1][3], embed_w], coming=(2,), going=(0,),
            )

    mlp_kept_all = jnp.stack([first_kept, last_kept])
    mlp_parts = chip_stage(chip_parts([mlp_kept_all], mlp_ways, MLP_CUTS, 4), 0)

    def moved_pair(values, amount):
        return jnp.concatenate([jnp.roll(now, amount, axis=0) for now in values], axis=0)

    embed_src = joined(embed_terms, 0)
    head_up = joined(head_terms, 1)
    g_embed = [
        dot_tn(embed_src, moved_pair([now[1] for now in embed_terms], OWN * (o - 1))).astype(NARROW)
        for o in range(3)
    ]
    g_head = [
        dot_tn(moved_pair([now[0] for now in head_terms], -OWN * (o - 1)), head_up).astype(NARROW)
        for o in range(3)
    ]
    g_spec, g_spec_b, g_norm, g_mlp_b = [], [], [], []
    for depth in range(L):
        pair_sum = sum(now[0] for now in spec_terms[depth]).reshape(2, 2, LANES, 2, LANES)
        pair_sum = pair_sum[:, :, :BS, :, :BS]
        g_real = pair_sum[:, 0, :, 0] + pair_sum[:, 1, :, 1]
        g_imag = pair_sum[:, 0, :, 1] - pair_sum[:, 1, :, 0]
        g_spec.append(jnp.stack([g_real, g_imag], axis=1))
        g_spec_b.append(sum(now[1] for now in spec_terms[depth]).reshape(2, 2, LANES)[:, :, :BS])
        one = sum(now[0] for now in sum_terms[depth])
        two = sum(now[1] for now in sum_terms[depth])
        g_norm.append(jnp.stack([one[0], one[1], two[1], two[2]]))
        up_sum = sum(now[2] for now in sum_terms[depth]).reshape(1, 2, 2, 2, -1)
        up_sum = by_place(up_sum.transpose(0, 2, 1, 3, 4)).reshape(-1)
        g_mlp_b.append(jnp.concatenate([up_sum, two[0]]))
    full_spec = jnp.zeros((L, 2, 2, NB, BS, BS), NARROW)
    full_spec = lax.dynamic_update_slice_in_dim(
        full_spec, jnp.stack(g_spec).astype(NARROW)[:, :, :, None], block, 3
    )
    full_spec_b = lax.dynamic_update_slice_in_dim(
        jnp.zeros((L, 2, 2, D), f32), jnp.stack(g_spec_b), block * BS, 3
    )
    small = jnp.concatenate(
        [sum(embed_sums), sum(head_sums)[0], full_spec_b.reshape(-1),
         jnp.stack(g_norm).reshape(-1), jnp.stack(g_mlp_b).reshape(-1)]
    ).astype(NARROW)
    rest_grad = jnp.concatenate([full_spec.reshape(-1), small])
    rest_grad = jnp.pad(rest_grad, (0, -rest_grad.shape[0] % (8 * LANES))).reshape(-1, 8, LANES)
    plan = pack_plan(width, total, devices)
    window_set = ((2, 2, 2, 2, WINDOW, 8, LANES), NARROW)
    kept, sent = launch(
        functools.partial(pack_kernel, plan), "pack", [window_set, window_set],
        [place] + [tiles_of(g) for g in g_embed + g_head] + [rest_grad],
        near=(0,), far_out=True, scratch=(sem((len(plan),)),), limit=8,
    )
    ways = [(2, "x", None), (3, "y", None), (1, "zl", None)]
    got = swap(sent, "c")
    mlp_parts, got = held_back(mlp_parts, got)
    parts = chip_parts([kept, got], ways, WINDOW_CUTS, 4)
    for stage in range(3):
        parts = chip_stage(parts, stage)
        if stage:
            mlp_parts = chip_stage(mlp_parts, stage)
    mlp_pair = chip_join(mlp_parts, 4).reshape(2, rows_own, D)
    mlp_send = jnp.where(zh == 0, mlp_pair[1], mlp_pair[0])
    mlp_keep = jnp.where(zh == 0, mlp_pair[0], mlp_pair[1])
    mlp_mine = mlp_keep.astype(f32) + swap(mlp_send, "zh").astype(f32)
    flat_pair = chip_join(parts, 4).reshape(2, WINDOW, 8, LANES)
    flat_window = flat_pair[0].astype(f32) + swap(flat_pair[1], "zh").astype(f32)
    flat_piece = own_range(flat_window, device, width, total, devices)
    local = jnp.stack(
        [jnp.sum(jnp.where(own_mask > 0, flat_window * flat_window, 0.0)) + jnp.sum(mlp_mine * mlp_mine),
         sum(jnp.sum(now) for now in loss_sums)]
    )
    square_sum, loss_total = total_over(local, SUB_AXES)
    loss_total = loss_total / (STEPS * PIX * weight_sum)
    grad_norm = jnp.sqrt(square_sum)
    factor = jnp.minimum(1.0, CLIP_LEVEL / (grad_norm + 1e-06))

    mlp_grad = lax.all_gather(mlp_mine.astype(NARROW), LAT_AXES, axis=0, tiled=True)

    held = mlp_momentum.reshape(2 * L * 2, rows_own, D)
    held = lax.dynamic_index_in_dim(held, lat_index, 0, keepdims=False)
    mine_new = MOMENT_KEEP * held + mlp_mine * factor
    high = lax.Precision.HIGH
    gram = plane_sum(lax.dot_general(mine_new, mine_new, (((0,), (0,)), ((), ())), precision=high))
    inverse = 1.0 / (jnp.sqrt(jnp.trace(gram)) + 1e-07)
    lead, mid, last = POLY_COEF
    square = gram * (inverse * inverse)
    mul = functools.partial(jnp.dot, precision=high)
    poly_one = mid * square + last * mul(square, square)
    turned = mul(square, poly_one)
    square_two = lead * lead * square + 2.0 * lead * turned + mul(turned, poly_one)
    poly_two = mid * square_two + last * mul(square_two, square_two)
    mine_one, mine_two = (
        lax.dynamic_slice_in_dim(now, c * (D // 2), D // 2, 0) for now in (poly_one, poly_two)
    )
    change = (lead * (mine_one + mine_two) + mul(mine_one, poly_two)) * inverse
    level_high = inverse.astype(NARROW)
    level_mid = (inverse - level_high.astype(f32)).astype(NARROW)
    level_low = (inverse - level_high.astype(f32) - level_mid.astype(f32)).astype(NARROW)
    column = jnp.arange(D)[None]
    extra = jnp.where(column == 0, level_high, jnp.where(column == 1, level_mid, level_low))
    extra = jnp.broadcast_to(extra, (8, D))
    change = change.astype(NARROW)
    packed = jnp.concatenate([change, extra], axis=0)
    packed, mlp_grad = lax.optimization_barrier((packed, mlp_grad))
    gathered = line_gather(packed)
    mlp_grad = mlp_grad.reshape(mlp_momentum.shape).astype(f32)
    momentum_new = MOMENT_KEEP * mlp_momentum + mlp_grad * factor
    clipped = flat_piece * factor
    first_new = BETA_FIRST * adam_m + (1.0 - BETA_FIRST) * clipped
    second_new = BETA_SECOND * adam_v + (1.0 - BETA_SECOND) * clipped * clipped
    count_value = float(STEP_NUM)
    first_hat = first_new / (1.0 - BETA_FIRST**count_value)
    second_hat = second_new / (1.0 - BETA_SECOND**count_value)
    adam_new = adam_params - ADAM_RATE * (
        first_hat / (jnp.sqrt(second_hat) + 1e-08) + DECAY_RATE * adam_params
    )
    gathered, momentum_new, adam_new, first_new, second_new = lax.optimization_barrier(
        (gathered, momentum_new, adam_new, first_new, second_new)
    )
    levels = jnp.sum(gathered[:, D // 2, :3].astype(f32), axis=-1)
    gathered = gathered[:, : D // 2]
    other = swap(gathered, "c")
    changes = jnp.concatenate(
        [jnp.where(c == 0, gathered, other), jnp.where(c == 0, other, gathered)], axis=1
    )
    (mlp_new,) = pl.pallas_call(
        muon_kernel,
        name="muon",
        grid=(2 * L, 2),
        out_shape=[jax.ShapeDtypeStruct((2 * L, D, D), f32)],
        in_specs=[pl.BlockSpec(memory_space=pltpu.SMEM)]
        + [pl.BlockSpec((None, rows_own, D), lambda m, h: (m, h, 0))] * 2
        + [pl.BlockSpec((None, D, D), lambda m, h: (m, 0, 0))],
        out_specs=[pl.BlockSpec((None, rows_own, D), lambda m, h: (m, h, 0))],
        compiler_params=pltpu.CompilerParams(vmem_limit_bytes=28 * 1024 * 1024),
    )(levels, momentum_new.reshape(2 * L, D, D), mlp_weights.reshape(2 * L, D, D), changes)
    mlp_new = mlp_new.reshape(mlp_weights.shape)

    return (adam_new, first_new, second_new, mlp_new, momentum_new, loss_total, grad_norm)


def solution(mesh):
    if tuple(mesh.shape.items()) == (("lat", 8), ("lon", 4)):
        fine = Mesh(mesh.devices.reshape(2, 2, 2, 2, 2), SUB_AXES)
        return placed(fast_body, fine, LAT_AXES, LON_AXES)
    return placed(body, mesh, ("lat",), ("lon",))


def placed(step, mesh, lat, lon):
    flat = P(lat + lon)
    halves = P(None, None, lon, None)
    return jax.shard_map(
        step,
        mesh=mesh,
        in_specs=(
            P(None, lat, lon, None),
            P(None, None, lat, lon, None),
            P(None, lat, lon),
            P(lat),
            flat,
            flat,
            flat,
            halves,
            halves,
        ),
        out_specs=(flat, flat, flat, halves, halves, P(), P()),
        check_vma=False,
    )
```

```python
import functools
import math

import jax
import ml_dtypes
import numpy as np
import jax.numpy as jnp
from jax import lax
from jax.experimental import pallas as pl
from jax.experimental.pallas import tpu as pltpu
from jax.sharding import Mesh
from jax.sharding import PartitionSpec as P

D = 768
FF = 3072
NB = 8
PIX = 1280
BS = 96
L = 2
STEPS = 2
NS_STEPS = 2
STEP_NUM = 5


HIGH_PREC = lax.Precision.HIGHEST
NORM_EPS = 1e-05
CLIP_LEVEL = 0.001
BETA_FIRST = 0.9
BETA_SECOND = 0.95
ADAM_RATE = 0.01
MUON_RATE = 0.8
DECAY_RATE = 0.05
MOMENT_KEEP = 0.95
POLY_COEF = (3.4445, -4.775, 2.0315)


def for_sending(value):

    def short(part):
        return part.astype(jnp.bfloat16) if part.dtype == jnp.float32 else part

    return jax.tree.map(short, value)


def with_halo(block, sides, width):
    for axis, dim in sides:
        count = lax.axis_size(axis)
        forward = [(i, i + 1) for i in range(count - 1)]
        forward.append((count - 1, 0))
        backward = [(target, source) for source, target in forward]
        low = lax.ppermute(
            lax.slice_in_dim(block, block.shape[dim] - width, None, axis=dim), axis, forward
        )
        high = lax.ppermute(lax.slice_in_dim(block, 0, width, axis=dim), axis, backward)
        block = jnp.concatenate([low, block, high], axis=dim)
    return block


def unpack(flat_params):
    layout = [
        (3, PIX, D),
        (3, D, PIX),
        (L, 2, 2, NB, BS, BS),
        (D,),
        (PIX,),
        (L, 2, 2, D),
        (L, 4, D),
        (L, FF + D),
    ]
    pieces_out = []
    offset = 0
    for dims_now in layout:
        amount = math.prod(dims_now)
        pieces_out.append(flat_params[offset : offset + amount].reshape(dims_now))
        offset = offset + amount
    return pieces_out


def along(matrix, values, axis_dim):
    if axis_dim == 1:
        return jnp.einsum("kn,bncd->bkcd", matrix, values, precision=HIGH_PREC)
    return jnp.einsum("kn,brnd->brkd", matrix, values, precision=HIGH_PREC)


def phase_table(out_count, in_count, length_all):
    out_index = jnp.arange(out_count, dtype=jnp.int32)
    in_index = jnp.arange(in_count, dtype=jnp.int32)
    phase = out_index[:, None] * in_index[None, :] % length_all
    angle = phase.astype(jnp.float32) * (2.0 * math.pi / length_all)
    scale_value = 1.0 / math.sqrt(length_all)
    return (jnp.cos(angle) * scale_value, jnp.sin(angle) * scale_value)


def combine(pieces, axis_dim, sign_value, tables, real_only):
    cosine, sine_table = tables
    values = [piece_now.astype(jnp.float32) for piece_now in pieces]
    real_out = along(cosine, values[0], axis_dim)
    if len(values) > 1:
        real_out = real_out - sign_value * along(sine_table, values[1], axis_dim)
    if real_only:
        return (real_out,)
    imag_out = sign_value * along(sine_table, values[0], axis_dim)
    if len(values) > 1:
        imag_out = imag_out + along(cosine, values[1], axis_dim)
    return (real_out, imag_out)


def turn_transform(pieces, axis_dim, sign_value, real_only):
    if axis_dim == 1:
        wide = jax.tree.map(
            lambda part, own: part.astype(own.dtype),
            lax.all_to_all(for_sending(pieces), "lat", split_axis=3, concat_axis=1, tiled=True),
            pieces,
        )
        length_all = wide[0].shape[1]
        result = combine(
            wide, 1, sign_value, phase_table(length_all, length_all, length_all), real_only
        )
        narrow = tuple((piece_now.astype(jnp.bfloat16) for piece_now in result))
        returned = jax.tree.map(
            lambda part, own: part.astype(own.dtype),
            lax.all_to_all(for_sending(narrow), "lat", split_axis=1, concat_axis=3, tiled=True),
            narrow,
        )
        return tuple((piece_now.astype(jnp.float32) for piece_now in returned))
    wide = jax.tree.map(
        lambda part, own: part.astype(own.dtype),
        lax.all_to_all(for_sending(pieces), "lon", split_axis=3, concat_axis=2, tiled=True),
        pieces,
    )
    length_all = wide[0].shape[2]
    result = combine(
        wide, 2, sign_value, phase_table(length_all, length_all, length_all), real_only
    )
    return jax.tree.map(
        lambda part, own: part.astype(own.dtype),
        lax.all_to_all(for_sending(result), "lon", split_axis=2, concat_axis=3, tiled=True),
        result,
    )


def transform(pieces, axis_dim, sign_value, real_only):
    return turn_transform(pieces, axis_dim, sign_value, real_only)


def to_low(pieces):
    return tuple((piece_now.astype(jnp.bfloat16) for piece_now in pieces))


def exact_gelu(values):
    return jax.nn.gelu(values, approximate=False)


def gelu_back(values, upstream):
    return jax.vjp(exact_gelu, values)[1](upstream)[0]


def norm_forward(inputs, gain, shift):
    center = inputs - jnp.mean(inputs, axis=-1, keepdims=True)
    inverse = lax.rsqrt(jnp.mean(center * center, axis=-1, keepdims=True) + NORM_EPS)
    scaled = center * inverse
    return (scaled * gain + shift, (scaled, inverse))


def norm_backward(upstream, saved, gain):
    scaled, inverse = saved
    g_gain = jnp.sum(upstream * scaled, axis=(0, 1, 2))
    g_shift = jnp.sum(upstream, axis=(0, 1, 2))
    g_scaled = upstream * gain
    g_input = inverse * (
        g_scaled
        - jnp.mean(g_scaled, axis=-1, keepdims=True)
        - scaled * jnp.mean(g_scaled * scaled, axis=-1, keepdims=True)
    )
    return (g_input, g_gain, g_shift)


def block_mix(pieces, weights, bias):
    shaped = [piece_now.reshape(piece_now.shape[:-1] + (NB, BS)) for piece_now in pieces]

    def multiply(left_side, right_side):
        return jnp.einsum(
            "brcni,nio->brcno", left_side, right_side, preferred_element_type=jnp.float32
        )

    real_out = multiply(shaped[0], weights[0]) - multiply(shaped[1], weights[1])
    imag_out = multiply(shaped[0], weights[1]) + multiply(shaped[1], weights[0])
    full_dims = pieces[0].shape
    return (
        real_out.reshape(full_dims) + bias[0].astype(jnp.float32),
        imag_out.reshape(full_dims) + bias[1].astype(jnp.float32),
    )


def block_back(grads_low, pieces, weights):
    shaped = [piece_now.reshape(piece_now.shape[:-1] + (NB, BS)) for piece_now in pieces]
    g_shaped = [grad_now.reshape(grad_now.shape[:-1] + (NB, BS)) for grad_now in grads_low]

    def back_multiply(grad_side, weight_side):
        return jnp.einsum(
            "brcno,nio->brcni", grad_side, weight_side, preferred_element_type=jnp.float32
        )

    def weight_multiply(input_side, grad_side):
        return jnp.einsum(
            "brcni,brcno->nio", input_side, grad_side, preferred_element_type=jnp.float32
        )

    g_real = back_multiply(g_shaped[0], weights[0]) + back_multiply(g_shaped[1], weights[1])
    g_imag = back_multiply(g_shaped[1], weights[0]) - back_multiply(g_shaped[0], weights[1])
    g_w_real = weight_multiply(shaped[0], g_shaped[0]) + weight_multiply(shaped[1], g_shaped[1])
    g_w_imag = weight_multiply(shaped[0], g_shaped[1]) - weight_multiply(shaped[1], g_shaped[0])
    g_bias = jnp.stack(
        [jnp.sum(grad_now.astype(jnp.float32), axis=(0, 1, 2)) for grad_now in grads_low]
    )
    full_dims = pieces[0].shape
    return (
        (g_real.reshape(full_dims), g_imag.reshape(full_dims)),
        jnp.stack([g_w_real, g_w_imag]),
        g_bias,
    )


def halo_rows(values):
    return with_halo(values, (("lat", 1),), 1)


def rows_conv(source_low, weight3, bias):
    padded = halo_rows(source_low)
    row_count = source_low.shape[1]
    window = jnp.concatenate(
        [padded[:, offset : offset + row_count] for offset in range(3)], axis=-1
    )
    flat_weight = weight3.reshape(-1, weight3.shape[-1])
    result = jnp.einsum("brci,io->brco", window, flat_weight, preferred_element_type=jnp.float32)
    return (result + bias.astype(jnp.float32), window)


def rows_back(grad_low, weight3, need_source):
    g_bias = jnp.sum(grad_low.astype(jnp.float32), axis=(0, 1, 2))
    if not need_source:
        return (g_bias, None)
    padded = halo_rows(grad_low)
    row_count = grad_low.shape[1]
    window_back = jnp.concatenate(
        [padded[:, 2 - offset : 2 - offset + row_count] for offset in range(3)], axis=-1
    )
    flipped = jnp.transpose(weight3, (0, 2, 1)).reshape(-1, weight3.shape[1])
    g_source = jnp.einsum("brco,oi->brci", window_back, flipped, preferred_element_type=jnp.float32)
    return (g_bias, g_source)


def conv_weight_grad(terms_list, weight3):
    window = jnp.concatenate([terms_now[0] for terms_now in terms_list], axis=0)
    grads_low = jnp.concatenate([terms_now[1] for terms_now in terms_list], axis=0)
    return jnp.einsum(
        "brci,brco->io", window, grads_low, preferred_element_type=jnp.float32
    ).reshape(weight3.shape)


def layer_forward(state, params_now):
    spec_w, spec_b, norm_vals, mlp_pair, mlp_bias = params_now
    normed, first_saved = norm_forward(state, norm_vals[0], norm_vals[1])
    spectrum = transform((normed.astype(jnp.bfloat16),), 2, -1.0, False)
    spectrum = transform(to_low(spectrum), 1, -1.0, False)
    mixed_in = to_low(spectrum)
    inner = block_mix(mixed_in, spec_w[0], spec_b[0])
    activated = to_low(tuple((exact_gelu(piece_now) for piece_now in inner)))
    outer = block_mix(activated, spec_w[1], spec_b[1])
    spectrum = transform(to_low(outer), 1, 1.0, False)
    spatial = transform(to_low(spectrum), 2, 1.0, True)[0]
    mixed = state + spatial + normed
    second, second_saved = norm_forward(mixed, norm_vals[2], norm_vals[3])
    hidden_in = second.astype(jnp.bfloat16)
    before = (
        jnp.einsum("brcd,fd->brcf", hidden_in, mlp_pair[0], preferred_element_type=jnp.float32)
        + mlp_bias[:FF]
    )
    hidden = exact_gelu(before).astype(jnp.bfloat16)
    result = (
        jnp.einsum("brcf,fd->brcd", hidden, mlp_pair[1], preferred_element_type=jnp.float32)
        + mlp_bias[FF:]
    )
    return (
        mixed + result,
        (first_saved, mixed_in, inner, activated, second_saved, hidden_in, before, hidden),
    )


def layer_backward(upstream, cache, params_now):
    spec_w, spec_b, norm_vals, mlp_pair, mlp_bias = params_now
    first_saved, mixed_in, inner, activated, second_saved, hidden_in, before, hidden = cache
    grad_out = upstream.astype(jnp.bfloat16)
    g_down_bias = jnp.sum(grad_out.astype(jnp.float32), axis=(0, 1, 2))
    g_hidden = jnp.einsum(
        "brcd,fd->brcf", grad_out, mlp_pair[1], preferred_element_type=jnp.float32
    )
    g_before = gelu_back(before, g_hidden).astype(jnp.bfloat16)
    g_up_bias = jnp.sum(g_before.astype(jnp.float32), axis=(0, 1, 2))
    g_second = jnp.einsum(
        "brcf,fd->brcd", g_before, mlp_pair[0], preferred_element_type=jnp.float32
    )
    g_norm_in, g_gain_two, g_shift_two = norm_backward(g_second, second_saved, norm_vals[2])
    g_mixed = upstream + g_norm_in
    g_spectrum = transform((g_mixed.astype(jnp.bfloat16),), 2, -1.0, False)
    g_outer = to_low(transform(to_low(g_spectrum), 1, -1.0, False))
    g_activated, g_w_outer, g_b_outer = block_back(g_outer, activated, spec_w[1])
    g_inner = to_low(
        tuple((gelu_back(piece_now, grad_now) for piece_now, grad_now in zip(inner, g_activated)))
    )
    g_mixed_in, g_w_inner, g_b_inner = block_back(g_inner, mixed_in, spec_w[0])
    g_spectrum = transform(to_low(g_mixed_in), 1, 1.0, False)
    g_normed = transform(to_low(g_spectrum), 2, 1.0, True)[0] + g_mixed
    g_state_norm, g_gain_one, g_shift_one = norm_backward(g_normed, first_saved, norm_vals[0])
    layer_grads = (
        jnp.stack([g_w_inner, g_w_outer]),
        jnp.stack([g_b_inner, g_b_outer]),
        jnp.stack([g_gain_one, g_shift_one, g_gain_two, g_shift_two]),
        jnp.concatenate([g_up_bias, g_down_bias]),
    )
    return (g_mixed + g_state_norm, layer_grads, (hidden, grad_out, g_before, hidden_in))


def body(pixels, targets, mask, lat_rows, adam_params, adam_m, adam_v, mlp_weights, mlp_momentum):
    flat_low = lax.all_gather(adam_params.astype(jnp.bfloat16), ("lat", "lon"), axis=0, tiled=True)
    mlp_low = lax.all_gather(mlp_weights.astype(jnp.bfloat16), "lon", axis=2, tiled=True)
    embed_w, head_w, spec_w, embed_b, head_b, spec_b, norm_params, mlp_b = unpack(flat_low)
    row_count = pixels.shape[1]
    lat_total = lax.axis_size("lat") * row_count
    row_weight = jnp.sin(math.pi * (lat_rows.astype(jnp.float32) + 0.5) / lat_total)
    weight_map = row_weight[None, :, None] * mask.astype(jnp.float32)
    weight_sum = lax.psum(jnp.sum(weight_map), ("lat", "lon"))
    loss_scale = 2.0 / (STEPS * PIX * weight_sum)

    def params_at(depth_idx):
        return (
            spec_w[depth_idx],
            spec_b[depth_idx],
            norm_params[depth_idx].astype(jnp.float32),
            mlp_low[depth_idx],
            mlp_b[depth_idx].astype(jnp.float32),
        )

    current = pixels
    saved_steps = []
    loss_local = jnp.zeros((), jnp.float32)
    for roll_idx in range(STEPS):
        state, embed_window = rows_conv(current.astype(jnp.bfloat16), embed_w, embed_b)
        caches = []
        for depth_idx in range(L):
            state, cache_now = layer_forward(state, params_at(depth_idx))
            caches.append(cache_now)
        predicted, head_window = rows_conv(state.astype(jnp.bfloat16), head_w, head_b)
        differ = predicted - targets[roll_idx].astype(jnp.float32)
        loss_local = loss_local + jnp.sum(weight_map[..., None] * differ * differ)
        saved_steps.append(
            (embed_window, caches, head_window, weight_map[..., None] * differ * loss_scale)
        )
        current = predicted
    g_embed_b = jnp.zeros(embed_b.shape, jnp.float32)
    g_head_b = jnp.zeros(head_b.shape, jnp.float32)
    head_terms = []
    embed_terms = []
    mlp_terms = [[] for unused in range(L)]
    g_layers = [None] * L
    carried = None
    for roll_idx in reversed(range(STEPS)):
        embed_window, caches, head_window, loss_grad = saved_steps[roll_idx]
        upstream = loss_grad if carried is None else loss_grad + carried
        upstream_low = upstream.astype(jnp.bfloat16)
        head_terms.append((head_window, upstream_low))
        grad_b, grad_state = rows_back(upstream_low, head_w, True)
        g_head_b = g_head_b + grad_b
        for depth_idx in reversed(range(L)):
            grad_state, layer_grads, mlp_now = layer_backward(
                grad_state, caches[depth_idx], params_at(depth_idx)
            )
            mlp_terms[depth_idx].append(mlp_now)
            if g_layers[depth_idx] is None:
                g_layers[depth_idx] = layer_grads
            else:
                g_layers[depth_idx] = jax.tree.map(jnp.add, g_layers[depth_idx], layer_grads)
        state_low = grad_state.astype(jnp.bfloat16)
        embed_terms.append((embed_window, state_low))
        grad_b, carried = rows_back(state_low, embed_w, roll_idx > 0)
        g_embed_b = g_embed_b + grad_b
    g_embed_w = conv_weight_grad(embed_terms, embed_w)
    g_head_w = conv_weight_grad(head_terms, head_w)
    mlp_grads = []
    for depth_idx in range(L):
        joined = [
            jnp.concatenate([terms_now[member] for terms_now in mlp_terms[depth_idx]], axis=0)
            for member in range(4)
        ]
        g_up = jnp.einsum("brcf,brcd->fd", joined[2], joined[3], preferred_element_type=jnp.float32)
        g_down = jnp.einsum(
            "brcf,brcd->fd", joined[0], joined[1], preferred_element_type=jnp.float32
        )
        mlp_grads.append(jnp.stack([g_up, g_down]))
    full_mlp = jnp.stack(mlp_grads)
    stacked = [
        jnp.stack([g_layers[depth_idx][member] for depth_idx in range(L)]) for member in range(4)
    ]
    flat_grad = jnp.concatenate(
        [
            g_embed_w.reshape(-1),
            g_head_w.reshape(-1),
            stacked[0].reshape(-1),
            g_embed_b,
            g_head_b,
            stacked[1].reshape(-1),
            stacked[2].reshape(-1),
            stacked[3].reshape(-1),
        ]
    )
    lon_count = lax.axis_size("lon")
    lat_count = lax.axis_size("lat")
    dev_count = lon_count * lat_count
    per_block = full_mlp.shape[2] // dev_count
    mlp_rows = (
        full_mlp.reshape(L, 2, lon_count, lat_count, per_block, D)
        .transpose(3, 2, 0, 1, 4, 5)
        .reshape(dev_count, -1)
    )
    flat_rows = flat_grad.reshape(dev_count, -1)
    flat_width = flat_rows.shape[1]
    summed = lax.psum_scatter(
        jnp.concatenate([flat_rows, mlp_rows], axis=1),
        ("lat", "lon"),
        scatter_dimension=0,
        tiled=True,
    )[0]
    flat_piece = summed[:flat_width]
    mlp_piece = summed[flat_width:].reshape(L, 2, per_block, D)
    local_square = jnp.sum(flat_piece * flat_piece) + jnp.sum(mlp_piece * mlp_piece)
    loss_total, square_sum = lax.psum(
        (loss_local / (STEPS * PIX * weight_sum), local_square), ("lat", "lon")
    )
    mlp_grad = lax.all_gather(mlp_piece.astype(jnp.bfloat16), "lat", axis=2, tiled=True).astype(
        mlp_piece.dtype
    )
    grad_norm = jnp.sqrt(square_sum)
    factor = jnp.minimum(1.0, CLIP_LEVEL / (grad_norm + 1e-06))
    clipped = flat_piece * factor
    first_new = BETA_FIRST * adam_m + (1.0 - BETA_FIRST) * clipped
    second_new = BETA_SECOND * adam_v + (1.0 - BETA_SECOND) * clipped * clipped
    count_value = float(STEP_NUM)
    first_hat = first_new / (1.0 - BETA_FIRST**count_value)
    second_hat = second_new / (1.0 - BETA_SECOND**count_value)
    adam_new = adam_params - ADAM_RATE * (
        first_hat / (jnp.sqrt(second_hat) + 1e-08) + DECAY_RATE * adam_params
    )
    momentum_new = MOMENT_KEEP * mlp_momentum + mlp_grad * factor
    ortho = momentum_new
    for ns_idx in range(NS_STEPS):
        partial_gram = jnp.einsum("lkfd,lkfe->lkde", ortho, ortho, precision=HIGH_PREC)
        square = lax.psum(partial_gram.astype(jnp.bfloat16), "lon").astype(jnp.float32)
        if ns_idx == 0:
            trace_val = jnp.trace(square, axis1=2, axis2=3)
            inverse = 1.0 / (jnp.sqrt(trace_val) + 1e-07)
            ortho = ortho * inverse[:, :, None, None]
            square = square * (inverse * inverse)[:, :, None, None]
        poly = POLY_COEF[1] * square + POLY_COEF[2] * jnp.einsum(
            "lkde,lkef->lkdf", square, square, precision=HIGH_PREC
        )
        ortho = POLY_COEF[0] * ortho + jnp.einsum(
            "lkfd,lkde->lkfe", ortho, poly, precision=HIGH_PREC
        )
    mlp_new = mlp_weights * (1.0 - MUON_RATE * DECAY_RATE) - MUON_RATE * (FF / D) ** 0.5 * ortho
    return (adam_new, first_new, second_new, mlp_new, momentum_new, loss_total, grad_norm)


ROWS = 48
COLS = 48
GROUP = 16
OWN = 3
TOK = ROWS * OWN
HALF_TOK = TOK // 2
PAIRS = 12
LANES = 128
WIDE = NB * LANES
FREQ = PAIRS * 96
NARROW = jnp.bfloat16
WINDOW = 212
MLP_LIMIT = 26
WINDOW_CUTS = (0, 72, 142, WINDOW)
MLP_CUTS = (0, 128, 256, 384)
EMBED_AT = 2
Z_AXES = ("zh", "zl")
EMBED_SIZE = 3 * PIX * D
SUB_AXES = ("zh", "zl", "x", "y", "c")
LAT_AXES = ("zh", "zl", "x")
LON_AXES = ("y", "c")
ITEM_AXES = ("zl", "x", "y", "c")


def shift_tables():
    table = np.zeros((3, TOK, TOK), np.float32)
    spots = np.arange(TOK)
    for offset in range(3):
        table[offset, spots, (spots + OWN * (offset - 1)) % TOK] = 1.0
    return table


def row_table():
    table = np.zeros((TOK, TOK), np.float64)
    rows = np.arange(ROWS)
    for pair in range(2 * PAIRS):
        if pair == 0:
            waves = (np.ones(ROWS), np.cos(np.pi * rows))
        else:
            angle = 2.0 * np.pi * (pair * rows % ROWS) / ROWS
            waves = (np.cos(angle), np.sin(angle))
        for part in range(2):
            for own in range(OWN):
                table[pair * 6 + part * OWN + own, rows * OWN + own] = waves[part]
    return table / math.sqrt(ROWS)


def column_tables():
    freq = np.arange(COLS)[:, None]
    table = np.zeros((2, 192, 128), np.float64)
    for source in range(GROUP):
        quad, lon = source // 4, source % 4
        for own in range(OWN):
            column = lon * 12 + quad * OWN + own
            angle = 2.0 * np.pi * (freq[:, 0] * column % COLS) / COLS
            cosine, sine = np.cos(angle), np.sin(angle)
            first, second = source * 8 + own, source * 8 + OWN + own
            table[0, 0:48, first] = cosine
            table[0, 96:144, first] = -sine
            table[0, 48:96, second] = cosine
            table[0, 144:192, second] = -sine
            table[1, 0:48, first] = cosine
            table[1, 48:96, first] = cosine
            table[1, 96:144, first] = -sine
            table[1, 144:192, first] = -sine
            table[1, 0:48, second] = -sine
            table[1, 48:96, second] = sine
            table[1, 96:144, second] = -cosine
            table[1, 144:192, second] = cosine
    return table / math.sqrt(COLS)


def spread_table():
    table = np.zeros((384, 512), np.float32)
    spots = np.arange(384)
    table[spots, spots // BS * LANES + spots % BS] = 1.0
    return table


def two_terms(table):
    high = table.astype(ml_dtypes.bfloat16)
    low = (table - high.astype(np.float64)).astype(ml_dtypes.bfloat16)
    return np.stack([high, low])


def dot(left, right):
    return lax.dot_general(left, right, (((1,), (0,)), ((), ())), preferred_element_type=jnp.float32)


def dot_nt(left, right):
    return lax.dot_general(left, right, (((1,), (1,)), ((), ())), preferred_element_type=jnp.float32)


def dot_tn(left, right):
    return lax.dot_general(left, right, (((0,), (0,)), ((), ())), preferred_element_type=jnp.float32)


def normalize(values):
    center = values - jnp.mean(values, axis=-1, keepdims=True)
    inverse = lax.rsqrt(jnp.mean(center * center, axis=-1, keepdims=True) + NORM_EPS)
    return center * inverse, inverse


def normalize_back(upstream, scaled, inverse, gain):
    inner = upstream * gain
    return inverse * (
        inner
        - jnp.mean(inner, axis=-1, keepdims=True)
        - scaled * jnp.mean(inner * scaled, axis=-1, keepdims=True)
    )


def column_sum(values):
    return jnp.sum(values, axis=0, keepdims=True)


def bell(values):
    return 0.5 * (1.0 + lax.erf(values * math.sqrt(0.5)))


def bell_slope(values, area):
    return area + values * jnp.exp(-0.5 * values * values) * (1.0 / math.sqrt(2.0 * math.pi))


def send_rows(low, spread_ref, row_ref, out_ref):
    wide = jnp.concatenate(
        [dot(low[:, :384], spread_ref[...]), dot(low[:, 384:], spread_ref[...])], axis=1
    ).astype(NARROW)
    turned = dot(row_ref[0], wide) + dot(row_ref[1], wide)
    for side in range(2):
        for block in range(NB):
            out_ref[side * NB + block] = turned[
                side * HALF_TOK : (side + 1) * HALF_TOK, block * LANES : (block + 1) * LANES
            ].astype(NARROW)


def take_rows(in_ref, spread_ref, row_back_ref):
    sides = []
    for side in range(2):
        sides.append(
            jnp.concatenate(
                [in_ref[side * NB + block].astype(jnp.float32) for block in range(NB)], axis=1
            )
        )
    wide = jnp.concatenate(sides, axis=0).astype(NARROW)
    low = jnp.concatenate(
        [dot_nt(wide[:, :512], spread_ref[...]), dot_nt(wide[:, 512:], spread_ref[...])], axis=1
    ).astype(NARROW)
    return dot(row_back_ref[0], low) + dot(row_back_ref[1], low)


def fetch(sources, held_ref, sems):
    copies = [pltpu.make_async_copy(src, held_ref.at[i], sems.at[i]) for i, src in enumerate(sources)]
    for copy in copies:
        copy.start()
    return copies


def thirds(w_ref, size):
    return [w_ref[i * size : (i + 1) * size] for i in range(3)]


def embed_kernel(src_ref, shift_ref, bias_ref, norm_ref, spread_ref, row_ref, w_ref,
                 state_ref, send_ref):
    src = src_ref[...]
    state = bias_ref[...]
    for offset, weight in enumerate(thirds(w_ref, PIX)):
        moved = src if offset == 1 else dot(shift_ref[offset], src).astype(NARROW)
        state = state + dot(moved, weight)
    state_ref.put(state)
    scaled, _unused = normalize(state)
    normed = scaled * norm_ref[0:1] + norm_ref[1:2]
    send_rows(normed.astype(NARROW), spread_ref, row_ref, send_ref)


def turn_columns(wide_ref, col_ref, pair):
    kind = 0 if pair == 0 else 1
    low = wide_ref[:, 6 * pair : 6 * pair + 8, :].reshape(128, 128).astype(NARROW)
    both = dot(col_ref[0, kind], low) + dot(col_ref[1, kind], low)
    return jnp.concatenate([both[:96], both[96:]], axis=1).astype(NARROW)


def back_columns(wide_ref, col_back_ref, pair, low):
    kind = 0 if pair == 0 else 1
    both = jnp.concatenate([low[:, :128], low[:, 128:]], axis=0)
    back = dot(col_back_ref[0, kind], both) + dot(col_back_ref[1, kind], both)
    wide_ref[:, 6 * pair : 6 * pair + 8, :] = back.reshape(16, 8, 128)


def spec_kernel(
    in_ref, col_ref, col_back_ref, w_ref, b_ref, out_ref, mixed_ref, wide_ref, wide_out_ref
):
    wide_ref[:, :HALF_TOK, :] = in_ref[...].astype(jnp.float32)
    wide_ref[:, HALF_TOK:, :] = jnp.zeros((16, 8, 128), jnp.float32)
    for chunk in range(4):
        pairs = range(chunk * 3, chunk * 3 + 3)
        mixed = jnp.concatenate([turn_columns(wide_ref, col_ref, pair) for pair in pairs], axis=0)
        mixed_ref.put(mixed, slice(chunk * 288, (chunk + 1) * 288), slice(None))
        inner = dot(mixed, w_ref[0]) + b_ref[0:1]
        act = (inner * bell(inner)).astype(NARROW)
        outer = (dot(act, w_ref[1]) + b_ref[1:2]).astype(NARROW)
        for place, pair in enumerate(pairs):
            back_columns(wide_out_ref, col_back_ref, pair, outer[place * 96 : place * 96 + 96])
    out_ref[...] = wide_out_ref[:, :HALF_TOK, :].astype(NARROW)


def spec_back_kernel(
    in_ref, col_ref, col_back_ref, w_ref, b_ref, mixed_ref,
    out_ref, gw_ref, gb_ref, wide_ref, wide_out_ref,
):
    wide_ref[:, :HALF_TOK, :] = in_ref[...].astype(jnp.float32)
    wide_ref[:, HALF_TOK:, :] = jnp.zeros((16, 8, 128), jnp.float32)
    for chunk in range(4):
        pairs = range(chunk * 3, chunk * 3 + 3)
        g_outer = jnp.concatenate([turn_columns(wide_ref, col_ref, pair) for pair in pairs], axis=0)
        mixed = mixed_ref()[chunk * 288 : (chunk + 1) * 288, :]
        inner = dot(mixed, w_ref[0]) + b_ref[0:1]
        area = bell(inner)
        act = (inner * area).astype(NARROW)
        g_inner = (bell_slope(inner, area) * dot_nt(g_outer, w_ref[1])).astype(NARROW)
        g_mixed = dot_nt(g_inner, w_ref[0]).astype(NARROW)
        first, second = dot_tn(mixed, g_inner), dot_tn(act, g_outer)
        sums = jnp.concatenate(
            [column_sum(g_inner.astype(jnp.float32)), column_sum(g_outer.astype(jnp.float32))], axis=0
        )
        if chunk == 0:
            gw_ref[0], gw_ref[1], gb_ref[...] = first, second, sums
        else:
            gw_ref[0] += first
            gw_ref[1] += second
            gb_ref[...] += sums
        for place, pair in enumerate(pairs):
            back_columns(wide_out_ref, col_back_ref, pair, g_mixed[place * 96 : place * 96 + 96])
    out_ref[...] = wide_out_ref[:, :HALF_TOK, :].astype(NARROW)


def mlp_kernel(has_next, in_ref, state_ref, norm_ref, next_norm_ref, up_b_ref, down_b_ref,
               spread_ref, row_ref, row_back_ref, w0_ref, w1_ref, w2_ref, w3_ref, *rest):
    held_ref, sems = rest[-2:]
    mixed_ref, hidden_in_ref, before_ref, hidden_ref, out_ref = rest[:5]
    copies = fetch((w0_ref, w1_ref, w2_ref, w3_ref), held_ref, sems)
    spatial = take_rows(in_ref, spread_ref, row_back_ref)
    state = state_ref()[...]
    scaled, _unused = normalize(state)
    mixed = state + spatial + (scaled * norm_ref[0:1] + norm_ref[1:2])
    mixed_ref.put(mixed)
    again, _unused = normalize(mixed)
    hidden_in = (again * norm_ref[2:3] + norm_ref[3:4]).astype(NARROW)
    hidden_in_ref.put(hidden_in)
    out = mixed + down_b_ref[...]
    for part in range(4):
        spot = slice(part * D, (part + 1) * D)
        copies[part].wait()
        before = dot_nt(hidden_in, held_ref[part, 0]) + up_b_ref[:, spot]
        before_ref.put(before, slice(None), spot)
        hidden = (before * bell(before)).astype(NARROW)
        hidden_ref.put(hidden, slice(None), spot)
        out = out + dot(hidden, held_ref[part, 1])
    out_ref.put(out)
    if has_next:
        scaled, _unused = normalize(out)
        normed = scaled * next_norm_ref[0:1] + next_norm_ref[1:2]
        send_rows(normed.astype(NARROW), spread_ref, row_ref, rest[5])


def head_kernel(state_ref, shift_ref, bias_ref, target_ref, weight_ref, w_ref,
                low_ref, pred_ref, grad_ref, loss_ref):
    low = state_ref()[...].astype(NARROW)
    low_ref.put(low)
    predicted = bias_ref[...]
    for offset, weight in enumerate(thirds(w_ref, D)):
        moved = low if offset == 1 else dot(shift_ref[offset], low).astype(NARROW)
        predicted = predicted + dot(moved, weight)
    pred_ref[...] = predicted.astype(NARROW)
    differ = predicted - target_ref()[...].astype(jnp.float32)
    grad_ref.put(weight_ref[:, 1:2] * differ)
    loss_ref[...] = column_sum(weight_ref[:, 0:1] * differ * differ)


def head_back_kernel(grad_ref, shift_ref, w_ref, low_ref, sum_ref, out_ref):
    low = grad_ref()[...].astype(NARROW)
    low_ref.put(low)
    sum_ref[...] = column_sum(low.astype(jnp.float32))
    total = None
    for offset, weight in enumerate(thirds(w_ref, D)):
        moved = low if offset == 1 else dot(shift_ref[2 - offset], low).astype(NARROW)
        part = dot_nt(moved, weight)
        total = part if total is None else total + part
    out_ref[...] = total


def embed_back_kernel(low_ref, shift_ref, add_ref, w_ref, out_ref):
    low = low_ref[...]
    total = None
    for offset, weight in enumerate(thirds(w_ref, PIX)):
        moved = low if offset == 1 else dot(shift_ref[2 - offset], low).astype(NARROW)
        part = dot_nt(moved, weight)
        total = part if total is None else total + part
    out_ref.put(add_ref()[...] + total)


def mlp_back_kernel(up_ref, before_ref, mixed_ref, norm_ref, spread_ref, row_ref,
                    w0_ref, w1_ref, w2_ref, w3_ref,
                    grad_out_ref, g_before_ref, g_mixed_ref, g_up_b_ref, sums_ref, send_ref,
                    held_ref, sems):
    copies = fetch((w0_ref, w1_ref, w2_ref, w3_ref), held_ref, sems)
    upstream = up_ref[...]
    grad_out = upstream.astype(NARROW)
    grad_out_ref.put(grad_out)
    sums_ref[0:1] = column_sum(grad_out.astype(jnp.float32))
    g_second = None
    for part in range(4):
        spot = slice(part * D, (part + 1) * D)
        before = before_ref()[:, spot]
        slope = bell_slope(before, bell(before))
        copies[part].wait()
        g_before = (slope * dot_nt(grad_out, held_ref[part, 1])).astype(NARROW)
        g_before_ref.put(g_before, slice(None), spot)
        g_up_b_ref[:, spot] = column_sum(g_before.astype(jnp.float32))
        now = dot(g_before, held_ref[part, 0])
        g_second = now if g_second is None else g_second + now
    scaled, inverse = normalize(mixed_ref()[...])
    sums_ref[1:2] = column_sum(g_second * scaled)
    sums_ref[2:3] = column_sum(g_second)
    g_mixed = upstream + normalize_back(g_second, scaled, inverse, norm_ref[2:3])
    g_mixed_ref.put(g_mixed)
    send_rows(g_mixed.astype(NARROW), spread_ref, row_ref, send_ref)


def norm_back_kernel(in_ref, g_mixed_ref, state_ref, norm_ref, spread_ref, row_back_ref,
                     out_ref, low_ref, sums_ref):
    g_normed = take_rows(in_ref, spread_ref, row_back_ref)
    g_mixed = g_mixed_ref()[...]
    g_normed = g_normed + g_mixed
    scaled, inverse = normalize(state_ref()[...])
    out = g_mixed + normalize_back(g_normed, scaled, inverse, norm_ref[0:1])
    out_ref[...] = out
    low = out.astype(NARROW)
    low_ref[...] = low
    sums_ref[0:1] = column_sum(g_normed * scaled)
    sums_ref[1:2] = column_sum(g_normed)
    sums_ref[2:3] = column_sum(low.astype(jnp.float32))


def narrow_kernel(place_ref, in_ref, out_ref):
    out_ref[...] = in_ref[...].astype(NARROW)


def own_quarters(weights, depth, place):
    size = weights.shape[2] // 4

    def from_spot(m, q, place_ref):
        return (depth, m, (q // 2 + place_ref[0]) % 2 * 2 + q % 2, 0)

    return pl.pallas_call(
        narrow_kernel,
        name="narrow",
        out_shape=jax.ShapeDtypeStruct((2, 2, 2, size, D), NARROW),
        grid_spec=pltpu.PrefetchScalarGridSpec(
            num_scalar_prefetch=1,
            grid=(2, 4),
            in_specs=[pl.BlockSpec((None, None, size, D), from_spot)],
            out_specs=pl.BlockSpec(
                (None, None, None, size, D), lambda m, q, place_ref: (m, q // 2, q % 2, 0, 0)
            ),
        ),
    )(place, weights)


def muon_kernel(level_ref, momentum_ref, weight_ref, change_ref, out_ref):
    momentum = momentum_ref[...]
    ortho = POLY_COEF[0] * POLY_COEF[0] * level_ref[pl.program_id(0)] * momentum
    ortho = ortho + dot(momentum.astype(NARROW), change_ref[...])
    out_ref[...] = weight_ref[...] * (1.0 - MUON_RATE * DECAY_RATE) - MUON_RATE * (FF / D) ** 0.5 * ortho


class Coming:
    def __init__(self, far_ref, held_ref, sem):
        self.held, self.copy = held_ref, pltpu.make_async_copy(far_ref, held_ref, sem)
        self.copy.start()

    def __call__(self):
        if self.copy is not None:
            self.copy.wait()
        self.copy = None
        return self.held


class Going:
    def __init__(self, far_ref, held_ref, sems):
        self.far, self.held, self.sems, self.copies = far_ref, held_ref, sems, []

    def put(self, value, *spot):
        if spot:
            self.held[spot] = value
            source, target = self.held.at[spot], self.far.at[spot]
        else:
            self.held[...] = value
            source, target = self.held, self.far
        copy = pltpu.make_async_copy(source, target, self.sems.at[len(self.copies)])
        copy.start()
        self.copies.append(copy)


PIECES = 4


def launch(kernel, name, out_dims, operands, far=(), far_out=False, near=(), scratch=(), limit=16,
           coming=(), going=()):
    anywhere = pl.BlockSpec(memory_space=pltpu.HBM)
    local = pl.BlockSpec(memory_space=pltpu.VMEM)
    in_specs = []
    for i in range(len(operands)):
        if i in near:
            in_specs.append(pl.BlockSpec(memory_space=pltpu.SMEM))
        else:
            in_specs.append(anywhere if i in far or i in coming else local)
    sem = pltpu.SemaphoreType.DMA
    staged = [pltpu.VMEM(operands[i].shape, operands[i].dtype) for i in coming]
    staged += [pltpu.VMEM(*out_dims[i]) for i in going]
    staged += [sem((len(coming),))] * bool(coming) + [sem((PIECES,))] * len(going)
    ins, outs = len(operands), len(out_dims)

    def body(*refs):
        refs, rest = list(refs[: ins + outs]), refs[ins + outs :]
        held, rest = rest[: len(staged)], rest[len(staged) :]
        tail = len(coming) + len(going)
        for number, i in enumerate(coming):
            refs[i] = Coming(refs[i], held[number], held[tail].at[number])
        sent = []
        for number, i in enumerate(going):
            sems = held[tail + bool(coming) + number]
            refs[ins + i] = Going(refs[ins + i], held[len(coming) + number], sems)
            sent.append(refs[ins + i])
        kernel(*refs, *rest)
        for way in sent:
            for copy in way.copies:
                copy.wait()

    operands = [
        pltpu.with_memory_space_constraint(a, pltpu.HBM) if i in far or i in coming else a
        for i, a in enumerate(operands)
    ]
    out_shape = [
        pltpu.HBM(*dims) if far_out or i in going else jax.ShapeDtypeStruct(*dims)
        for i, dims in enumerate(out_dims)
    ]
    return pl.pallas_call(
        body,
        name=name,
        out_shape=out_shape,
        in_specs=in_specs,
        out_specs=[anywhere if far_out or i in going else local for i in range(outs)],
        scratch_shapes=staged + list(scratch),
        compiler_params=pltpu.CompilerParams(vmem_limit_bytes=limit * 1024 * 1024),
    )(*operands)


def exchange(values):
    return lax.all_to_all(values, ITEM_AXES, split_axis=0, concat_axis=0, tiled=True)


def total_over(values, axes):
    count = lax.axis_size(axes)
    spread = jnp.broadcast_to(jnp.pad(values, (0, LANES - values.shape[0])), (count, 1, LANES))
    got = lax.all_to_all(spread, axes, split_axis=0, concat_axis=0, tiled=True)
    return jnp.sum(got, axis=(0, 1))[: values.shape[0]]


KINDS = {"embed": (D, 6), "head": (PIX, 10), "rest": (LANES, 1)}


def kind_ranges(total):
    edges = (0, EMBED_SIZE, 2 * EMBED_SIZE, total)
    return dict(zip(KINDS, zip(edges[:-1], edges[1:])))


def window_pieces(index, width, total):
    found = []
    for kind, (low, high) in kind_ranges(total).items():
        begin, end = max(index * width, low), min((index + 1) * width, high)
        if begin >= end:
            continue
        row, tiles = KINDS[kind]
        first = (begin - low) // (8 * row)
        last = -(-(end - low) // (8 * row))
        found.append([kind, first, last, 0, begin, end])
    spot = {"embed": EMBED_AT, "head": 0, "rest": 0}
    kinds = [piece[0] for piece in found]
    for piece in found:
        piece[3] = spot[piece[0]]
    if kinds == ["embed", "head"]:
        used = (found[1][2] - found[1][1]) * 10
        found[0][3] = EMBED_AT + -(-(used - EMBED_AT) // 6) * 6
    if kinds == ["head", "rest"]:
        found[1][3] = (found[0][2] - found[0][1]) * 10
    for piece in found:
        assert piece[3] + (piece[2] - piece[1]) * KINDS[piece[0]][1] <= WINDOW
    return found


def form_range(kind, device, width, total, count):
    row, tiles = KINDS[kind]
    base, edge = kind_ranges(total)[kind]
    origin = device * width
    low = jnp.clip(base - origin, 0, width)
    high = jnp.clip(edge - origin, 0, width)
    inside = jnp.maximum(origin - base, 0)
    start = inside % (8 * row) - low
    first = EMBED_AT if kind == "embed" else 0
    for index in range(count):
        for piece in window_pieces(index, width, total):
            if piece[0] == kind and piece[3] != first:
                start = start + jnp.where(device == index, (piece[3] - first) * 8 * LANES, 0)
    return start, low, high


def form_tiles(kind):
    if kind == "embed":
        return EMBED_AT, (WINDOW - EMBED_AT) // 6
    return (0, WINDOW // 10) if kind == "head" else (0, WINDOW)


def own_window(own, device, width, total, count):
    spot = jnp.arange(width, dtype=jnp.int32)
    window = jnp.zeros((WINDOW, 8, LANES), jnp.float32)
    for kind, (row, tiles) in KINDS.items():
        start, low, high = form_range(kind, device, width, total, count)
        first, groups = form_tiles(kind)
        length = groups * tiles * 8 * LANES
        held = jnp.where((spot >= low) & (spot < high), own, 0.0)
        held = jnp.pad(held, (length, length))
        form = lax.dynamic_slice(held, (length - start,), (length,))
        form = form.reshape(groups, 8, tiles, LANES).transpose(0, 2, 1, 3).reshape(-1, 8, LANES)
        window = window + jnp.pad(form, ((first, WINDOW - first - groups * tiles), (0, 0), (0, 0)))
    return window


def own_range(window, device, width, total, count):
    spot = jnp.arange(width, dtype=jnp.int32)
    result = jnp.zeros((width,), jnp.float32)
    for kind, (row, tiles) in KINDS.items():
        start, low, high = form_range(kind, device, width, total, count)
        first, groups = form_tiles(kind)
        form = window[first : first + groups * tiles].reshape(groups, tiles, 8, LANES)
        form = jnp.pad(form.transpose(0, 2, 1, 3).reshape(-1), (width, width))
        held = lax.dynamic_slice(form, (width + start,), (width,))
        result = jnp.where((spot >= low) & (spot < high), held, result)
    return result


def gather_windows(own, *early):
    value, *early = lax.optimization_barrier((jnp.stack([own, swap(own, "zh")]), *early))
    thirds = []
    ways = ["x", "y", "zl"]
    for i in range(3):
        part = value[:, WINDOW_CUTS[i] : WINDOW_CUTS[i + 1]]
        for axis in ways[i:] + ways[:i]:
            part = jnp.stack([part, swap(part, axis)])
        thirds.append((part, swap(part, "c")))
    return thirds, *early


def join_plan(kind, width, total, count):
    tiles = KINDS[kind][1]
    pieces = []
    for index in range(count):
        for piece in window_pieces(index, width, total):
            if piece[0] == kind:
                pieces.append((index, piece[1] * tiles, piece[2] * tiles, piece[3]))
    single, double = [], []
    for spot, (index, first, last, tile) in enumerate(pieces):
        begin, end = first, last
        if spot and pieces[spot - 1][2] > first:
            before, before_first, begin, before_tile = pieces[spot - 1]
            double.append((first, begin - first, before, before_tile + first - before_first, index, tile))
        if spot + 1 < len(pieces):
            end = min(last, pieces[spot + 1][1])
        if begin < end:
            single.append((begin, end - begin, index, tile + begin - first))
    return single, double


def by_thirds(size, tile):
    found = []
    for third in range(3):
        begin, end = max(tile, WINDOW_CUTS[third]), min(tile + size, WINDOW_CUTS[third + 1])
        if begin < end:
            found.append((third, begin - WINDOW_CUTS[third], end - begin, begin - tile))
    return found


def join_kernel(single, double, place_ref, *refs):
    sources, (out_ref, left_ref, right_ref, sems) = refs[:6], refs[6:]
    own = [place_ref[i] for i in range(5)]
    count = 0

    def start(index, size, tile, target_ref, at):
        nonlocal count
        rel = {
            axis: (index // unit + spot) % 2
            for axis, unit, spot in zip(SUB_AXES, (16, 8, 4, 2, 1), own)
        }
        ways = ["x", "y", "zl"]
        ends = []
        for third, begin, amount, offset in by_thirds(size, tile):
            spots = [rel[axis] for axis in (ways[third:] + ways[:third])[::-1]] + [rel["zh"]]
            sources_now = sources[2 * third : 2 * third + 2]
            copies = [
                pltpu.make_async_copy(
                    ref.at[(*spots, pl.ds(begin, amount))],
                    target_ref.at[pl.ds(at + offset, amount)],
                    sems.at[count],
                )
                for ref in sources_now
            ]
            count += 1

            @pl.when(rel["c"] == 0)
            def _():
                copies[0].start()

            @pl.when(rel["c"] == 1)
            def _():
                copies[1].start()

            ends.append(copies[0])
        return ends

    edges = []
    for spot, (begin, size, before, before_tile, index, tile) in enumerate(double):
        edges += start(before, size, before_tile, left_ref.at[spot], 0)
        edges += start(index, size, tile, right_ref.at[spot], 0)
    ends = []
    for begin, size, index, tile in single:
        ends += start(index, size, tile, out_ref, begin)
    for copy in edges:
        copy.wait()
    for spot, (begin, size, *unused) in enumerate(double):
        both = left_ref[spot, :size].astype(jnp.float32) + right_ref[spot, :size].astype(jnp.float32)
        out_ref[begin : begin + size] = both.astype(NARROW)
    for copy in ends:
        copy.wait()


def join_windows(thirds, place, kind, width, total, count):
    row, tiles = KINDS[kind]
    low, high = kind_ranges(total)[kind]
    single, double = join_plan(kind, width, total, count)
    groups = -(-(high - low) // (8 * row))
    amount = sum(len(by_thirds(size, tile)) for begin, size, index, tile in single)
    for begin, size, before, before_tile, index, tile in double:
        amount += len(by_thirds(size, before_tile)) + len(by_thirds(size, tile))
    held = pltpu.VMEM((max(len(double), 1), max([d[1] for d in double] + [1]), 8, LANES), NARROW)
    (out,) = launch(
        functools.partial(join_kernel, single, double), "join_" + kind,
        [((groups * tiles, 8, LANES), NARROW)], [place] + [ref for pair in thirds for ref in pair],
        near=(0,), far=tuple(range(1, 7)), scratch=(held, held, pltpu.SemaphoreType.DMA((amount,))),
    )
    return out.reshape(groups, tiles, 8, LANES).transpose(0, 2, 1, 3).reshape(groups * 8, row)


def pack_plan(width, total, count):
    plan = []
    for index in range(count):
        for kind, first, last, tile, begin, end in window_pieces(index, width, total):
            tiles = KINDS[kind][1]
            if kind == "rest":
                plan.append((index, 6, first, last - first, tile))
                continue
            size = (PIX if kind == "embed" else D) // 8
            while first < last:
                source = first // size
                stop = min(last, (source + 1) * size)
                number = source + (0 if kind == "embed" else 3)
                plan.append((index, number, (first - source * size) * tiles, (stop - first) * tiles, tile))
                tile += (stop - first) * tiles
                first = stop
    return plan


def pack_kernel(plan, place_ref, *refs):
    sources, (keep_ref, send_ref, sems) = refs[:7], refs[7:]
    zh, zl, x, y, c = (place_ref[i] for i in range(5))
    ends = []
    for number, (index, source, begin, size, tile) in enumerate(plan):
        core = index % 2
        place = zip((16, 8, 4, 2), (zh, zl, x, y))
        spot = tuple((index // unit + own) % 2 for unit, own in place) + (pl.ds(tile, size),)
        from_ref = sources[source].at[pl.ds(begin, size)]
        keep = pltpu.make_async_copy(from_ref, keep_ref.at[spot], sems.at[number])
        send = pltpu.make_async_copy(from_ref, send_ref.at[spot], sems.at[number])

        @pl.when(c == core)
        def _():
            keep.start()

        @pl.when(c != core)
        def _():
            send.start()

        ends.append(keep)
    for copy in ends:
        copy.wait()


def tiles_of(values):
    rows, columns = values.shape
    split = values.reshape(rows // 8, 8, columns // LANES, LANES)
    return split.transpose(0, 2, 1, 3).reshape(-1, 8, LANES)


def swap(values, axis):
    return lax.ppermute(values, axis, [(0, 1), (1, 0)])


def add_low(*values):
    return sum(v.astype(jnp.float32) for v in values).astype(NARROW)


def side(values, dim, which, turn):
    if turn is None:
        return lax.index_in_dim(values, which, dim, keepdims=True)
    return lax.dynamic_slice_in_dim(values, (which + turn) % 2, 1, dim)


def chip_parts(kept, ways, cuts, cut_dim):
    return [
        ([lax.slice_in_dim(v, cuts[i], cuts[i + 1], axis=cut_dim) for v in kept], ways[i:] + ways[:i])
        for i in range(3)
    ]


def chip_stage(parts, stage):
    result = []
    for values, order in parts:
        dim, axis, turn = order[stage]
        got = swap(add_low(*(side(v, dim, 1, turn) for v in values)), axis)
        result.append(([add_low(got, *(side(v, dim, 0, turn) for v in values))], order))
    return result


def chip_join(parts, cut_dim):
    return jnp.concatenate([values[0] for values, order in parts], axis=cut_dim)


def held_back(parts, *others):
    flat = [values[0] for values, order in parts]
    flat, others = lax.optimization_barrier((flat, others))
    return [([v], order) for v, (unused, order) in zip(flat, parts)], *others


def plane_sum(values):
    rows = values.shape[0]
    core = lax.axis_index("c")
    halves = values.reshape(2, rows // 2, values.shape[1])
    kept = lax.dynamic_index_in_dim(halves, core, 0, keepdims=False)
    sent = lax.dynamic_index_in_dim(halves, 1 - core, 0, keepdims=False).astype(NARROW)
    kept = kept + swap(sent, "c").astype(jnp.float32)
    quarter = rows // 4
    parts = []
    for start, order in ((0, ("x", "y")), (quarter, ("y", "x"))):
        value = kept[start : start + quarter]
        for axis in order:
            low = value.astype(NARROW)
            value = low.astype(jnp.float32) + swap(low, axis).astype(jnp.float32)
        parts.append(value)
    mine = jnp.concatenate(parts, axis=0).astype(NARROW)
    other = swap(mine, "c")
    first = jnp.where(core == 0, mine, other)
    second = jnp.where(core == 0, other, mine)
    return jnp.concatenate([first, second], axis=0).astype(jnp.float32)


def line_gather(own):
    plane = lax.axis_index(Z_AXES)
    below, above = [], []
    value = own
    for step in (1, 2, 3):
        value = lax.ppermute(value, Z_AXES, [(i, i + 1) for i in range(step - 1, 3)])
        below.append(value)
    value = own
    for step in (1, 2, 3):
        value = lax.ppermute(value, Z_AXES, [(i, i - 1) for i in range(1, 5 - step)])
        above.append(value)
    stack = jnp.stack(below[::-1] + [own] + above)
    return lax.dynamic_slice_in_dim(stack, 3 - plane, 4, 0)


def unpack_rest(rest):
    found = []
    offset = 0
    for dims in ((D,), (PIX,), (L, 2, 2, D), (L, 4, D), (L, FF + D)):
        amount = math.prod(dims)
        found.append(rest[offset : offset + amount].reshape(dims))
        offset += amount
    return found


def fast_body(pixels, targets, mask, lat_rows, adam_params, adam_m, adam_v, mlp_weights, mlp_momentum):
    lat_index, lon_index = lax.axis_index(LAT_AXES), lax.axis_index(LON_AXES)
    device = lax.axis_index(SUB_AXES)
    devices = lax.axis_size(SUB_AXES)
    width = adam_params.shape[0]
    total = width * devices
    low_side = lax.axis_index("zl") == 0
    x, y, c = lax.axis_index("x"), lax.axis_index("y"), lax.axis_index("c")
    block = lax.axis_index(("x", "y", "c"))
    shifts = jnp.asarray(shift_tables(), NARROW)
    row_fwd = jnp.asarray(two_terms(row_table()))
    row_back = jnp.asarray(two_terms(row_table().T))
    col_fwd = jnp.asarray(two_terms(column_tables()))
    col_back = jnp.asarray(two_terms(column_tables().transpose(0, 2, 1)))
    col_fwd = jnp.where(low_side, col_fwd, col_fwd[:, 1:2])
    col_back = jnp.where(low_side, col_back, col_back[:, 1:2])
    spread = jnp.asarray(spread_table(), NARROW)

    def to_items(values):
        rest = values.shape[4:]
        lead, items, rows, cols = values.shape[:4]
        split = values.reshape((lead, items, rows, 4, OWN) + rest)
        order = (1, 3, 0, 2, 4) + tuple(range(5, 5 + len(rest)))
        packed = split.transpose(order).reshape((items * 4, lead * rows * OWN) + rest)
        got = lax.all_to_all(packed, LAT_AXES, split_axis=0, concat_axis=0, tiled=True)
        got = got.reshape((items * 4, lead, rows * OWN) + rest)
        return jnp.moveaxis(got, 1, 0).reshape((lead, TOK) + rest)

    source = to_items(pixels[None])[0]
    zh, zl = lax.axis_index("zh"), lax.axis_index("zl")
    place = jnp.stack([zh, zl, x, y, c])
    own = own_window(adam_params, device, width, total, devices).astype(NARROW)
    quarters = [own_quarters(mlp_weights, depth, x[None]) for depth in range(L)]
    windows, source, *quarters = gather_windows(own, source, *quarters)
    own_mask = own_window(jnp.ones((width,), jnp.float32), device, width, total, devices)
    first = swap(lax.dynamic_index_in_dim(quarters[0][:, 0], zl, 1, keepdims=False), "y")
    second = swap(first, "x")
    others = swap(jnp.stack([first, second], axis=1), "zl")
    third = swap(quarters[1][:, 0], "y")
    coming = (first, second, others, third, swap(third, "x"))

    def feed_forward(coming):
        first, second, others, third, fourth = coming
        both = jnp.stack([first, second], axis=1)
        across = (
            jnp.where(zl == 0, jnp.stack([both, others], axis=2), jnp.stack([others, both], axis=2)),
            jnp.stack([third, fourth], axis=1),
        )
        return [
            [chunk.reshape(2, D, D) for chunk in (own, far, swap(own, "c"), swap(far, "c"))]
            for own, far in zip(quarters, across)
        ]

    wanted = to_items(targets)
    row_weight = jnp.sin(math.pi * (lat_rows.astype(jnp.float32) + 0.5) / ROWS)
    weight_local = row_weight[None, :, None] * mask.astype(jnp.float32)
    weights = to_items(weight_local[None])[0]
    weight_sum = total_over(jnp.sum(weight_local)[None], SUB_AXES)[0]
    loss_scale = 2.0 / (STEPS * PIX * weight_sum)
    weight_pair = jnp.stack([weights, weights * loss_scale], axis=1)

    embed_w = join_windows(windows, place, "embed", width, total, devices)
    head_w = join_windows(windows, place, "head", width, total, devices)
    rest = join_windows(windows, place, "rest", width, total, devices)
    spec_rows = L * 4 * NB * BS * BS // LANES
    spec_w = rest[:spec_rows].reshape(L, 2, 2, NB, BS, BS)
    embed_b, head_b, spec_b, norm_params, mlp_b = unpack_rest(rest[spec_rows:].reshape(-1))
    embed_b, head_b = embed_b.astype(jnp.float32)[None], head_b.astype(jnp.float32)[None]
    norms = norm_params.astype(jnp.float32)
    mlp_b = mlp_b.astype(jnp.float32)

    def by_place(values):
        for dim, side in ((1, y), (2, c), (3, x)):
            values = jnp.where(side == 0, values, jnp.flip(values, dim))
        return values

    up_b = by_place(mlp_b[:, :FF].reshape(L, 2, 2, 2, -1)).transpose(0, 2, 1, 3, 4)
    up_b = up_b.reshape(L, 1, FF)
    down_b = mlp_b[:, None, FF:]
    gap = LANES - BS
    own_w = lax.dynamic_index_in_dim(spec_w, block, 3, keepdims=False)
    own_w = jnp.pad(own_w, ((0, 0),) * 3 + ((0, gap), (0, gap)))
    real, imag = own_w[:, :, 0], own_w[:, :, 1]
    pair_w = jnp.concatenate(
        [jnp.concatenate([real, imag], axis=-1), jnp.concatenate([-imag, real], axis=-1)], axis=-2
    )
    own_b = lax.dynamic_slice_in_dim(spec_b, block * BS, BS, 3).astype(jnp.float32)
    pair_b = jnp.pad(own_b, ((0, 0),) * 3 + ((0, gap),)).reshape(L, 2, 2 * LANES)

    f32 = jnp.float32
    payload = ((GROUP, HALF_TOK, LANES), NARROW)
    state_f32 = ((TOK, D), f32)
    wide = pltpu.VMEM((GROUP, HALF_TOK + 8, LANES), f32)
    sem = pltpu.SemaphoreType.DMA
    held_mlp = (pltpu.VMEM((4, 2, D, D), NARROW), sem((4,)))

    current = source
    saved = []
    loss_sums = []
    for roll_idx in range(STEPS):
        state, sent = launch(
            embed_kernel, "embed", [state_f32, payload],
            [current, shifts, embed_b, norms[0], spread, row_fwd, embed_w], going=(0,),
        )
        if roll_idx == 0:
            sent, wanted, weight_pair = lax.optimization_barrier((sent, wanted, weight_pair))
        layers = []
        for depth in range(L):
            got = exchange(sent)
            out, mixed_in = launch(
                spec_kernel, "spec", [payload, ((FREQ, 2 * LANES), NARROW)],
                [got, col_fwd, col_back, pair_w[depth], pair_b[depth]], scratch=(wide, wide),
                going=(1,),
            )
            if roll_idx == 0 and depth == 0:
                unused, coming = lax.optimization_barrier((out, coming))
                mlp_low = feed_forward(coming)
            got = exchange(out)
            has_next = depth + 1 < L
            outs = [state_f32, ((TOK, D), NARROW), ((TOK, FF), f32), ((TOK, FF), NARROW), state_f32]
            results = launch(
                functools.partial(mlp_kernel, has_next), "mlp", outs + [payload] * has_next,
                [got, state, norms[depth], norms[min(depth + 1, L - 1)], up_b[depth], down_b[depth],
                 spread, row_fwd, row_back, *mlp_low[depth]], far=(9, 10, 11, 12), scratch=held_mlp, limit=MLP_LIMIT,
                coming=(1,), going=(0, 1, 2, 3, 4),
            )
            layers.append((state, mixed_in) + tuple(results[:4]))
            state = results[4]
            if has_next:
                sent = results[5]
        low, predicted, loss_grad, loss_part = launch(
            head_kernel, "head",
            [((TOK, D), NARROW), ((TOK, PIX), NARROW), ((TOK, PIX), f32), ((1, PIX), f32)],
            [state, shifts, head_b, wanted[roll_idx], weight_pair, head_w], coming=(0, 3), going=(0, 2),
        )
        loss_sums.append(loss_part)
        saved.append((current, layers, low, loss_grad))
        current = predicted

    rows_own = mlp_momentum.shape[2] // 2
    half_ff = FF // 2

    def joined(terms, member):
        return jnp.concatenate([now[member] for now in terms], axis=0)

    mlp_ways = [(3, "x", None), (2, "y", None), (1, "zl", zl)]

    def mlp_sends(depth):
        g_before, hidden_in, hidden, grad_out = (joined(mlp_terms[depth], m) for m in range(4))
        pairs = ((g_before, hidden_in), (hidden, grad_out))
        return pairs, [swap(dot_tn(a[:, half_ff:], b).astype(NARROW), "c") for a, b in pairs]

    def mlp_kept(pairs, got):
        kept = [
            (dot_tn(a[:, :half_ff], b) + sent.astype(f32)).astype(NARROW)
            for (a, b), sent in zip(pairs, got)
        ]
        return jnp.stack(kept).reshape(2, 2, 2, rows_own, D)

    head_terms, embed_terms = [], []
    mlp_terms = [[] for unused in range(L)]
    spec_terms = [[] for unused in range(L)]
    sum_terms = [[] for unused in range(L)]
    head_sums, embed_sums = [], []
    upstream = None
    for roll_idx in reversed(range(STEPS)):
        current, layers, low, loss_grad = saved[roll_idx]
        upstream = loss_grad if upstream is None else upstream
        upstream_low, head_sum, grad_state = launch(
            head_back_kernel, "head_back",
            [((TOK, PIX), NARROW), ((1, PIX), f32), state_f32], [upstream, shifts, head_w],
            coming=(0,), going=(0,),
        )
        head_terms.append((low, upstream_low))
        head_sums.append(head_sum)
        for depth in reversed(range(L)):
            state, mixed_in, mixed, hidden_in, before, hidden = layers[depth]
            grad_out, g_before, g_mixed, g_up_b, sums_two, sent = launch(
                mlp_back_kernel, "mlp_back",
                [((TOK, D), NARROW), ((TOK, FF), NARROW), state_f32, ((1, FF), f32), ((3, D), f32),
                 payload],
                [grad_state, before, mixed, norms[depth], spread, row_fwd, *mlp_low[depth]],
                far=(6, 7, 8, 9), scratch=held_mlp, limit=MLP_LIMIT,
                coming=(1, 2), going=(0, 1, 2),
            )
            mlp_terms[depth].append((g_before, hidden_in, hidden, grad_out))
            got = exchange(sent)
            if roll_idx == 0 and depth == L - 1:
                last_sends = mlp_sends(depth)
                last_kept, got = lax.optimization_barrier((mlp_kept(*last_sends), got))
            if roll_idx == 0 and depth == 0:
                first_kept, got = lax.optimization_barrier((mlp_kept(*mlp_sends(0)), got))
            out, g_pair, g_pair_b = launch(
                spec_back_kernel, "spec_back",
                [payload, ((2, 2 * LANES, 2 * LANES), f32), ((2, 2 * LANES), f32)],
                [got, col_fwd, col_back, pair_w[depth], pair_b[depth], mixed_in],
                scratch=(wide, wide), coming=(5,),
            )
            got = exchange(out)
            if roll_idx == 0 and depth == 0:
                last_kept, first_kept, got = lax.optimization_barrier((last_kept, first_kept, got))
            grad_state, state_low, sums_one = launch(
                norm_back_kernel, "norm_back", [state_f32, ((TOK, D), NARROW), ((3, D), f32)],
                [got, g_mixed, state, norms[depth], spread, row_back], coming=(1, 2),
            )
            spec_terms[depth].append((g_pair, g_pair_b))
            sum_terms[depth].append((sums_one, sums_two, g_up_b))
        embed_terms.append((current, state_low))
        embed_sums.append(sums_one[2])
        if roll_idx:
            (upstream,) = launch(
                embed_back_kernel, "embed_back", [((TOK, PIX), f32)],
                [state_low, shifts, saved[roll_idx - 1][3], embed_w], coming=(2,), going=(0,),
            )

    mlp_kept_all = jnp.stack([first_kept, last_kept])
    mlp_parts = chip_stage(chip_parts([mlp_kept_all], mlp_ways, MLP_CUTS, 4), 0)

    def moved_pair(values, amount):
        return jnp.concatenate([jnp.roll(now, amount, axis=0) for now in values], axis=0)

    embed_src = joined(embed_terms, 0)
    head_up = joined(head_terms, 1)
    g_embed = [
        dot_tn(embed_src, moved_pair([now[1] for now in embed_terms], OWN * (o - 1))).astype(NARROW)
        for o in range(3)
    ]
    g_head = [
        dot_tn(moved_pair([now[0] for now in head_terms], -OWN * (o - 1)), head_up).astype(NARROW)
        for o in range(3)
    ]
    g_spec, g_spec_b, g_norm, g_mlp_b = [], [], [], []
    for depth in range(L):
        pair_sum = sum(now[0] for now in spec_terms[depth]).reshape(2, 2, LANES, 2, LANES)
        pair_sum = pair_sum[:, :, :BS, :, :BS]
        g_real = pair_sum[:, 0, :, 0] + pair_sum[:, 1, :, 1]
        g_imag = pair_sum[:, 0, :, 1] - pair_sum[:, 1, :, 0]
        g_spec.append(jnp.stack([g_real, g_imag], axis=1))
        g_spec_b.append(sum(now[1] for now in spec_terms[depth]).reshape(2, 2, LANES)[:, :, :BS])
        one = sum(now[0] for now in sum_terms[depth])
        two = sum(now[1] for now in sum_terms[depth])
        g_norm.append(jnp.stack([one[0], one[1], two[1], two[2]]))
        up_sum = sum(now[2] for now in sum_terms[depth]).reshape(1, 2, 2, 2, -1)
        up_sum = by_place(up_sum.transpose(0, 2, 1, 3, 4)).reshape(-1)
        g_mlp_b.append(jnp.concatenate([up_sum, two[0]]))
    full_spec = jnp.zeros((L, 2, 2, NB, BS, BS), NARROW)
    full_spec = lax.dynamic_update_slice_in_dim(
        full_spec, jnp.stack(g_spec).astype(NARROW)[:, :, :, None], block, 3
    )
    full_spec_b = lax.dynamic_update_slice_in_dim(
        jnp.zeros((L, 2, 2, D), f32), jnp.stack(g_spec_b), block * BS, 3
    )
    small = jnp.concatenate(
        [sum(embed_sums), sum(head_sums)[0], full_spec_b.reshape(-1),
         jnp.stack(g_norm).reshape(-1), jnp.stack(g_mlp_b).reshape(-1)]
    ).astype(NARROW)
    rest_grad = jnp.concatenate([full_spec.reshape(-1), small])
    rest_grad = jnp.pad(rest_grad, (0, -rest_grad.shape[0] % (8 * LANES))).reshape(-1, 8, LANES)
    plan = pack_plan(width, total, devices)
    window_set = ((2, 2, 2, 2, WINDOW, 8, LANES), NARROW)
    kept, sent = launch(
        functools.partial(pack_kernel, plan), "pack", [window_set, window_set],
        [place] + [tiles_of(g) for g in g_embed + g_head] + [rest_grad],
        near=(0,), far_out=True, scratch=(sem((len(plan),)),), limit=8,
    )
    ways = [(2, "x", None), (3, "y", None), (1, "zl", None)]
    got = swap(sent, "c")
    mlp_parts, got = held_back(mlp_parts, got)
    parts = chip_parts([kept, got], ways, WINDOW_CUTS, 4)
    for stage in range(3):
        parts = chip_stage(parts, stage)
        if stage:
            mlp_parts = chip_stage(mlp_parts, stage)
    mlp_pair = chip_join(mlp_parts, 4).reshape(2, rows_own, D)
    mlp_send = jnp.where(zh == 0, mlp_pair[1], mlp_pair[0])
    mlp_keep = jnp.where(zh == 0, mlp_pair[0], mlp_pair[1])
    mlp_mine = mlp_keep.astype(f32) + swap(mlp_send, "zh").astype(f32)
    flat_pair = chip_join(parts, 4).reshape(2, WINDOW, 8, LANES)
    flat_window = flat_pair[0].astype(f32) + swap(flat_pair[1], "zh").astype(f32)
    flat_piece = own_range(flat_window, device, width, total, devices)
    local = jnp.stack(
        [jnp.sum(jnp.where(own_mask > 0, flat_window * flat_window, 0.0)) + jnp.sum(mlp_mine * mlp_mine),
         sum(jnp.sum(now) for now in loss_sums)]
    )
    square_sum, loss_total = total_over(local, SUB_AXES)
    loss_total = loss_total / (STEPS * PIX * weight_sum)
    grad_norm = jnp.sqrt(square_sum)
    factor = jnp.minimum(1.0, CLIP_LEVEL / (grad_norm + 1e-06))

    mlp_grad = lax.all_gather(mlp_mine.astype(NARROW), LAT_AXES, axis=0, tiled=True)

    held = mlp_momentum.reshape(2 * L * 2, rows_own, D)
    held = lax.dynamic_index_in_dim(held, lat_index, 0, keepdims=False)
    mine_new = MOMENT_KEEP * held + mlp_mine * factor
    high = lax.Precision.HIGH
    gram = plane_sum(lax.dot_general(mine_new, mine_new, (((0,), (0,)), ((), ())), precision=high))
    inverse = 1.0 / (jnp.sqrt(jnp.trace(gram)) + 1e-07)
    lead, mid, last = POLY_COEF
    square = gram * (inverse * inverse)
    mul = functools.partial(jnp.dot, precision=high)
    poly_one = mid * square + last * mul(square, square)
    turned = mul(square, poly_one)
    square_two = lead * lead * square + 2.0 * lead * turned + mul(turned, poly_one)
    poly_two = mid * square_two + last * mul(square_two, square_two)
    mine_one, mine_two = (
        lax.dynamic_slice_in_dim(now, c * (D // 2), D // 2, 0) for now in (poly_one, poly_two)
    )
    change = (lead * (mine_one + mine_two) + mul(mine_one, poly_two)) * inverse
    level_high = inverse.astype(NARROW)
    level_mid = (inverse - level_high.astype(f32)).astype(NARROW)
    level_low = (inverse - level_high.astype(f32) - level_mid.astype(f32)).astype(NARROW)
    column = jnp.arange(D)[None]
    extra = jnp.where(column == 0, level_high, jnp.where(column == 1, level_mid, level_low))
    extra = jnp.broadcast_to(extra, (8, D))
    change = change.astype(NARROW)
    packed = jnp.concatenate([change, extra], axis=0)
    packed, mlp_grad = lax.optimization_barrier((packed, mlp_grad))
    gathered = line_gather(packed)
    mlp_grad = mlp_grad.reshape(mlp_momentum.shape).astype(f32)
    momentum_new = MOMENT_KEEP * mlp_momentum + mlp_grad * factor
    clipped = flat_piece * factor
    first_new = BETA_FIRST * adam_m + (1.0 - BETA_FIRST) * clipped
    second_new = BETA_SECOND * adam_v + (1.0 - BETA_SECOND) * clipped * clipped
    count_value = float(STEP_NUM)
    first_hat = first_new / (1.0 - BETA_FIRST**count_value)
    second_hat = second_new / (1.0 - BETA_SECOND**count_value)
    adam_new = adam_params - ADAM_RATE * (
        first_hat / (jnp.sqrt(second_hat) + 1e-08) + DECAY_RATE * adam_params
    )
    gathered, momentum_new, adam_new, first_new, second_new = lax.optimization_barrier(
        (gathered, momentum_new, adam_new, first_new, second_new)
    )
    levels = jnp.sum(gathered[:, D // 2, :3].astype(f32), axis=-1)
    gathered = gathered[:, : D // 2]
    other = swap(gathered, "c")
    changes = jnp.concatenate(
        [jnp.where(c == 0, gathered, other), jnp.where(c == 0, other, gathered)], axis=1
    )
    (mlp_new,) = pl.pallas_call(
        muon_kernel,
        name="muon",
        grid=(2 * L, 2),
        out_shape=[jax.ShapeDtypeStruct((2 * L, D, D), f32)],
        in_specs=[pl.BlockSpec(memory_space=pltpu.SMEM)]
        + [pl.BlockSpec((None, rows_own, D), lambda m, h: (m, h, 0))] * 2
        + [pl.BlockSpec((None, D, D), lambda m, h: (m, 0, 0))],
        out_specs=[pl.BlockSpec((None, rows_own, D), lambda m, h: (m, h, 0))],
        compiler_params=pltpu.CompilerParams(vmem_limit_bytes=28 * 1024 * 1024),
    )(levels, momentum_new.reshape(2 * L, D, D), mlp_weights.reshape(2 * L, D, D), changes)
    mlp_new = mlp_new.reshape(mlp_weights.shape)

    return (adam_new, first_new, second_new, mlp_new, momentum_new, loss_total, grad_norm)


def solution(mesh):
    if tuple(mesh.shape.items()) == (("lat", 8), ("lon", 4)):
        fine = Mesh(mesh.devices.reshape(2, 2, 2, 2, 2), SUB_AXES)
        return placed(fast_body, fine, LAT_AXES, LON_AXES)
    return placed(body, mesh, ("lat",), ("lon",))


def placed(step, mesh, lat, lon):
    flat = P(lat + lon)
    halves = P(None, None, lon, None)
    return jax.shard_map(
        step,
        mesh=mesh,
        in_specs=(
            P(None, lat, lon, None),
            P(None, None, lat, lon, None),
            P(None, lat, lon),
            P(lat),
            flat,
            flat,
            flat,
            halves,
            halves,
        ),
        out_specs=(flat, flat, flat, halves, halves, P(), P()),
        check_vma=False,
    )
```
